32 devices in a mesh: clip: 2 (over y), rows: 8 (over z, x), section: 2 (over core).
Axes of the slice: x: 2, y: 2, z: 4, core: 2. Of those that a mesh axis runs over, the one named last changes fastest.
Arguments:
- codes: int32 [8, 32, 24], P('clip', 'rows'), parts along dimension 0, may hold values from 0 to 262143
- in_proj: bfloat16 [18, 512], replicated, may hold values from -1.5 to 1.5
- gain_up: float32 [512], replicated, may hold values from 0.5 to 2
- up_kernel: bfloat16 [27, 512, 256], P(None, None, 'section'), may hold values from -0.0546875 to 0.0546875
- gain_res: float32 [256], replicated, may hold values from 0.5 to 2
- out_kernel: bfloat16 [27, 128, 256], P(None, 'section'), may hold values from -0.078125 to 0.078125
Outputs:
- decoded: bfloat16 [8, 64, 48, 128], P('clip', 'rows', None, 'section'), parts along dimension 0
The draws below stay inside these ranges and needn't reach their ends.
There are 2 independent parts, one for each index of `clip`. The reference program is written for one: setup_inputs(seed, part) draws one part's arguments, and reference() takes and returns one part's arrays. A program takes and returns all parts, laid end to end along the dimension named above; an argument that names none is the same for every part. Nothing has to cross between parts.
All inputs are finite; a program needn't handle non-finite values.
Results may differ from the reference program's by a relative error of at most 0.0058.
Values may be sent and summed in bfloat16 or wider, within the bound.
No kernel may reach another device: no remote copies, remote signals or barrier semaphores. Data moves between devices by JAX's collectives and lax.ppermute only.
A program may use at most 128 MiB of HBM per device.

```python
import math
import jax
import jax.numpy as jnp
from jax import lax

C_LAT = 512
C_HID = 256
C_OUT = 128
CODE_BITS = 18
FRAMES = 4
COLS = 24
ROWS = 32


def with_ends(array, own_key, low, top_value):
    spot = [jax.random.randint(jax.random.fold_in(own_key, axis), (), 0, length) for axis, length in enumerate(array.shape)]
    longest = array.shape.index(max(array.shape))
    next_to = spot[:longest] + [(spot[longest] + 1) % array.shape[longest]] + spot[longest + 1:]
    return array.at[tuple(spot)].set(low).at[tuple(next_to)].set(top_value)


def block_scale(stream_key, shape, pieces, least, largest):
    gain, own = 1.0, jax.random.fold_in(stream_key, 6)
    for position, shards_of in pieces:
        draws = jnp.exp(jax.random.uniform(jax.random.fold_in(own, position), (shards_of,), jnp.float32, least / len(pieces), largest / len(pieces)))
        gain = gain * jnp.repeat(draws, shape[position] // shards_of).reshape([-1 if axis == position else 1 for axis in range(len(shape))])
    return gain


def scatter_about(own_key, dims, deviation, reach, split=(), kind=jnp.bfloat16):
    level = block_scale(own_key, dims, split, -0.22, 0.18) if split else 1.0
    drawn = jax.random.normal(own_key, dims, jnp.float32) * deviation * level
    return jnp.minimum(jnp.maximum(drawn, -reach), reach).astype(kind)


def setup_inputs(seed: int = 0, part: int = 0) -> dict:
    keys = jax.random.split(jax.random.key(seed), 7)
    part_splits = jax.random.split(jax.random.fold_in(keys[6], part), 7)
    codes = with_ends(jax.random.randint(part_splits[0], (FRAMES, ROWS, COLS), 0, 262144), jax.random.fold_in(part_splits[0], 1), 0, 262143).astype(jnp.int32)
    in_proj = scatter_about(keys[1], (CODE_BITS, C_LAT), CODE_BITS ** -0.5, 1.5)
    gain_up = jnp.clip(jnp.exp(jax.random.uniform(keys[2], (C_LAT,), jnp.float32, math.log(0.5), math.log(2.0))), 0.5, 2.0)
    up_kernel = scatter_about(keys[3], (27, C_LAT, C_HID), (27 * C_LAT) ** -0.5, 0.0546875, ((2, 2),))
    gain_res = jnp.clip(jnp.exp(jax.random.uniform(keys[4], (C_HID,), jnp.float32, math.log(0.5), math.log(2.0))), 0.5, 2.0)
    out_kernel = scatter_about(keys[5], (27, C_OUT, C_HID), (27 * C_HID) ** -0.5, 0.078125, ((1, 2),))
    return {"codes": codes, "in_proj": in_proj, "gain_up": gain_up, "up_kernel": up_kernel, "gain_res": gain_res, "out_kernel": out_kernel}


def norm_act(values, gain_vec):
    mean_square = lax.optimization_barrier(jnp.mean(values * values, axis=-1, keepdims=True))
    return jax.nn.silu(values * lax.rsqrt(mean_square + 1e-06) * gain_vec)

def causal_conv(source, shaped):
    result = lax.conv_general_dilated(source[None], shaped, (1, 1, 1), [(2, 0), (1, 1), (1, 1)], dimension_numbers=('NDHWC', 'DHWIO', 'NDHWC'), preferred_element_type=jnp.float32)
    return result[0]

def reference(codes, in_proj, gain_up, up_kernel, gain_res, out_kernel):
    bit_shifts = jnp.arange(CODE_BITS, dtype=jnp.int32)
    bits = ((jnp.right_shift(codes[..., None], bit_shifts) & 1) * 2 - 1).astype(jnp.bfloat16)
    flat_bits = bits.reshape(-1, CODE_BITS)
    latent = jnp.dot(flat_bits, in_proj, preferred_element_type=jnp.float32)
    latent = latent.reshape(codes.shape[0], codes.shape[1], codes.shape[2], -1)
    active = norm_act(latent, gain_up).astype(jnp.bfloat16)
    enlarged = jnp.repeat(jnp.repeat(active, 2, axis=1), 2, axis=2)
    up_shaped = up_kernel.reshape(3, 3, 3, up_kernel.shape[1], up_kernel.shape[2])
    hidden = causal_conv(enlarged, up_shaped)
    normed = norm_act(hidden, gain_res).astype(jnp.bfloat16)
    out_shaped = jnp.transpose(out_kernel, (0, 2, 1)).reshape(3, 3, 3, out_kernel.shape[2], out_kernel.shape[1])
    return causal_conv(normed, out_shaped).astype(jnp.bfloat16)
```

```python
import functools

import jax
import jax.numpy as jnp
from jax import lax
from jax.experimental import pallas as pl
from jax.experimental.pallas import tpu as pltpu
from jax.sharding import PartitionSpec as P

BITS = 18
EPS = 1e-06
F32 = jnp.float32
BF16 = jnp.bfloat16
VMEM_LIMIT = 48 * 1024 * 1024


def silu(v):
    return 0.5 * v * (1.0 + jnp.tanh(0.5 * v))


def latent_rows(rows, in_proj, gain):
    cols = rows[0].shape[1]
    count = len(rows)
    wide = jnp.concatenate([jnp.broadcast_to(row, (cols, cols)) for row in rows], axis=0)
    sub = lax.broadcasted_iota(jnp.int32, (count, cols, cols), 1).reshape(count * cols, cols)
    lane = lax.broadcasted_iota(jnp.int32, (count * cols, cols), 1)
    picked = jnp.where(sub == lane, wide, 0).astype(F32)
    column = jnp.sum(picked, axis=1, keepdims=True).astype(jnp.int32)
    spread = jnp.broadcast_to(column, (count * cols, BITS))
    shift = lax.broadcasted_iota(jnp.int32, (count * cols, BITS), 1)
    bits = ((jnp.right_shift(spread, shift) & 1) * 2 - 1).astype(F32).astype(BF16)
    latent = jnp.dot(bits, in_proj, preferred_element_type=F32)
    mean = jnp.mean(latent * latent, axis=1, keepdims=True)
    return silu(latent * lax.rsqrt(mean + EPS) * gain)


def prep_kernel(codes_ref, proj_ref, gain_ref, up_hbm, out_hbm, w1_ref, w2_ref, act_ref, up_ref, tap_ref, sems):
    copies = [
        pltpu.make_async_copy(up_hbm.at[pl.ds(9 * a, 9)], up_ref.at[pl.ds(9 * a, 9)], sems.at[a])
        for a in range(3)
    ]
    copies.append(pltpu.make_async_copy(out_hbm, tap_ref, sems.at[3]))
    for copy in copies:
        copy.start()

    frames, rows, cols = codes_ref.shape
    size = frames * cols
    for r in range(rows):
        act = latent_rows([codes_ref[t, r : r + 1, :] for t in range(frames)], proj_ref[...], gain_ref[...])
        act_ref[r] = act.astype(BF16)

    width = up_ref.shape[1]
    out_w = up_ref.shape[2]
    step = 32
    for a in range(3):
        copies[a].wait()

        @pl.loop(0, width // step)
        def _(i, a=a):
            k = pl.multiple_of(i * step, step)
            tap = [[up_ref[9 * a + 3 * b + c, pl.ds(k, step), :].astype(F32) for c in range(3)] for b in range(3)]
            row_sets = (
                ([tap[0][c] + tap[1][c] for c in range(3)], tap[0]),
                (tap[2], [tap[1][c] + tap[2][c] for c in range(3)]),
            )
            for half in range(2):
                for py in range(2):
                    x = row_sets[half][py]
                    parts = (x[0], x[1] + x[2], x[0] + x[1], x[2])
                    for v in range(4):
                        w1_ref[a, pl.ds(half * width + k, step), pl.ds((4 * py + v) * out_w, out_w)] = parts[v].astype(BF16)

    copies[3].wait()
    ow, ch = tap_ref.shape[1], tap_ref.shape[2]
    zero = jnp.zeros((ow, ch), BF16)
    for ab in range(9):
        w = [tap_ref[3 * ab + c] for c in range(3)]
        table = ((w[1], w[2]), (w[0], w[1]), (zero, w[0]), (w[2], zero))
        for n in range(4):
            for k in range(2):
                w2_ref[ab, pl.ds(n * ow, ow), pl.ds(k * ch, ch)] = table[n][k]


def shifted(x, cols, amount):
    rows, lanes = x.shape
    place = lax.broadcasted_iota(jnp.int32, (rows // cols, cols, lanes), 1).reshape(rows, lanes)
    moved = pltpu.roll(x, amount % rows, 0)
    return jnp.where(place == (0 if amount == 1 else cols - 1), 0.0, moved)


def reach(frames, cols, a):
    need = (frames - 2 + a) * cols
    return -(-need // 16) * 16


def hidden_kernel(axis, lo_ref, hi_ref, proj_ref, gain_ref, own_ref, w1_ref, h_ref, act_ref, acc_ref):
    frames, rows, cols = lo_ref.shape
    size = frames * cols
    width = own_ref.shape[2]
    place = lax.axis_index(axis)
    last = lax.axis_size(axis) - 1
    for edge, (src, row, ok) in enumerate(((lo_ref, rows - 1, place > 0), (hi_ref, 0, place < last))):
        act = latent_rows([src[t, row : row + 1, :] for t in range(frames)], proj_ref[...], gain_ref[...])
        act_ref[edge * (rows + 1)] = jnp.where(ok, act, 0.0).astype(BF16)
    act_ref[pl.ds(1, rows)] = own_ref[...]

    pairs = rows + 1

    @pl.loop(0, 4)
    def _(n):
        lanes = pl.ds(pl.multiple_of(n * 256, 256), 256)
        for a in (2, 1, 0):
            m = reach(frames, cols, a)
            total = None
            for half in range(2):
                part = jnp.dot(
                    act_ref[pl.ds(half, pairs), pl.ds(0, m), :].reshape(pairs * m, width),
                    w1_ref[a, pl.ds(half * width, width), lanes],
                    preferred_element_type=F32,
                )
                total = part if total is None else total + part
            total = total.reshape(pairs, m, 256)
            if a == 2:
                acc_ref[...] = total
            else:
                skip = (2 - a) * cols
                acc_ref[:, pl.ds(skip, size - skip), :] += total[:, : size - skip, :]
        full = acc_ref[...].reshape(pairs * size, 256)
        left, right = full[:, :128], full[:, 128:]
        px = n % 2

        @pl.when(px == 0)
        def _():
            h_ref[:, pl.ds(pl.multiple_of(n * 128, 128), 128)] = (right + shifted(left, cols, 1)).astype(BF16)

        @pl.when(px == 1)
        def _():
            h_ref[:, pl.ds(pl.multiple_of(n * 128, 128), 128)] = (left + shifted(right, cols, -1)).astype(BF16)


def out_kernel_body(axis, frames, cols, g_ref, gain_ref, w2_ref, o_ref, norm_ref, acc_ref, mix_ref):
    size = frames * cols
    pairs = g_ref.shape[1] // size
    half_ch = g_ref.shape[2] // 4
    place = lax.axis_index(axis)
    last = lax.axis_size(axis) - 1
    for q in range(pairs):
        for py in range(2):
            for px in range(2):
                n = 2 * py + px
                x = [g_ref[s, pl.ds(q * size, size), pl.ds(n * half_ch, half_ch)].astype(F32) for s in range(2)]
                mean = jnp.sum(x[0] * x[0] + x[1] * x[1], axis=1, keepdims=True) / (2 * half_ch)
                scale = lax.rsqrt(mean + EPS)
                if q == 0 and py == 0:
                    scale = jnp.where(place > 0, scale, 0.0)
                if q == pairs - 1 and py == 1:
                    scale = jnp.where(place < last, scale, 0.0)
                for s in range(2):
                    value = silu(x[s] * scale * gain_ref[:, pl.ds(s * half_ch, half_ch)])
                    norm_ref[2 * q + py, :, pl.ds((2 * px + s) * half_ch, half_ch)] = value.astype(BF16)

    height = 2 * (pairs - 1)
    depth = norm_ref.shape[2]
    for a in (2, 1, 0):
        m = reach(frames, cols, a)
        total = None
        for b in range(3):
            part = lax.dot_general(
                norm_ref[pl.ds(b, height), pl.ds(0, m), :].reshape(height * m, depth),
                w2_ref[3 * a + b],
                (((1,), (1,)), ((), ())),
                preferred_element_type=F32,
            )
            total = part if total is None else total + part
        total = total.reshape(height, m, 256)
        if a == 2:
            acc_ref[...] = total
        else:
            skip = (2 - a) * cols
            acc_ref[:, pl.ds(skip, size - skip), :] += total[:, : size - skip, :]

    ow = o_ref.shape[3]
    for y in range(height):
        full = acc_ref[y]
        side = full[:, 128:]
        lane = lax.broadcasted_iota(jnp.int32, side.shape, 1)
        both = full[:, :128] + jnp.where(lane < ow, shifted(side, cols, 1), shifted(side, cols, -1))
        mix_ref[pl.ds(0, size, stride=2), :] = both
        mix_ref[pl.ds(1, size, stride=2), :] = pltpu.roll(both, ow, 1)
        result = mix_ref[...][:, :ow].astype(BF16)
        for t in range(frames):
            o_ref[t, y] = result[2 * cols * t : 2 * cols * (t + 1)]


def params():
    return pltpu.CompilerParams(vmem_limit_bytes=VMEM_LIMIT)


def vmem():
    return pl.BlockSpec(memory_space=pltpu.VMEM)


def body(codes, in_proj, gain_up, up_kernel, gain_res, out_kernel):
    frames, rows, cols = codes.shape
    size = frames * cols
    taps, width, share = up_kernel.shape
    ow, ch = out_kernel.shape[1:]
    count = lax.axis_size("rows")
    forward = [(i, i + 1) for i in range(count - 1)]
    backward = [(i + 1, i) for i in range(count - 1)]
    low = lax.ppermute(codes, "rows", forward)
    high = lax.ppermute(codes, "rows", backward)
    gain_up = gain_up.reshape(1, -1)
    gain_res = gain_res.reshape(1, -1)

    hbm = pl.BlockSpec(memory_space=pl.ANY)
    w1, w2, act = pl.pallas_call(
        prep_kernel,
        out_shape=(
            pltpu.VMEM((3, 2 * width, 8 * share), BF16),
            pltpu.VMEM((9, 4 * ow, 2 * ch), BF16),
            pltpu.VMEM((rows, size, width), BF16),
        ),
        in_specs=[vmem(), vmem(), vmem(), hbm, hbm],
        out_specs=(vmem(), vmem(), vmem()),
        scratch_shapes=[
            pltpu.VMEM(up_kernel.shape, BF16),
            pltpu.VMEM(out_kernel.shape, BF16),
            pltpu.SemaphoreType.DMA((4,)),
        ],
        compiler_params=params(),
        cost_estimate=pl.CostEstimate(flops=10**9, bytes_accessed=2 * 10**7, transcendentals=0),
        name="prep",
    )(codes, in_proj, gain_up, up_kernel, out_kernel)

    pairs = rows + 1
    hidden = pl.pallas_call(
        functools.partial(hidden_kernel, "rows"),
        out_shape=jax.ShapeDtypeStruct((pairs * size, 4 * share), BF16),
        in_specs=[vmem()] * 6,
        out_specs=vmem(),
        scratch_shapes=[
            pltpu.VMEM((rows + 2, size, width), BF16),
            pltpu.VMEM((pairs, size, 256), F32),
        ],
        compiler_params=params(),
        name="hidden",
    )(low, high, in_proj, gain_up, act, w1)

    gathered = lax.all_gather(hidden, "section", axis=0)

    return pl.pallas_call(
        functools.partial(out_kernel_body, "rows", frames, cols),
        out_shape=jax.ShapeDtypeStruct((frames, 2 * rows, 2 * cols, ow), BF16),
        in_specs=[vmem()] * 3,
        out_specs=vmem(),
        scratch_shapes=[
            pltpu.VMEM((2 * pairs, size, 2 * ch), BF16),
            pltpu.VMEM((2 * rows, size, 256), F32),
            pltpu.VMEM((2 * size, 128), F32),
        ],
        compiler_params=params(),
        name="decode",
    )(gathered, gain_res, w2)


def solution(mesh):
    in_specs = (
        P("clip", "rows", None),
        P(),
        P(),
        P(None, None, "section"),
        P(),
        P(None, "section", None),
    )
    out_specs = P("clip", "rows", None, "section")
    return jax.shard_map(body, mesh=mesh, in_specs=in_specs, out_specs=out_specs, check_vma=False)
```

```python
import functools

import jax
import jax.numpy as jnp
from jax import lax
from jax.experimental import pallas as pl
from jax.experimental.pallas import tpu as pltpu
from jax.sharding import PartitionSpec as P

BITS = 18
EPS = 1e-06
F32 = jnp.float32
BF16 = jnp.bfloat16
MIB = 1024 * 1024


def silu(v):
    return 0.5 * v * (1.0 + jnp.tanh(0.5 * v))


def latent_rows(rows, in_proj, gain):
    cols = rows[0].shape[1]
    count = len(rows)
    wide = jnp.concatenate([jnp.broadcast_to(row, (cols, cols)) for row in rows], axis=0)
    sub = lax.broadcasted_iota(jnp.int32, (count, cols, cols), 1).reshape(count * cols, cols)
    lane = lax.broadcasted_iota(jnp.int32, (count * cols, cols), 1)
    picked = jnp.where(sub == lane, wide, 0).astype(F32)
    column = jnp.sum(picked, axis=1, keepdims=True).astype(jnp.int32)
    spread = jnp.broadcast_to(column, (count * cols, BITS))
    shift = lax.broadcasted_iota(jnp.int32, (count * cols, BITS), 1)
    bits = ((jnp.right_shift(spread, shift) & 1) * 2 - 1).astype(F32).astype(BF16)
    latent = jnp.dot(bits, in_proj, preferred_element_type=F32)
    mean = jnp.mean(latent * latent, axis=1, keepdims=True)
    return silu(latent * lax.rsqrt(mean + EPS) * gain)


def prep_kernel(codes_ref, proj_ref, gain_ref, up_hbm, out_hbm, w1_ref, w2_ref, act_ref, up_ref, tap_ref, sems):
    copies = [
        pltpu.make_async_copy(up_hbm.at[pl.ds(9 * a, 9)], up_ref.at[pl.ds(9 * a, 9)], sems.at[a])
        for a in range(3)
    ]
    copies.append(pltpu.make_async_copy(out_hbm, tap_ref, sems.at[3]))
    for copy in copies:
        copy.start()

    frames, rows, cols = codes_ref.shape
    size = frames * cols
    for r in range(rows):
        act = latent_rows([codes_ref[t, r : r + 1, :] for t in range(frames)], proj_ref[...], gain_ref[...])
        act_ref[r] = act.astype(BF16)

    width = up_ref.shape[1]
    out_w = up_ref.shape[2]
    step = 32
    for a in range(3):
        copies[a].wait()

        @pl.loop(0, width // step)
        def _(i, a=a):
            k = pl.multiple_of(i * step, step)
            tap = [[up_ref[9 * a + 3 * b + c, pl.ds(k, step), :].astype(F32) for c in range(3)] for b in range(3)]
            row_sets = (
                ([tap[0][c] + tap[1][c] for c in range(3)], tap[0]),
                (tap[2], [tap[1][c] + tap[2][c] for c in range(3)]),
            )
            for half in range(2):
                for py in range(2):
                    x = row_sets[half][py]
                    parts = (x[0], x[1] + x[2], x[0] + x[1], x[2])
                    for v in range(4):
                        w1_ref[a, pl.ds(half * width + k, step), pl.ds((4 * py + v) * out_w, out_w)] = parts[v].astype(BF16)

    copies[3].wait()
    ow, half_ch = tap_ref.shape[1], tap_ref.shape[2] // 2
    zero = jnp.zeros((ow, half_ch), BF16)
    section = lax.axis_index("section")
    for slot, part in enumerate((section, 1 - section)):
        lanes = pl.ds(pl.multiple_of(part * half_ch, half_ch), half_ch)
        for ab in range(9):
            w = [tap_ref[3 * ab + c, :, lanes] for c in range(3)]
            table = ((w[1], w[2]), (w[0], w[1]), (zero, w[0]), (w[2], zero))
            for n in range(4):
                for px in range(2):
                    w2_ref[ab, pl.ds(n * ow, ow), pl.ds((2 * px + slot) * half_ch, half_ch)] = table[n][px]


def shifted(x, cols, amount):
    rows, lanes = x.shape
    place = lax.broadcasted_iota(jnp.int32, (rows // cols, cols, lanes), 1).reshape(rows, lanes)
    moved = pltpu.roll(x, amount % rows, 0)
    return jnp.where(place == (0 if amount == 1 else cols - 1), 0.0, moved)


def reach(frames, cols, a):
    need = (frames - 2 + a) * cols
    return -(-need // 16) * 16


def hidden_kernel(axis, lo_ref, hi_ref, proj_ref, gain_ref, own_ref, w1_ref, h_ref, act_ref, acc_ref):
    frames, rows, cols = lo_ref.shape
    size = frames * cols
    width = own_ref.shape[2]
    place = lax.axis_index(axis)
    last = lax.axis_size(axis) - 1
    for edge, (src, row, ok) in enumerate(((lo_ref, rows - 1, place > 0), (hi_ref, 0, place < last))):
        act = latent_rows([src[t, row : row + 1, :] for t in range(frames)], proj_ref[...], gain_ref[...])
        act_ref[edge * (rows + 1)] = jnp.where(ok, act, 0.0).astype(BF16)
    act_ref[pl.ds(1, rows)] = own_ref[...]

    pairs = rows + 1

    @pl.loop(0, 4)
    def _(n):
        lanes = pl.ds(pl.multiple_of(n * 256, 256), 256)
        for a in (2, 1, 0):
            m = reach(frames, cols, a)
            total = None
            for half in range(2):
                part = jnp.dot(
                    act_ref[pl.ds(half, pairs), pl.ds(0, m), :].reshape(pairs * m, width),
                    w1_ref[a, pl.ds(half * width, width), lanes],
                    preferred_element_type=F32,
                )
                total = part if total is None else total + part
            total = total.reshape(pairs, m, 256)
            if a == 2:
                acc_ref[...] = total
            else:
                skip = (2 - a) * cols
                acc_ref[:, pl.ds(skip, size - skip), :] += total[:, : size - skip, :]
        full = acc_ref[...].reshape(pairs * size, 256)
        left, right = full[:, :128], full[:, 128:]
        px = n % 2

        @pl.when(px == 0)
        def _():
            h_ref[:, pl.ds(pl.multiple_of(n * 128, 128), 128)] = (right + shifted(left, cols, 1)).astype(BF16)

        @pl.when(px == 1)
        def _():
            h_ref[:, pl.ds(pl.multiple_of(n * 128, 128), 128)] = (left + shifted(right, cols, -1)).astype(BF16)


def out_kernel_body(axis, frames, cols, own_ref, other_ref, gain_ref, w2_ref, o_ref, norm_ref, acc_ref, mix_ref):
    size = frames * cols
    pairs = own_ref.shape[0] // size
    half_ch = own_ref.shape[1] // 4
    section = lax.axis_index("section")
    gains = [gain_ref[:, pl.ds(pl.multiple_of(k * half_ch, half_ch), half_ch)] for k in (section, 1 - section)]
    place = lax.axis_index(axis)
    last = lax.axis_size(axis) - 1
    for q in range(pairs):
        for py in range(2):
            for px in range(2):
                n = 2 * py + px
                x = [r[pl.ds(q * size, size), pl.ds(n * half_ch, half_ch)].astype(F32) for r in (own_ref, other_ref)]
                mean = jnp.sum(x[0] * x[0] + x[1] * x[1], axis=1, keepdims=True) / (2 * half_ch)
                scale = lax.rsqrt(mean + EPS)
                if q == 0 and py == 0:
                    scale = jnp.where(place > 0, scale, 0.0)
                if q == pairs - 1 and py == 1:
                    scale = jnp.where(place < last, scale, 0.0)
                for s in range(2):
                    value = silu(x[s] * scale * gains[s])
                    norm_ref[2 * q + py, :, pl.ds((2 * px + s) * half_ch, half_ch)] = value.astype(BF16)

    height = 2 * (pairs - 1)
    depth = norm_ref.shape[2]
    for a in (2, 1, 0):
        m = reach(frames, cols, a)
        total = None
        for b in range(3):
            part = lax.dot_general(
                norm_ref[pl.ds(b, height), pl.ds(0, m), :].reshape(height * m, depth),
                w2_ref[3 * a + b],
                (((1,), (1,)), ((), ())),
                preferred_element_type=F32,
            )
            total = part if total is None else total + part
        total = total.reshape(height, m, 256)
        if a == 2:
            acc_ref[...] = total
        else:
            skip = (2 - a) * cols
            acc_ref[:, pl.ds(skip, size - skip), :] += total[:, : size - skip, :]

    ow = o_ref.shape[3]
    for y in range(height):
        full = acc_ref[y]
        side = full[:, 128:]
        lane = lax.broadcasted_iota(jnp.int32, side.shape, 1)
        both = full[:, :128] + jnp.where(lane < ow, shifted(side, cols, 1), shifted(side, cols, -1))
        mix_ref[pl.ds(0, size, stride=2), :] = both
        mix_ref[pl.ds(1, size, stride=2), :] = pltpu.roll(both, ow, 1)
        result = mix_ref[...][:, :ow].astype(BF16)
        for t in range(frames):
            o_ref[t, y] = result[2 * cols * t : 2 * cols * (t + 1)]


def params(mib):
    return pltpu.CompilerParams(vmem_limit_bytes=mib * MIB)


def in_vmem(*arrays):
    return tuple(pltpu.with_memory_space_constraint(x, pltpu.VMEM) for x in arrays)


def vmem():
    return pl.BlockSpec(memory_space=pltpu.VMEM)


def body(codes, in_proj, gain_up, up_kernel, gain_res, out_kernel):
    frames, rows, cols = codes.shape
    size = frames * cols
    taps, width, share = up_kernel.shape
    ow, ch = out_kernel.shape[1:]
    count = lax.axis_size("rows")
    forward = [(i, i + 1) for i in range(count - 1)]
    backward = [(i + 1, i) for i in range(count - 1)]
    low = lax.ppermute(codes, "rows", forward)
    high = lax.ppermute(codes, "rows", backward)
    gain_up = gain_up.reshape(1, -1)
    gain_res = gain_res.reshape(1, -1)

    hbm = pl.BlockSpec(memory_space=pl.ANY)
    w1, w2, act = pl.pallas_call(
        prep_kernel,
        out_shape=(
            pltpu.VMEM((3, 2 * width, 8 * share), BF16),
            pltpu.VMEM((9, 4 * ow, 2 * ch), BF16),
            pltpu.VMEM((rows, size, width), BF16),
        ),
        in_specs=[vmem(), vmem(), vmem(), hbm, hbm],
        out_specs=(vmem(), vmem(), vmem()),
        scratch_shapes=[
            pltpu.VMEM(up_kernel.shape, BF16),
            pltpu.VMEM(out_kernel.shape, BF16),
            pltpu.SemaphoreType.DMA((4,)),
        ],
        compiler_params=params(12),
        cost_estimate=pl.CostEstimate(flops=10**9, bytes_accessed=2 * 10**7, transcendentals=0),
        name="prep",
    )(codes, in_proj, gain_up, up_kernel, out_kernel)

    pairs = rows + 1
    w1, w2, act, low, high = in_vmem(w1, w2, act, low, high)
    hidden = pl.pallas_call(
        functools.partial(hidden_kernel, "rows"),
        out_shape=pltpu.VMEM((pairs * size, 4 * share), BF16),
        in_specs=[vmem()] * 6,
        out_specs=vmem(),
        scratch_shapes=[
            pltpu.VMEM((rows + 2, size, width), BF16),
            pltpu.VMEM((pairs, size, 256), F32),
        ],
        compiler_params=params(8),
        name="hidden",
    )(low, high, in_proj, gain_up, act, w1)

    other = lax.ppermute(hidden, "section", [(0, 1), (1, 0)])

    return pl.pallas_call(
        functools.partial(out_kernel_body, "rows", frames, cols),
        out_shape=jax.ShapeDtypeStruct((frames, 2 * rows, 2 * cols, ow), BF16),
        in_specs=[vmem()] * 4,
        out_specs=vmem(),
        scratch_shapes=[
            pltpu.VMEM((2 * pairs, size, 2 * ch), BF16),
            pltpu.VMEM((2 * rows, size, 256), F32),
            pltpu.VMEM((2 * size, 128), F32),
        ],
        compiler_params=params(12),
        name="decode",
    )(*in_vmem(hidden, other), gain_res, w2)


def solution(mesh):
    in_specs = (
        P("clip", "rows", None),
        P(),
        P(),
        P(None, None, "section"),
        P(),
        P(None, "section", None),
    )
    out_specs = P("clip", "rows", None, "section")
    return jax.shard_map(body, mesh=mesh, in_specs=in_specs, out_specs=out_specs, check_vma=False)
```

```python
import functools

import jax
import jax.numpy as jnp
from jax import lax
from jax.experimental import pallas as pl
from jax.experimental.pallas import tpu as pltpu
from jax.sharding import PartitionSpec as P

BITS = 18
EPS = 1e-06
F32 = jnp.float32
BF16 = jnp.bfloat16
MIB = 1024 * 1024


def silu(v):
    return 0.5 * v * (1.0 + jnp.tanh(0.5 * v))


def latent_rows(rows, in_proj, gain):
    cols = rows[0].shape[1]
    count = len(rows)
    wide = jnp.concatenate([jnp.broadcast_to(row, (cols, cols)) for row in rows], axis=0)
    sub = lax.broadcasted_iota(jnp.int32, (count, cols, cols), 1).reshape(count * cols, cols)
    lane = lax.broadcasted_iota(jnp.int32, (count * cols, cols), 1)
    picked = jnp.where(sub == lane, wide, 0).astype(F32)
    column = jnp.sum(picked, axis=1, keepdims=True).astype(jnp.int32)
    spread = jnp.broadcast_to(column, (count * cols, BITS))
    shift = lax.broadcasted_iota(jnp.int32, (count * cols, BITS), 1)
    bits = ((jnp.right_shift(spread, shift) & 1) * 2 - 1).astype(F32).astype(BF16)
    latent = jnp.dot(bits, in_proj, preferred_element_type=F32)
    mean = jnp.mean(latent * latent, axis=1, keepdims=True)
    return silu(latent * lax.rsqrt(mean + EPS) * gain)


def up_prep_kernel(up_hbm, w1_ref, up_ref, sems):
    copies = [
        pltpu.make_async_copy(up_hbm.at[pl.ds(9 * a, 9)], up_ref.at[pl.ds(9 * a, 9)], sems.at[a])
        for a in range(3)
    ]
    for copy in copies:
        copy.start()

    width = up_ref.shape[1]
    out_w = up_ref.shape[2]
    step = 32
    for a in range(3):
        copies[a].wait()

        @pl.loop(0, width // step)
        def _(i, a=a):
            k = pl.multiple_of(i * step, step)
            tap = [[up_ref[9 * a + 3 * b + c, pl.ds(k, step), :].astype(F32) for c in range(3)] for b in range(3)]
            row_sets = (
                ([tap[0][c] + tap[1][c] for c in range(3)], tap[0]),
                (tap[2], [tap[1][c] + tap[2][c] for c in range(3)]),
            )
            for half in range(2):
                for py in range(2):
                    x = row_sets[half][py]
                    parts = (x[0], x[1] + x[2], x[0] + x[1], x[2])
                    for v in range(4):
                        w1_ref[a, pl.ds(half * width + k, step), pl.ds((4 * py + v) * out_w, out_w)] = parts[v].astype(BF16)


def own_prep_kernel(codes_hbm, proj_hbm, gain_hbm, out_hbm, after_ref, w2_ref, act_ref, proj_ref, gain_ref, codes_ref, tap_ref, sems):
    pairs = ((codes_hbm, codes_ref), (proj_hbm, proj_ref), (gain_hbm, gain_ref), (out_hbm, tap_ref))
    copies = [pltpu.make_async_copy(src, dst, sems.at[n]) for n, (src, dst) in enumerate(pairs)]
    for copy in copies:
        copy.start()
    for copy in copies[:3]:
        copy.wait()

    frames, rows, cols = codes_ref.shape
    for r in range(rows):
        act = latent_rows([codes_ref[t, r : r + 1, :] for t in range(frames)], proj_ref[...], gain_ref[...])
        act_ref[r] = act.astype(BF16)

    copies[3].wait()
    ow, half_ch = tap_ref.shape[1], tap_ref.shape[2] // 2
    zero = jnp.zeros((ow, half_ch), BF16)
    section = lax.axis_index("section")
    for slot, part in enumerate((section, 1 - section)):
        lanes = pl.ds(pl.multiple_of(part * half_ch, half_ch), half_ch)
        for ab in range(9):
            w = [tap_ref[3 * ab + c, :, lanes] for c in range(3)]
            table = ((w[1], w[2]), (w[0], w[1]), (zero, w[0]), (w[2], zero))
            for n in range(4):
                for px in range(2):
                    w2_ref[ab, pl.ds(n * ow, ow), pl.ds((2 * px + slot) * half_ch, half_ch)] = table[n][px]


def shifted(x, cols, amount):
    rows, lanes = x.shape
    place = lax.broadcasted_iota(jnp.int32, (rows // cols, cols, lanes), 1).reshape(rows, lanes)
    moved = pltpu.roll(x, amount % rows, 0)
    return jnp.where(place == (0 if amount == 1 else cols - 1), 0.0, moved)


def reach(frames, cols, a):
    need = (frames - 2 + a) * cols
    return -(-need // 16) * 16


def hidden_kernel(axis, near_ref, far_ref, proj_ref, gain_ref, own_ref, w1_ref, h_ref, act_ref, acc_ref):
    frames, rows, cols = near_ref.shape
    size = frames * cols
    width = own_ref.shape[2]
    first = lax.axis_index("section") == 0
    place = lax.axis_index(axis)
    last = lax.axis_size(axis) - 1
    for edge, (row, ok) in enumerate(((rows - 1, place > 0), (0, place < last))):
        one, two = (near_ref, far_ref) if edge == 0 else (far_ref, near_ref)
        codes = [jnp.where(first, one[t, row : row + 1, :], two[t, row : row + 1, :]) for t in range(frames)]
        act = latent_rows(codes, proj_ref[...], gain_ref[...])
        act_ref[edge * (rows + 1)] = jnp.where(ok, act, 0.0).astype(BF16)
    act_ref[pl.ds(1, rows)] = own_ref[...]

    pairs = rows + 1

    @pl.loop(0, 4)
    def _(n):
        lanes = pl.ds(pl.multiple_of(n * 256, 256), 256)
        for a in (2, 1, 0):
            m = reach(frames, cols, a)
            total = None
            for half in range(2):
                part = jnp.dot(
                    act_ref[pl.ds(half, pairs), pl.ds(0, m), :].reshape(pairs * m, width),
                    w1_ref[a, pl.ds(half * width, width), lanes],
                    preferred_element_type=F32,
                )
                total = part if total is None else total + part
            total = total.reshape(pairs, m, 256)
            if a == 2:
                acc_ref[...] = total
            else:
                skip = (2 - a) * cols
                acc_ref[:, pl.ds(skip, size - skip), :] += total[:, : size - skip, :]
        full = acc_ref[...].reshape(pairs * size, 256)
        left, right = full[:, :128], full[:, 128:]
        px = n % 2

        @pl.when(px == 0)
        def _():
            h_ref[:, pl.ds(pl.multiple_of(n * 128, 128), 128)] = (right + shifted(left, cols, 1)).astype(BF16)

        @pl.when(px == 1)
        def _():
            h_ref[:, pl.ds(pl.multiple_of(n * 128, 128), 128)] = (left + shifted(right, cols, -1)).astype(BF16)


def out_kernel_body(axis, frames, cols, own_ref, other_ref, gain_ref, w2_ref, o_ref, norm_ref, acc_ref, mix_ref):
    size = frames * cols
    pairs = own_ref.shape[0] // size
    half_ch = own_ref.shape[1] // 4
    section = lax.axis_index("section")
    gains = [gain_ref[:, pl.ds(pl.multiple_of(k * half_ch, half_ch), half_ch)] for k in (section, 1 - section)]
    place = lax.axis_index(axis)
    last = lax.axis_size(axis) - 1
    for q in range(pairs):
        for py in range(2):
            for px in range(2):
                n = 2 * py + px
                x = [r[pl.ds(q * size, size), pl.ds(n * half_ch, half_ch)].astype(F32) for r in (own_ref, other_ref)]
                mean = jnp.sum(x[0] * x[0] + x[1] * x[1], axis=1, keepdims=True) / (2 * half_ch)
                scale = lax.rsqrt(mean + EPS)
                if q == 0 and py == 0:
                    scale = jnp.where(place > 0, scale, 0.0)
                if q == pairs - 1 and py == 1:
                    scale = jnp.where(place < last, scale, 0.0)
                for s in range(2):
                    value = silu(x[s] * scale * gains[s])
                    norm_ref[2 * q + py, :, pl.ds((2 * px + s) * half_ch, half_ch)] = value.astype(BF16)

    height = 2 * (pairs - 1)
    depth = norm_ref.shape[2]
    for a in (2, 1, 0):
        m = reach(frames, cols, a)
        total = None
        for b in range(3):
            part = lax.dot_general(
                norm_ref[pl.ds(b, height), pl.ds(0, m), :].reshape(height * m, depth),
                w2_ref[3 * a + b],
                (((1,), (1,)), ((), ())),
                preferred_element_type=F32,
            )
            total = part if total is None else total + part
        total = total.reshape(height, m, 256)
        if a == 2:
            acc_ref[...] = total
        else:
            skip = (2 - a) * cols
            acc_ref[:, pl.ds(skip, size - skip), :] += total[:, : size - skip, :]

    ow = o_ref.shape[3]
    for y in range(height):
        full = acc_ref[y]
        side = full[:, 128:]
        lane = lax.broadcasted_iota(jnp.int32, side.shape, 1)
        both = full[:, :128] + jnp.where(lane < ow, shifted(side, cols, 1), shifted(side, cols, -1))
        mix_ref[pl.ds(0, size, stride=2), :] = both
        mix_ref[pl.ds(1, size, stride=2), :] = pltpu.roll(both, ow, 1)
        result = mix_ref[...][:, :ow].astype(BF16)
        for t in range(frames):
            o_ref[t, y] = result[2 * cols * t : 2 * cols * (t + 1)]


def params(mib):
    return pltpu.CompilerParams(vmem_limit_bytes=mib * MIB)


def vmem():
    return pl.BlockSpec(memory_space=pltpu.VMEM)


def in_space(space, *arrays):
    return tuple(pltpu.with_memory_space_constraint(x, space) for x in arrays)


def body(codes, in_proj, gain_up, up_kernel, gain_res, out_kernel):
    frames, rows, cols = codes.shape
    size = frames * cols
    width, share = up_kernel.shape[1:]
    ow, ch = out_kernel.shape[1:]
    pairs = rows + 1
    count = lax.axis_size("rows")
    joint = [(2 * i, 2 * i + 2) for i in range(count - 1)] + [(2 * i + 3, 2 * i + 1) for i in range(count - 1)]
    swap = [(0, 1), (1, 0)]
    near = lax.ppermute(codes, ("rows", "section"), joint)
    far = lax.ppermute(near, "section", swap)
    gain_res = gain_res.reshape(1, -1)
    up_kernel, out_kernel, codes, in_proj, gain_up = in_space(
        pltpu.HBM, up_kernel, out_kernel, codes, in_proj, gain_up.reshape(1, -1)
    )

    hbm = pl.BlockSpec(memory_space=pltpu.HBM)
    w1 = pl.pallas_call(
        up_prep_kernel,
        out_shape=pltpu.VMEM((3, 2 * width, 8 * share), BF16),
        in_specs=[hbm],
        out_specs=vmem(),
        scratch_shapes=[pltpu.VMEM(up_kernel.shape, BF16), pltpu.SemaphoreType.DMA((3,))],
        compiler_params=params(8),
        cost_estimate=pl.CostEstimate(flops=10**9, bytes_accessed=2 * 10**7, transcendentals=0),
        name="up_prep",
    )(up_kernel)
    near, far = in_space(pltpu.VMEM, near, far)
    w2, act, proj, gain = pl.pallas_call(
        own_prep_kernel,
        out_shape=(
            pltpu.VMEM((9, 4 * ow, 2 * ch), BF16),
            pltpu.VMEM((rows, size, width), BF16),
            pltpu.VMEM(in_proj.shape, BF16),
            pltpu.VMEM(gain_up.shape, F32),
        ),
        in_specs=[hbm] * 4 + [vmem()],
        out_specs=(vmem(),) * 4,
        scratch_shapes=[
            pltpu.VMEM(codes.shape, jnp.int32),
            pltpu.VMEM(out_kernel.shape, BF16),
            pltpu.SemaphoreType.DMA((4,)),
        ],
        compiler_params=params(8),
        cost_estimate=pl.CostEstimate(flops=10**8, bytes_accessed=10**7, transcendentals=0),
        name="own_prep",
    )(codes, in_proj, gain_up, out_kernel, near)

    w1, w2, act, proj, gain = in_space(pltpu.VMEM, w1, w2, act, proj, gain)
    hidden = pl.pallas_call(
        functools.partial(hidden_kernel, "rows"),
        out_shape=pltpu.VMEM((pairs * size, 4 * share), BF16),
        in_specs=[vmem()] * 6,
        out_specs=vmem(),
        scratch_shapes=[
            pltpu.VMEM((rows + 2, size, width), BF16),
            pltpu.VMEM((pairs, size, 256), F32),
        ],
        compiler_params=params(8),
        name="hidden",
    )(near, far, proj, gain, act, w1)

    other = lax.ppermute(hidden, "section", swap)

    return pl.pallas_call(
        functools.partial(out_kernel_body, "rows", frames, cols),
        out_shape=jax.ShapeDtypeStruct((frames, 2 * rows, 2 * cols, ow), BF16),
        in_specs=[vmem()] * 4,
        out_specs=vmem(),
        scratch_shapes=[
            pltpu.VMEM((2 * pairs, size, 2 * ch), BF16),
            pltpu.VMEM((2 * rows, size, 256), F32),
            pltpu.VMEM((2 * size, 128), F32),
        ],
        compiler_params=params(12),
        name="decode",
    )(*in_space(pltpu.VMEM, hidden, other), gain_res, w2)


def solution(mesh):
    in_specs = (
        P("clip", "rows", None),
        P(),
        P(),
        P(None, None, "section"),
        P(),
        P(None, "section", None),
    )
    out_specs = P("clip", "rows", None, "section")
    return jax.shard_map(body, mesh=mesh, in_specs=in_specs, out_specs=out_specs, check_vma=False)
```

```python
import functools

import jax
import jax.numpy as jnp
from jax import lax
from jax.experimental import pallas as pl
from jax.experimental.pallas import tpu as pltpu
from jax.sharding import PartitionSpec as P

BITS = 18
EPS = 1e-06
F32 = jnp.float32
BF16 = jnp.bfloat16
SPLIT = 6
MIB = 1024 * 1024


def silu(v):
    return 0.5 * v * (1.0 + jnp.tanh(0.5 * v))


def latent_rows(rows, in_proj, gain):
    cols = rows[0].shape[1]
    count = len(rows)
    wide = jnp.concatenate([jnp.broadcast_to(row, (cols, cols)) for row in rows], axis=0)
    sub = lax.broadcasted_iota(jnp.int32, (count, cols, cols), 1).reshape(count * cols, cols)
    lane = lax.broadcasted_iota(jnp.int32, (count * cols, cols), 1)
    picked = jnp.where(sub == lane, wide, 0).astype(F32)
    column = jnp.sum(picked, axis=1, keepdims=True).astype(jnp.int32)
    spread = jnp.broadcast_to(column, (count * cols, BITS))
    shift = lax.broadcasted_iota(jnp.int32, (count * cols, BITS), 1)
    bits = ((jnp.right_shift(spread, shift) & 1) * 2 - 1).astype(F32).astype(BF16)
    latent = jnp.dot(bits, in_proj, preferred_element_type=F32)
    mean = jnp.mean(latent * latent, axis=1, keepdims=True)
    return silu(latent * lax.rsqrt(mean + EPS) * gain)


def products(act, frame_rows, w_ref, acc_ref, start, stop):
    n = frame_rows
    share = w_ref.shape[2]

    def taps(a, first, count):
        return jnp.concatenate([w_ref[9 * a + first + k] for k in range(count)], axis=1)

    def dot(frames, weights):
        return jnp.dot(act[pl.ds(0, frames * n), :], weights, preferred_element_type=F32)

    def put(first, lanes, p2, p1, p0):
        lanes = pl.ds((first - start) * share, lanes)
        acc_ref[pl.ds(0, n), lanes] = p2[:n]
        acc_ref[pl.ds(n, n), lanes] = p2[n : 2 * n] + p1[:n]
        acc_ref[pl.ds(2 * n, 2 * n), lanes] = p2[2 * n :] + p1[n : 3 * n] + p0

    for first in range(start, stop - 1, 2):
        put(first, 2 * share, dot(4, taps(2, first, 2)), dot(3, taps(1, first, 2)), dot(2, taps(0, first, 2)))
    if (stop - start) % 2:
        k = stop - 1
        both = dot(4, jnp.concatenate([w_ref[18 + k], w_ref[9 + k]], axis=1))
        put(k, share, both[:, :share], both[:, share:], dot(2, w_ref[k]))


def own_kernel(codes_hbm, proj_hbm, gain_hbm, up_hbm, acc_ref, act_ref, w_ref, proj_ref, gain_ref, codes_ref, sems):
    pairs = [(codes_hbm, codes_ref), (proj_hbm, proj_ref), (gain_hbm, gain_ref)]
    pairs += [(up_hbm.at[pl.ds(9 * a, 9)], w_ref.at[pl.ds(9 * a, 9)]) for a in range(3)]
    copies = [pltpu.make_async_copy(src, dst, sems.at[n]) for n, (src, dst) in enumerate(pairs)]
    for copy in copies:
        copy.start()
    for copy in copies[:3]:
        copy.wait()
    frames, rows, cols = codes_ref.shape
    codes = [codes_ref[t, r : r + 1, :] for t in range(frames) for r in range(rows)]
    act_ref[...] = latent_rows(codes, proj_ref[...], gain_ref[...]).astype(BF16)
    for copy in copies[3:]:
        copy.wait()
    products(act_ref, rows * cols, w_ref, acc_ref, 0, SPLIT)


def rest_kernel(frame_rows, act_ref, w_ref, after_ref, acc_ref):
    products(act_ref, frame_rows, w_ref, acc_ref, SPLIT, 9)


def tap_kernel(out_hbm, w2_ref, tap_ref, sem):
    copy = pltpu.make_async_copy(out_hbm, tap_ref, sem)
    copy.start()
    copy.wait()
    ow, half_ch = tap_ref.shape[1], tap_ref.shape[2] // 2
    zero = jnp.zeros((ow, half_ch), BF16)
    section = lax.axis_index("section")
    for slot, part in enumerate((section, 1 - section)):
        lanes = pl.ds(pl.multiple_of(part * half_ch, half_ch), half_ch)
        for ab in range(9):
            w = [tap_ref[3 * ab + c, :, lanes] for c in range(3)]
            table = ((w[1], w[2]), (w[0], w[1]), (zero, w[0]), (w[2], zero))
            for n in range(4):
                for px in range(2):
                    w2_ref[ab, pl.ds(n * ow, ow), pl.ds((2 * px + slot) * half_ch, half_ch)] = table[n][px]


def shifted(x, cols, amount):
    rows, lanes = x.shape
    place = lax.broadcasted_iota(jnp.int32, (rows // cols, cols, lanes), 1).reshape(rows, lanes)
    moved = pltpu.roll(x, amount % rows, 0)
    return jnp.where(place == (0 if amount == 1 else cols - 1), 0.0, moved)


def reach(frames, cols, a):
    need = (frames - 2 + a) * cols
    return -(-need // 16) * 16


def hidden_kernel(near_ref, far_ref, proj_ref, gain_ref, w_ref, own_ref, rest_ref, h_ref, act_ref, halo_ref):
    frames, rows, cols = near_ref.shape
    share = w_ref.shape[2]
    size = frames * cols
    first = lax.axis_index("section") == 0
    place = lax.axis_index("rows")
    last = lax.axis_size("rows") - 1
    codes = []
    for t in range(frames):
        low = [ref[t, rows - 1 : rows, :] for ref in (near_ref, far_ref)]
        high = [ref[t, 0:1, :] for ref in (near_ref, far_ref)]
        codes += [jnp.where(first, low[0], low[1]), jnp.where(first, high[1], high[0])]
    act = latent_rows(codes, proj_ref[...], gain_ref[...])
    edge = lax.broadcasted_iota(jnp.int32, (frames, 2, cols, act.shape[1]), 1).reshape(act.shape)
    keep = jnp.where(edge == 0, (place > 0).astype(F32), (place < last).astype(F32))
    act_ref[...] = (act * keep).astype(BF16)
    products(act_ref, 2 * cols, w_ref, halo_ref, 0, 9)

    def taken(slot, pair, tap):
        ref = own_ref
        if slot in (0, rows + 1):
            ref, span, row = halo_ref, 2 * cols, 0 if slot == 0 else 1
        else:
            span, row = rows * cols, slot - 1
            if tap >= SPLIT:
                ref, tap = rest_ref, tap - SPLIT
        lanes = pl.ds(tap * share, share)
        return jnp.concatenate([ref[pl.ds(t * span + row * cols, cols), lanes] for t in (2 * pair, 2 * pair + 1)], axis=0)

    for pair in range(frames // 2):
        for q in range(rows + 1):
            sums = [[], []]
            for c in range(3):
                x = taken(q, pair, c) + taken(q + 1, pair, 6 + c)
                sums[0].append(x + taken(q, pair, 3 + c))
                sums[1].append(x + taken(q + 1, pair, 3 + c))
            out = pl.ds(q * size + pair * 2 * cols, 2 * cols)
            for py, (left, mid, right) in enumerate(sums):
                even = shifted(left, cols, 1) + (mid + right)
                odd = (left + mid) + shifted(right, cols, -1)
                h_ref[out, pl.ds(2 * py * share, share)] = even.astype(BF16)
                h_ref[out, pl.ds((2 * py + 1) * share, share)] = odd.astype(BF16)


def out_kernel_body(axis, frames, cols, own_ref, other_ref, gain_ref, w2_ref, o_ref, norm_ref, acc_ref, mix_ref):
    size = frames * cols
    pairs = own_ref.shape[0] // size
    half_ch = own_ref.shape[1] // 4
    section = lax.axis_index("section")
    gains = [gain_ref[:, pl.ds(pl.multiple_of(k * half_ch, half_ch), half_ch)] for k in (section, 1 - section)]
    place = lax.axis_index(axis)
    last = lax.axis_size(axis) - 1
    for q in range(pairs):
        for py in range(2):
            for px in range(2):
                n = 2 * py + px
                x = [r[pl.ds(q * size, size), pl.ds(n * half_ch, half_ch)].astype(F32) for r in (own_ref, other_ref)]
                mean = jnp.sum(x[0] * x[0] + x[1] * x[1], axis=1, keepdims=True) / (2 * half_ch)
                scale = lax.rsqrt(mean + EPS)
                if q == 0 and py == 0:
                    scale = jnp.where(place > 0, scale, 0.0)
                if q == pairs - 1 and py == 1:
                    scale = jnp.where(place < last, scale, 0.0)
                for s in range(2):
                    value = silu(x[s] * scale * gains[s])
                    norm_ref[2 * q + py, :, pl.ds((2 * px + s) * half_ch, half_ch)] = value.astype(BF16)

    height = 2 * (pairs - 1)
    depth = norm_ref.shape[2]
    for a in (2, 1, 0):
        m = reach(frames, cols, a)
        total = None
        for b in range(3):
            part = lax.dot_general(
                norm_ref[pl.ds(b, height), pl.ds(0, m), :].reshape(height * m, depth),
                w2_ref[3 * a + b],
                (((1,), (1,)), ((), ())),
                preferred_element_type=F32,
            )
            total = part if total is None else total + part
        total = total.reshape(height, m, 256)
        if a == 2:
            acc_ref[...] = total
        else:
            skip = (2 - a) * cols
            acc_ref[:, pl.ds(skip, size - skip), :] += total[:, : size - skip, :]

    ow = o_ref.shape[3]
    for y in range(height):
        full = acc_ref[y]
        side = full[:, 128:]
        lane = lax.broadcasted_iota(jnp.int32, side.shape, 1)
        both = full[:, :128] + jnp.where(lane < ow, shifted(side, cols, 1), shifted(side, cols, -1))
        mix_ref[pl.ds(0, size, stride=2), :] = both
        mix_ref[pl.ds(1, size, stride=2), :] = pltpu.roll(both, ow, 1)
        result = mix_ref[...][:, :ow].astype(BF16)
        for t in range(frames):
            o_ref[t, y] = result[2 * cols * t : 2 * cols * (t + 1)]


def params(mib):
    return pltpu.CompilerParams(vmem_limit_bytes=mib * MIB)


def vmem():
    return pl.BlockSpec(memory_space=pltpu.VMEM)


def in_space(space, *arrays):
    return tuple(pltpu.with_memory_space_constraint(x, space) for x in arrays)


def body(codes, in_proj, gain_up, up_kernel, gain_res, out_kernel):
    frames, rows, cols = codes.shape
    size = frames * cols
    width, share = up_kernel.shape[1:]
    ow, ch = out_kernel.shape[1:]
    pairs = rows + 1
    count = lax.axis_size("rows")
    joint = [(2 * i, 2 * i + 2) for i in range(count - 1)] + [(2 * i + 3, 2 * i + 1) for i in range(count - 1)]
    swap = [(0, 1), (1, 0)]
    near = lax.ppermute(codes, ("rows", "section"), joint)
    gain_res = gain_res.reshape(1, -1)
    up_kernel, out_kernel, codes, in_proj, gain_up = in_space(
        pltpu.HBM, up_kernel, out_kernel, codes, in_proj, gain_up.reshape(1, -1)
    )

    hbm = pl.BlockSpec(memory_space=pltpu.HBM)
    own, act, w1, proj, gain = pl.pallas_call(
        own_kernel,
        out_shape=(
            pltpu.VMEM((rows * size, SPLIT * share), F32),
            pltpu.VMEM((rows * size, width), BF16),
            pltpu.VMEM(up_kernel.shape, BF16),
            pltpu.VMEM(in_proj.shape, BF16),
            pltpu.VMEM(gain_up.shape, F32),
        ),
        in_specs=[hbm] * 4,
        out_specs=(vmem(),) * 5,
        scratch_shapes=[
            pltpu.VMEM(codes.shape, jnp.int32),
            pltpu.SemaphoreType.DMA((6,)),
        ],
        compiler_params=params(8),
        cost_estimate=pl.CostEstimate(flops=10**9, bytes_accessed=2 * 10**7, transcendentals=0),
        name="own",
    )(codes, in_proj, gain_up, up_kernel)
    own, act, w1, proj, gain = in_space(pltpu.VMEM, own, act, w1, proj, gain)
    near, proj = lax.optimization_barrier((near, proj))
    far = lax.ppermute(near, "section", swap)
    near, far = in_space(pltpu.VMEM, near, far)
    rest = pl.pallas_call(
        functools.partial(rest_kernel, rows * cols),
        out_shape=pltpu.VMEM((rows * size, (9 - SPLIT) * share), F32),
        in_specs=[vmem()] * 3,
        out_specs=vmem(),
        compiler_params=params(4),
        cost_estimate=pl.CostEstimate(flops=10**9, bytes_accessed=10**7, transcendentals=0),
        name="rest",
    )(act, w1, near)
    w2 = pl.pallas_call(
        tap_kernel,
        out_shape=pltpu.VMEM((9, 4 * ow, 2 * ch), BF16),
        in_specs=[hbm],
        out_specs=vmem(),
        scratch_shapes=[pltpu.VMEM(out_kernel.shape, BF16), pltpu.SemaphoreType.DMA],
        compiler_params=params(4),
        cost_estimate=pl.CostEstimate(flops=10**8, bytes_accessed=10**7, transcendentals=0),
        name="taps",
    )(out_kernel)

    rest, w2 = in_space(pltpu.VMEM, rest, w2)
    hidden = pl.pallas_call(
        hidden_kernel,
        out_shape=pltpu.VMEM((pairs * size, 4 * share), BF16),
        in_specs=[vmem()] * 7,
        out_specs=vmem(),
        scratch_shapes=[
            pltpu.VMEM((2 * size, width), BF16),
            pltpu.VMEM((2 * size, 9 * share), F32),
        ],
        compiler_params=params(8),
        name="hidden",
    )(near, far, proj, gain, w1, own, rest)

    other = lax.ppermute(hidden, "section", swap)

    return pl.pallas_call(
        functools.partial(out_kernel_body, "rows", frames, cols),
        out_shape=jax.ShapeDtypeStruct((frames, 2 * rows, 2 * cols, ow), BF16),
        in_specs=[vmem()] * 4,
        out_specs=vmem(),
        scratch_shapes=[
            pltpu.VMEM((2 * pairs, size, 2 * ch), BF16),
            pltpu.VMEM((2 * rows, size, 256), F32),
            pltpu.VMEM((2 * size, 128), F32),
        ],
        compiler_params=params(12),
        name="decode",
    )(*in_space(pltpu.VMEM, hidden, other), gain_res, w2)


def solution(mesh):
    in_specs = (
        P("clip", "rows", None),
        P(),
        P(),
        P(None, None, "section"),
        P(),
        P(None, "section", None),
    )
    out_specs = P("clip", "rows", None, "section")
    return jax.shard_map(body, mesh=mesh, in_specs=in_specs, out_specs=out_specs, check_vma=False)
```

```python
import functools

import jax
import jax.numpy as jnp
from jax import lax
from jax.experimental import pallas as pl
from jax.experimental.pallas import tpu as pltpu
from jax.sharding import PartitionSpec as P

BITS = 18
EPS = 1e-06
F32 = jnp.float32
BF16 = jnp.bfloat16
MIB = 1024 * 1024
GROUPS = ((0, 2), (2, 2), (4, 2), (6, 2), (8, 1))


def silu(v):
    return 0.5 * v * (1.0 + jnp.tanh(0.5 * v))


def latent_rows(rows, in_proj, gain):
    cols = rows[0].shape[1]
    count = len(rows)
    wide = jnp.concatenate([jnp.broadcast_to(row, (cols, cols)) for row in rows], axis=0)
    sub = lax.broadcasted_iota(jnp.int32, (count, cols, cols), 1).reshape(count * cols, cols)
    lane = lax.broadcasted_iota(jnp.int32, (count * cols, cols), 1)
    picked = jnp.where(sub == lane, wide, 0).astype(F32)
    column = jnp.sum(picked, axis=1, keepdims=True).astype(jnp.int32)
    spread = jnp.broadcast_to(column, (count * cols, BITS))
    shift = lax.broadcasted_iota(jnp.int32, (count * cols, BITS), 1)
    bits = ((jnp.right_shift(spread, shift) & 1) * 2 - 1).astype(F32).astype(BF16)
    latent = jnp.dot(bits, in_proj, preferred_element_type=F32)
    mean = jnp.mean(latent * latent, axis=1, keepdims=True)
    return silu(latent * lax.rsqrt(mean + EPS) * gain)


def shifted(x, cols, amount):
    rows, lanes = x.shape
    place = lax.broadcasted_iota(jnp.int32, (rows // cols, cols, lanes), 1).reshape(rows, lanes)
    moved = pltpu.roll(x, amount % rows, 0)
    return jnp.where(place == (0 if amount == 1 else cols - 1), 0.0, moved)


def weights(w_ref, a, group):
    return jnp.concatenate([w_ref[9 * a + group[0] + k] for k in range(group[1])], axis=1)


def early_products(act, n, w_ref, acc_ref, group):
    lanes = pl.ds(group[0] * w_ref.shape[2], group[1] * w_ref.shape[2])
    if group[1] == 1:
        both = jnp.concatenate([weights(w_ref, 2, group), weights(w_ref, 1, group)], axis=1)
        now = jnp.dot(act[pl.ds(0, 2 * n), :], both, preferred_element_type=F32)
        half = w_ref.shape[2]
        now, back = now[:, :half], now[:n, half:]
    else:
        now = jnp.dot(act[pl.ds(0, 2 * n), :], weights(w_ref, 2, group), preferred_element_type=F32)
        back = jnp.dot(act[pl.ds(0, n), :], weights(w_ref, 1, group), preferred_element_type=F32)
    acc_ref[pl.ds(0, n), lanes] = now[:n]
    acc_ref[pl.ds(n, n), lanes] = now[n:] + back


def late_products(act, n, w_ref, acc_ref, group):
    lanes = pl.ds(group[0] * w_ref.shape[2], group[1] * w_ref.shape[2])
    left = jnp.concatenate([act[pl.ds(a * n, 2 * n), :] for a in range(3)], axis=1)
    right = jnp.concatenate([weights(w_ref, a, group) for a in range(3)], axis=0)
    acc_ref[:, lanes] = jnp.dot(left, right, preferred_element_type=F32)


def own_kernel(codes_hbm, proj_hbm, gain_hbm, up_hbm, out_hbm, acc_ref, act_ref, w_ref, tap_ref, proj_ref, gain_ref, codes_ref, sems):
    pairs = [(codes_hbm, codes_ref), (proj_hbm, proj_ref), (gain_hbm, gain_ref)]
    for first, count in GROUPS:
        for a in range(3):
            part = pl.ds(9 * a + first, count)
            pairs.append((up_hbm.at[part], w_ref.at[part]))
    pairs.append((out_hbm, tap_ref))
    copies = [pltpu.make_async_copy(src, dst, sems.at[n]) for n, (src, dst) in enumerate(pairs)]
    for copy in copies:
        copy.start()
    for copy in copies[:3]:
        copy.wait()
    frames, rows, cols = codes_ref.shape
    codes = [codes_ref[t, r : r + 1, :] for t in range(frames) for r in range(rows)]
    act_ref[...] = latent_rows(codes, proj_ref[...], gain_ref[...]).astype(BF16)
    for g, group in enumerate(GROUPS):
        for copy in copies[3 + 3 * g : 6 + 3 * g]:
            copy.wait()
        early_products(act_ref, rows * cols, w_ref, acc_ref, group)
    copies[-1].wait()


def late_kernel(n, act_ref, w_ref, after_ref, acc_ref):
    for group in GROUPS:
        late_products(act_ref, n, w_ref, acc_ref, group)


def combine(rows, cols, share, own_ref, halo_ref, h_ref):
    def taken(slot, tap):
        if slot in (0, rows + 1):
            ref, span, row = halo_ref, 2 * cols, 0 if slot == 0 else 1
        else:
            ref, span, row = own_ref, rows * cols, slot - 1
        lanes = pl.ds(tap * share, share)
        return jnp.concatenate([ref[pl.ds(t * span + row * cols, cols), lanes] for t in range(2)], axis=0)

    for q in range(rows + 1):
        sums = [[], []]
        for c in range(3):
            x = taken(q, c) + taken(q + 1, 6 + c)
            sums[0].append(x + taken(q, 3 + c))
            sums[1].append(x + taken(q + 1, 3 + c))
        out = pl.ds(q * 2 * cols, 2 * cols)
        for py, (left, mid, right) in enumerate(sums):
            even = shifted(left, cols, 1) + (mid + right)
            odd = (left + mid) + shifted(right, cols, -1)
            h_ref[out, pl.ds(2 * py * share, share)] = even.astype(BF16)
            h_ref[out, pl.ds((2 * py + 1) * share, share)] = odd.astype(BF16)


def early_hidden_kernel(near_ref, far_ref, proj_ref, gain_ref, w_ref, own_ref, h_ref, act_ref, halo_ref):
    frames, rows, cols = near_ref.shape
    first = lax.axis_index("section") == 0
    place = lax.axis_index("rows")
    last = lax.axis_size("rows") - 1
    codes = []
    for t in range(frames):
        low = [ref[t, rows - 1 : rows, :] for ref in (near_ref, far_ref)]
        high = [ref[t, 0:1, :] for ref in (near_ref, far_ref)]
        codes += [jnp.where(first, low[0], low[1]), jnp.where(first, high[1], high[0])]
    act = latent_rows(codes, proj_ref[...], gain_ref[...])
    edge = lax.broadcasted_iota(jnp.int32, (frames, 2, cols, act.shape[1]), 1).reshape(act.shape)
    keep = jnp.where(edge == 0, (place > 0).astype(F32), (place < last).astype(F32))
    act_ref[...] = (act * keep).astype(BF16)
    for group in GROUPS:
        early_products(act_ref, 2 * cols, w_ref, halo_ref, group)
    combine(rows, cols, w_ref.shape[2], own_ref, halo_ref, h_ref)


def late_hidden_kernel(rows, cols, act_ref, w_ref, own_ref, h_ref, halo_ref):
    for group in GROUPS:
        late_products(act_ref, 2 * cols, w_ref, halo_ref, group)
    combine(rows, cols, w_ref.shape[2], own_ref, halo_ref, h_ref)


def normalise(size, own_ref, other_ref, gain_ref, norm_ref):
    pairs = own_ref.shape[0] // size
    part = own_ref.shape[1] // 4
    section = lax.axis_index("section")
    starts = [pl.multiple_of(k * part, part) for k in (section, 1 - section)]
    gains = [gain_ref[:, pl.ds(start, part)] for start in starts]
    place = lax.axis_index("rows")
    last = lax.axis_size("rows") - 1
    for q in range(pairs):
        for py in range(2):
            for px in range(2):
                lanes = pl.ds((2 * py + px) * part, part)
                x = [ref[pl.ds(q * size, size), lanes].astype(F32) for ref in (own_ref, other_ref)]
                mean = jnp.sum(x[0] * x[0] + x[1] * x[1], axis=1, keepdims=True) / (2 * part)
                scale = lax.rsqrt(mean + EPS)
                if q == 0 and py == 0:
                    scale = jnp.where(place > 0, scale, 0.0)
                if q == pairs - 1 and py == 1:
                    scale = jnp.where(place < last, scale, 0.0)
                for s in range(2):
                    value = silu(x[s] * scale * gains[s])
                    norm_ref[2 * q + py, :, pl.ds(starts[s] + 2 * px * part, part)] = value.astype(BF16)


def out_products(norm_ref, tap_ref, a, m):
    height = norm_ref.shape[0] - 2
    depth = norm_ref.shape[2]
    left = [norm_ref[pl.ds(b, height), pl.ds(0, m), :].reshape(height * m, depth) for b in range(3)]
    lines = [[], [], [], []]
    for b in range(3):
        w = [tap_ref[9 * a + 3 * b + c] for c in range(3)]
        zero = jnp.zeros_like(w[0])
        for line, cells in zip(lines, ((w[1], w[2]), (w[0], w[1]), (zero, w[0]), (w[2], zero))):
            line += cells
    right = jnp.concatenate([jnp.concatenate(line, axis=1) for line in lines], axis=0)
    total = lax.dot_general(
        jnp.concatenate(left, axis=1), right, (((1,), (1,)), ((), ())), preferred_element_type=F32
    )
    return total.reshape(height, m, right.shape[0])


def finish(y, full, cols, o_ref, mix_ref):
    rows = full.shape[0]
    ow = o_ref.shape[3]
    side = full[:, 2 * ow :]
    lane = lax.broadcasted_iota(jnp.int32, side.shape, 1)
    both = full[:, : 2 * ow] + jnp.where(lane < ow, shifted(side, cols, 1), shifted(side, cols, -1))
    mix_ref[y, pl.ds(0, rows, stride=2), :] = both
    mix_ref[y, pl.ds(1, rows, stride=2), :] = pltpu.roll(both, ow, 1)
    result = mix_ref[y][:, :ow].astype(BF16)
    for t in range(2):
        o_ref[t, y] = result[rows * t : rows * (t + 1)]


def early_out_kernel(cols, own_ref, other_ref, gain_ref, tap_ref, o_ref, acc_ref, norm_ref, mix_ref):
    size = 2 * cols
    normalise(size, own_ref, other_ref, gain_ref, norm_ref)
    now = out_products(norm_ref, tap_ref, 2, size)
    back = out_products(norm_ref, tap_ref, 1, size)
    acc_ref[...] = out_products(norm_ref, tap_ref, 0, size)
    acc_ref[:, pl.ds(0, cols), :] += back[:, cols:]
    for y in range(now.shape[0]):
        full = jnp.concatenate([now[y, :cols], now[y, cols:] + back[y, :cols]], axis=0)
        finish(y, full, cols, o_ref, mix_ref)


def late_out_kernel(cols, own_ref, other_ref, gain_ref, tap_ref, early_ref, acc_ref, o_hbm, o_ref, norm_ref, mix_ref, sems):
    size = 2 * cols
    first = pltpu.make_async_copy(early_ref, o_hbm.at[pl.ds(0, 2)], sems.at[0])
    first.start()
    normalise(size, own_ref, other_ref, gain_ref, norm_ref)
    now = out_products(norm_ref, tap_ref, 2, size)
    back = out_products(norm_ref, tap_ref, 1, -(-cols // 16) * 16)
    for y in range(now.shape[0]):
        held = acc_ref[y]
        full = jnp.concatenate([held[:cols] + now[y, :cols], held[cols:] + now[y, cols:] + back[y, :cols]], axis=0)
        finish(y, full, cols, o_ref, mix_ref)
    second = pltpu.make_async_copy(o_ref, o_hbm.at[pl.ds(2, 2)], sems.at[1])
    second.start()
    first.wait()
    second.wait()


def params(mib):
    return pltpu.CompilerParams(vmem_limit_bytes=mib * MIB)


def cost(mflops):
    return pl.CostEstimate(flops=mflops * 10**6, bytes_accessed=10**7, transcendentals=0)


def vmem():
    return pl.BlockSpec(memory_space=pltpu.VMEM)


def in_space(space, *arrays):
    return tuple(pltpu.with_memory_space_constraint(x, space) for x in arrays)


def body(codes, in_proj, gain_up, up_kernel, gain_res, out_kernel):
    frames, rows, cols = codes.shape
    size = 2 * cols
    width, share = up_kernel.shape[1:]
    ow, ch = out_kernel.shape[1:]
    pairs = rows + 1
    height = 2 * rows
    count = lax.axis_size("rows")
    joint = [(2 * i, 2 * i + 2) for i in range(count - 1)] + [(2 * i + 3, 2 * i + 1) for i in range(count - 1)]
    swap = [(0, 1), (1, 0)]
    near = lax.ppermute(codes, ("rows", "section"), joint)
    gain_res = gain_res.reshape(1, -1)
    up_kernel, out_kernel, codes, in_proj, gain_up = in_space(
        pltpu.HBM, up_kernel, out_kernel, codes, in_proj, gain_up.reshape(1, -1)
    )
    hbm = pl.BlockSpec(memory_space=pltpu.HBM)
    hidden_shape = pltpu.VMEM((pairs * size, 4 * share), BF16)

    own_early, act, w, tap, proj, gain = pl.pallas_call(
        own_kernel,
        out_shape=(
            pltpu.VMEM((2 * rows * cols, 9 * share), F32),
            pltpu.VMEM((frames * rows * cols, width), BF16),
            pltpu.VMEM(up_kernel.shape, BF16),
            pltpu.VMEM(out_kernel.shape, BF16),
            pltpu.VMEM(in_proj.shape, BF16),
            pltpu.VMEM(gain_up.shape, F32),
        ),
        in_specs=[hbm] * 5,
        out_specs=(vmem(),) * 6,
        scratch_shapes=[pltpu.VMEM(codes.shape, jnp.int32), pltpu.SemaphoreType.DMA((4 + 3 * len(GROUPS),))],
        compiler_params=params(6),
        cost_estimate=cost(2000),
        name="own_early",
    )(codes, in_proj, gain_up, up_kernel, out_kernel)
    own_early, act, w, tap, proj, gain = in_space(pltpu.VMEM, own_early, act, w, tap, proj, gain)

    near, proj = lax.optimization_barrier((near, proj))
    far = lax.ppermute(near, "section", swap)
    near, far = in_space(pltpu.VMEM, near, far)
    (own_late,) = in_space(
        pltpu.VMEM,
        pl.pallas_call(
            functools.partial(late_kernel, rows * cols),
            out_shape=pltpu.VMEM(own_early.shape, F32),
            in_specs=[vmem()] * 3,
            out_specs=vmem(),
            compiler_params=params(4),
            cost_estimate=cost(1000),
            name="own_late",
        )(act, w, near),
    )
    far, own_late = lax.optimization_barrier((far, own_late))

    early, halo = pl.pallas_call(
        early_hidden_kernel,
        out_shape=(hidden_shape, pltpu.VMEM((2 * frames * cols, width), BF16)),
        in_specs=[vmem()] * 6,
        out_specs=(vmem(),) * 2,
        scratch_shapes=[pltpu.VMEM((4 * cols, 9 * share), F32)],
        compiler_params=params(6),
        cost_estimate=cost(1000),
        name="hidden_early",
    )(near, far, proj, gain, w, own_early)
    early, halo = in_space(pltpu.VMEM, early, halo)
    early_other = lax.ppermute(early, "section", swap)

    (late,) = in_space(
        pltpu.VMEM,
        pl.pallas_call(
            functools.partial(late_hidden_kernel, rows, cols),
            out_shape=hidden_shape,
            in_specs=[vmem()] * 3,
            out_specs=vmem(),
            scratch_shapes=[pltpu.VMEM((4 * cols, 9 * share), F32)],
            compiler_params=params(6),
            cost_estimate=cost(1000),
            name="hidden_late",
        )(halo, w, own_late),
    )
    late_other = lax.ppermute(late, "section", swap)

    work = [pltpu.VMEM((2 * pairs, size, 2 * ch), BF16), pltpu.VMEM((height, 2 * size, 2 * ow), F32)]
    out_early, held = pl.pallas_call(
        functools.partial(early_out_kernel, cols),
        out_shape=(pltpu.VMEM((2, height, 2 * cols, ow), BF16), pltpu.VMEM((height, size, 4 * ow), F32)),
        in_specs=[vmem()] * 4,
        out_specs=(vmem(),) * 2,
        scratch_shapes=work,
        compiler_params=params(8),
        cost_estimate=cost(2000),
        name="out_early",
    )(early, *in_space(pltpu.VMEM, early_other), gain_res, tap)
    out_early, held = in_space(pltpu.VMEM, out_early, held)

    return pl.pallas_call(
        functools.partial(late_out_kernel, cols),
        out_shape=jax.ShapeDtypeStruct((frames, height, 2 * cols, ow), BF16),
        in_specs=[vmem()] * 6,
        out_specs=hbm,
        scratch_shapes=[pltpu.VMEM((2, height, 2 * cols, ow), BF16)] + work + [pltpu.SemaphoreType.DMA((2,))],
        compiler_params=params(8),
        cost_estimate=cost(1000),
        name="out_late",
    )(late, *in_space(pltpu.VMEM, late_other), gain_res, tap, out_early, held)


def solution(mesh):
    in_specs = (
        P("clip", "rows", None),
        P(),
        P(),
        P(None, None, "section"),
        P(),
        P(None, "section", None),
    )
    out_specs = P("clip", "rows", None, "section")
    return jax.shard_map(body, mesh=mesh, in_specs=in_specs, out_specs=out_specs, check_vma=False)
```

```python
import functools

import jax
import jax.numpy as jnp
from jax import lax
from jax.experimental import pallas as pl
from jax.experimental.pallas import tpu as pltpu
from jax.sharding import PartitionSpec as P

BITS = 18
EPS = 1e-06
F32 = jnp.float32
BF16 = jnp.bfloat16
MIB = 1024 * 1024
GROUPS = ((0, 2), (2, 2), (4, 2), (6, 2), (8, 1))


def silu(v):
    return 0.5 * v * (1.0 + jnp.tanh(0.5 * v))


def latent_rows(rows, in_proj, gain):
    cols = rows[0].shape[1]
    count = len(rows)
    wide = jnp.concatenate([jnp.broadcast_to(row, (cols, cols)) for row in rows], axis=0)
    sub = lax.broadcasted_iota(jnp.int32, (count, cols, cols), 1).reshape(count * cols, cols)
    lane = lax.broadcasted_iota(jnp.int32, (count * cols, cols), 1)
    picked = jnp.where(sub == lane, wide, 0).astype(F32)
    column = jnp.sum(picked, axis=1, keepdims=True).astype(jnp.int32)
    spread = jnp.broadcast_to(column, (count * cols, BITS))
    shift = lax.broadcasted_iota(jnp.int32, (count * cols, BITS), 1)
    bits = ((jnp.right_shift(spread, shift) & 1) * 2 - 1).astype(F32).astype(BF16)
    latent = jnp.dot(bits, in_proj, preferred_element_type=F32)
    mean = jnp.mean(latent * latent, axis=1, keepdims=True)
    return silu(latent * lax.rsqrt(mean + EPS) * gain)


def shifted(x, cols, amount):
    rows, lanes = x.shape
    place = lax.broadcasted_iota(jnp.int32, (rows // cols, cols, lanes), 1).reshape(rows, lanes)
    moved = pltpu.roll(x, amount % rows, 0)
    return jnp.where(place == (0 if amount == 1 else cols - 1), 0.0, moved)


def weights(w_refs, a, group):
    ref, first = (w_refs[0], 0) if a == 0 else (w_refs[1], 9 * (a - 1))
    return jnp.concatenate([ref[first + group[0] + k] for k in range(group[1])], axis=1)


def early_products(act, n, w_refs, acc_ref, group):
    share = w_refs[1].shape[2]
    lanes = pl.ds(group[0] * share, group[1] * share)
    if group[1] == 1:
        both = jnp.concatenate([weights(w_refs, 2, group), weights(w_refs, 1, group)], axis=1)
        now = jnp.dot(act[pl.ds(0, 2 * n), :], both, preferred_element_type=F32)
        now, back = now[:, :share], now[:n, share:]
    else:
        now = jnp.dot(act[pl.ds(0, 2 * n), :], weights(w_refs, 2, group), preferred_element_type=F32)
        back = jnp.dot(act[pl.ds(0, n), :], weights(w_refs, 1, group), preferred_element_type=F32)
    acc_ref[pl.ds(0, n), lanes] = now[:n]
    acc_ref[pl.ds(n, n), lanes] = now[n:] + back


def late_products(act, n, w_refs, acc_ref, group):
    share = w_refs[1].shape[2]
    lanes = pl.ds(group[0] * share, group[1] * share)
    left = jnp.concatenate([act[pl.ds(a * n, 2 * n), :] for a in range(3)], axis=1)
    right = jnp.concatenate([weights(w_refs, a, group) for a in range(3)], axis=0)
    acc_ref[:, lanes] = jnp.dot(left, right, preferred_element_type=F32)


def own_kernel(codes_hbm, proj_hbm, gain_hbm, up_hbm, acc_ref, act_ref, w_ref, proj_ref, gain_ref, codes_ref, sems):
    pairs = [(codes_hbm, codes_ref), (proj_hbm, proj_ref), (gain_hbm, gain_ref)]
    for first, count in GROUPS:
        for a in (1, 2):
            pairs.append((up_hbm.at[pl.ds(9 * a + first, count)], w_ref.at[pl.ds(9 * (a - 1) + first, count)]))
    copies = [pltpu.make_async_copy(src, dst, sems.at[n]) for n, (src, dst) in enumerate(pairs)]
    for copy in copies:
        copy.start()
    for copy in copies[:3]:
        copy.wait()
    frames, rows, cols = codes_ref.shape
    codes = [codes_ref[t, r : r + 1, :] for t in range(frames) for r in range(rows)]
    act_ref[...] = latent_rows(codes, proj_ref[...], gain_ref[...]).astype(BF16)
    for g, group in enumerate(GROUPS):
        for copy in copies[3 + 2 * g : 5 + 2 * g]:
            copy.wait()
        early_products(act_ref, rows * cols, (None, w_ref), acc_ref, group)


def late_kernel(n, act_ref, w_ref, up_hbm, after_ref, acc_ref, first_ref, sems):
    copies = []
    for g, (first, count) in enumerate(GROUPS):
        part = pl.ds(first, count)
        copies.append(pltpu.make_async_copy(up_hbm.at[part], first_ref.at[part], sems.at[g]))
    for copy in copies:
        copy.start()
    for copy, group in zip(copies, GROUPS):
        copy.wait()
        late_products(act_ref, n, (first_ref, w_ref), acc_ref, group)


def combine(rows, cols, share, own_ref, halo_ref, h_ref):
    def taken(slot, tap):
        if slot in (0, rows + 1):
            ref, span, row = halo_ref, 2 * cols, 0 if slot == 0 else 1
        else:
            ref, span, row = own_ref, rows * cols, slot - 1
        lanes = pl.ds(tap * share, share)
        return jnp.concatenate([ref[pl.ds(t * span + row * cols, cols), lanes] for t in range(2)], axis=0)

    for q in range(rows + 1):
        sums = [[], []]
        for c in range(3):
            x = taken(q, c) + taken(q + 1, 6 + c)
            sums[0].append(x + taken(q, 3 + c))
            sums[1].append(x + taken(q + 1, 3 + c))
        out = pl.ds(q * 2 * cols, 2 * cols)
        for py, (left, mid, right) in enumerate(sums):
            even = shifted(left, cols, 1) + (mid + right)
            odd = (left + mid) + shifted(right, cols, -1)
            h_ref[out, pl.ds(2 * py * share, share)] = even.astype(BF16)
            h_ref[out, pl.ds((2 * py + 1) * share, share)] = odd.astype(BF16)


def early_hidden_kernel(near_ref, far_ref, proj_ref, gain_ref, w_ref, own_ref, h_ref, act_ref, halo_ref):
    frames, rows, cols = near_ref.shape
    first = lax.axis_index("section") == 0
    place = lax.axis_index("rows")
    last = lax.axis_size("rows") - 1
    codes = []
    for t in range(frames):
        low = [ref[t, rows - 1 : rows, :] for ref in (near_ref, far_ref)]
        high = [ref[t, 0:1, :] for ref in (near_ref, far_ref)]
        codes += [jnp.where(first, low[0], low[1]), jnp.where(first, high[1], high[0])]
    act = latent_rows(codes, proj_ref[...], gain_ref[...])
    edge = lax.broadcasted_iota(jnp.int32, (frames, 2, cols, act.shape[1]), 1).reshape(act.shape)
    keep = jnp.where(edge == 0, (place > 0).astype(F32), (place < last).astype(F32))
    act_ref[...] = (act * keep).astype(BF16)
    for group in GROUPS:
        early_products(act_ref, 2 * cols, (None, w_ref), halo_ref, group)
    combine(rows, cols, w_ref.shape[2], own_ref, halo_ref, h_ref)


def late_hidden_kernel(rows, cols, act_ref, first_ref, w_ref, own_ref, h_ref, halo_ref):
    for group in GROUPS:
        late_products(act_ref, 2 * cols, (first_ref, w_ref), halo_ref, group)
    combine(rows, cols, w_ref.shape[2], own_ref, halo_ref, h_ref)


def normalise(size, own_ref, other_ref, gain_ref, norm_ref):
    pairs = own_ref.shape[0] // size
    part = own_ref.shape[1] // 4
    section = lax.axis_index("section")
    starts = [pl.multiple_of(k * part, part) for k in (section, 1 - section)]
    gains = [gain_ref[:, pl.ds(start, part)] for start in starts]
    place = lax.axis_index("rows")
    last = lax.axis_size("rows") - 1
    for q in range(pairs):
        for py in range(2):
            for px in range(2):
                lanes = pl.ds((2 * py + px) * part, part)
                x = [ref[pl.ds(q * size, size), lanes].astype(F32) for ref in (own_ref, other_ref)]
                mean = jnp.sum(x[0] * x[0] + x[1] * x[1], axis=1, keepdims=True) / (2 * part)
                scale = lax.rsqrt(mean + EPS)
                if q == 0 and py == 0:
                    scale = jnp.where(place > 0, scale, 0.0)
                if q == pairs - 1 and py == 1:
                    scale = jnp.where(place < last, scale, 0.0)
                for s in range(2):
                    value = silu(x[s] * scale * gains[s])
                    norm_ref[2 * q + py, :, pl.ds(starts[s] + 2 * px * part, part)] = value.astype(BF16)


def out_products(norm_ref, tap_ref, a, m):
    height = norm_ref.shape[0] - 2
    depth = norm_ref.shape[2]
    left = [norm_ref[pl.ds(b, height), pl.ds(0, m), :].reshape(height * m, depth) for b in range(3)]
    lines = [[], [], [], []]
    for b in range(3):
        w = [tap_ref[9 * a + 3 * b + c] for c in range(3)]
        zero = jnp.zeros_like(w[0])
        for line, cells in zip(lines, ((w[1], w[2]), (w[0], w[1]), (zero, w[0]), (w[2], zero))):
            line += cells
    right = jnp.concatenate([jnp.concatenate(line, axis=1) for line in lines], axis=0)
    total = lax.dot_general(
        jnp.concatenate(left, axis=1), right, (((1,), (1,)), ((), ())), preferred_element_type=F32
    )
    return total.reshape(height, m, right.shape[0])


def finish(y, full, cols, o_ref, mix_ref):
    rows = full.shape[0]
    ow = o_ref.shape[3]
    side = full[:, 2 * ow :]
    lane = lax.broadcasted_iota(jnp.int32, side.shape, 1)
    both = full[:, : 2 * ow] + jnp.where(lane < ow, shifted(side, cols, 1), shifted(side, cols, -1))
    mix_ref[y, pl.ds(0, rows, stride=2), :] = both
    mix_ref[y, pl.ds(1, rows, stride=2), :] = pltpu.roll(both, ow, 1)
    result = mix_ref[y][:, :ow].astype(BF16)
    for t in range(2):
        o_ref[t, y] = result[rows * t : rows * (t + 1)]


def early_out_kernel(cols, own_ref, other_ref, gain_ref, tap_ref, o_ref, acc_ref, norm_ref, mix_ref):
    size = 2 * cols
    normalise(size, own_ref, other_ref, gain_ref, norm_ref)
    now = out_products(norm_ref, tap_ref, 2, size)
    back = out_products(norm_ref, tap_ref, 1, size)
    acc_ref[...] = out_products(norm_ref, tap_ref, 0, size)
    acc_ref[:, pl.ds(0, cols), :] += back[:, cols:]
    for y in range(now.shape[0]):
        full = jnp.concatenate([now[y, :cols], now[y, cols:] + back[y, :cols]], axis=0)
        finish(y, full, cols, o_ref, mix_ref)


def late_out_kernel(cols, own_ref, other_ref, gain_ref, tap_ref, early_ref, acc_ref, o_hbm, o_ref, norm_ref, mix_ref, sems):
    size = 2 * cols
    first = pltpu.make_async_copy(early_ref, o_hbm.at[pl.ds(0, 2)], sems.at[0])
    first.start()
    normalise(size, own_ref, other_ref, gain_ref, norm_ref)
    now = out_products(norm_ref, tap_ref, 2, size)
    back = out_products(norm_ref, tap_ref, 1, -(-cols // 16) * 16)
    for y in range(now.shape[0]):
        held = acc_ref[y]
        full = jnp.concatenate([held[:cols] + now[y, :cols], held[cols:] + now[y, cols:] + back[y, :cols]], axis=0)
        finish(y, full, cols, o_ref, mix_ref)
    second = pltpu.make_async_copy(o_ref, o_hbm.at[pl.ds(2, 2)], sems.at[1])
    second.start()
    first.wait()
    second.wait()


def params(mib):
    return pltpu.CompilerParams(vmem_limit_bytes=mib * MIB)


def cost(mflops):
    return pl.CostEstimate(flops=mflops * 10**6, bytes_accessed=10**7, transcendentals=0)


def vmem():
    return pl.BlockSpec(memory_space=pltpu.VMEM)


def in_space(space, *arrays):
    return tuple(pltpu.with_memory_space_constraint(x, space) for x in arrays)


def body(codes, in_proj, gain_up, up_kernel, gain_res, out_kernel):
    frames, rows, cols = codes.shape
    size = 2 * cols
    width, share = up_kernel.shape[1:]
    ow, ch = out_kernel.shape[1:]
    pairs = rows + 1
    height = 2 * rows
    count = lax.axis_size("rows")
    joint = [(2 * i, 2 * i + 2) for i in range(count - 1)] + [(2 * i + 3, 2 * i + 1) for i in range(count - 1)]
    swap = [(0, 1), (1, 0)]
    near = lax.ppermute(codes, ("rows", "section"), joint)
    gain_res = gain_res.reshape(1, -1)
    up_kernel, codes, in_proj, gain_up = in_space(pltpu.HBM, up_kernel, codes, in_proj, gain_up.reshape(1, -1))
    (tap,) = in_space(pltpu.VMEM, out_kernel)
    hbm = pl.BlockSpec(memory_space=pltpu.HBM)
    hidden_shape = pltpu.VMEM((pairs * size, 4 * share), BF16)

    own_early, act, w, proj, gain = pl.pallas_call(
        own_kernel,
        out_shape=(
            pltpu.VMEM((2 * rows * cols, 9 * share), F32),
            pltpu.VMEM((frames * rows * cols, width), BF16),
            pltpu.VMEM((18, width, share), BF16),
            pltpu.VMEM(in_proj.shape, BF16),
            pltpu.VMEM(gain_up.shape, F32),
        ),
        in_specs=[hbm] * 4,
        out_specs=(vmem(),) * 5,
        scratch_shapes=[pltpu.VMEM(codes.shape, jnp.int32), pltpu.SemaphoreType.DMA((3 + 2 * len(GROUPS),))],
        compiler_params=params(6),
        cost_estimate=cost(2000),
        name="own_early",
    )(codes, in_proj, gain_up, up_kernel)
    own_early, act, w, proj, gain = in_space(pltpu.VMEM, own_early, act, w, proj, gain)

    near, proj = lax.optimization_barrier((near, proj))
    far = lax.ppermute(near, "section", swap)
    near, far = in_space(pltpu.VMEM, near, far)
    own_late, w_first = in_space(
        pltpu.VMEM,
        *pl.pallas_call(
            functools.partial(late_kernel, rows * cols),
            out_shape=(pltpu.VMEM(own_early.shape, F32), pltpu.VMEM((9, width, share), BF16)),
            in_specs=[vmem(), vmem(), hbm, vmem()],
            out_specs=(vmem(),) * 2,
            scratch_shapes=[pltpu.SemaphoreType.DMA((len(GROUPS),))],
            compiler_params=params(4),
            cost_estimate=cost(1000),
            name="own_late",
        )(act, w, up_kernel, near),
    )
    far, own_late = lax.optimization_barrier((far, own_late))

    early, halo = pl.pallas_call(
        early_hidden_kernel,
        out_shape=(hidden_shape, pltpu.VMEM((2 * frames * cols, width), BF16)),
        in_specs=[vmem()] * 6,
        out_specs=(vmem(),) * 2,
        scratch_shapes=[pltpu.VMEM((4 * cols, 9 * share), F32)],
        compiler_params=params(6),
        cost_estimate=cost(1000),
        name="hidden_early",
    )(near, far, proj, gain, w, own_early)
    early, halo = in_space(pltpu.VMEM, early, halo)
    early_other = lax.ppermute(early, "section", swap)

    (late,) = in_space(
        pltpu.VMEM,
        pl.pallas_call(
            functools.partial(late_hidden_kernel, rows, cols),
            out_shape=hidden_shape,
            in_specs=[vmem()] * 4,
            out_specs=vmem(),
            scratch_shapes=[pltpu.VMEM((4 * cols, 9 * share), F32)],
            compiler_params=params(6),
            cost_estimate=cost(1000),
            name="hidden_late",
        )(halo, w_first, w, own_late),
    )
    late_other = lax.ppermute(late, "section", swap)

    work = [pltpu.VMEM((2 * pairs, size, 2 * ch), BF16), pltpu.VMEM((height, 2 * size, 2 * ow), F32)]
    out_early, held = pl.pallas_call(
        functools.partial(early_out_kernel, cols),
        out_shape=(pltpu.VMEM((2, height, 2 * cols, ow), BF16), pltpu.VMEM((height, size, 4 * ow), F32)),
        in_specs=[vmem()] * 4,
        out_specs=(vmem(),) * 2,
        scratch_shapes=work,
        compiler_params=params(8),
        cost_estimate=cost(2000),
        name="out_early",
    )(early, *in_space(pltpu.VMEM, early_other), gain_res, tap)
    out_early, held = in_space(pltpu.VMEM, out_early, held)

    return pl.pallas_call(
        functools.partial(late_out_kernel, cols),
        out_shape=jax.ShapeDtypeStruct((frames, height, 2 * cols, ow), BF16),
        in_specs=[vmem()] * 6,
        out_specs=hbm,
        scratch_shapes=[pltpu.VMEM((2, height, 2 * cols, ow), BF16)] + work + [pltpu.SemaphoreType.DMA((2,))],
        compiler_params=params(8),
        cost_estimate=cost(1000),
        name="out_late",
    )(late, *in_space(pltpu.VMEM, late_other), gain_res, tap, out_early, held)


def solution(mesh):
    in_specs = (
        P("clip", "rows", None),
        P(),
        P(),
        P(None, None, "section"),
        P(),
        P(None, "section", None),
    )
    out_specs = P("clip", "rows", None, "section")
    return jax.shard_map(body, mesh=mesh, in_specs=in_specs, out_specs=out_specs, check_vma=False)
```

```python
import functools

import jax
import jax.numpy as jnp
from jax import lax
from jax.experimental import pallas as pl
from jax.experimental.pallas import tpu as pltpu
from jax.sharding import PartitionSpec as P

BITS = 18
EPS = 1e-06
F32 = jnp.float32
BF16 = jnp.bfloat16
MIB = 1024 * 1024
GROUPS = ((0, 2), (2, 2), (4, 2), (6, 2), (8, 1))
SPLIT = 1


def silu_of_half(h):
    return h + h * jnp.tanh(h)


def latent_rows(rows, in_proj, gain):
    cols = rows[0].shape[1]
    count = len(rows)
    wide = jnp.concatenate([jnp.broadcast_to(row, (cols, cols)) for row in rows], axis=0)
    sub = lax.broadcasted_iota(jnp.int32, (count, cols, cols), 1).reshape(count * cols, cols)
    lane = lax.broadcasted_iota(jnp.int32, (count * cols, cols), 1)
    picked = jnp.where(sub == lane, wide, 0).astype(F32)
    column = jnp.sum(picked, axis=1, keepdims=True).astype(jnp.int32)
    spread = jnp.broadcast_to(column, (count * cols, BITS))
    shift = lax.broadcasted_iota(jnp.int32, (count * cols, BITS), 1)
    bits = ((jnp.right_shift(spread, shift) & 1) * 2 - 1).astype(F32).astype(BF16)
    latent = jnp.dot(bits, in_proj, preferred_element_type=F32)
    mean = jnp.mean(latent * latent, axis=1, keepdims=True)
    return silu_of_half(latent * lax.rsqrt(mean + EPS) * (0.5 * gain))


def shifted(x, cols, amount):
    rows, lanes = x.shape
    place = lax.broadcasted_iota(jnp.int32, (rows // cols, cols, lanes), 1).reshape(rows, lanes)
    moved = pltpu.roll(x, amount % rows, 0)
    return jnp.where(place == (0 if amount == 1 else cols - 1), 0.0, moved)


def weights(w_ref, a, group):
    return jnp.concatenate([w_ref[9 * a + group[0] + k] for k in range(group[1])], axis=1)


def early_products(act, n, w_ref, group):
    share = w_ref.shape[2]
    if group[1] == 1:
        both = jnp.concatenate([weights(w_ref, 2, group), weights(w_ref, 1, group)], axis=1)
        now = jnp.dot(act[: 2 * n], both, preferred_element_type=F32)
        now, back = now[:, :share], now[:n, share:]
    else:
        now = jnp.dot(act[: 2 * n], weights(w_ref, 2, group), preferred_element_type=F32)
        back = jnp.dot(act[:n], weights(w_ref, 1, group), preferred_element_type=F32)
    return jnp.concatenate([now[:n], now[n:] + back], axis=0)


def late_products(act, n, w_ref, group):
    left = jnp.concatenate([act[a * n : (a + 2) * n] for a in range(3)], axis=1)
    right = jnp.concatenate([weights(w_ref, a, group) for a in range(3)], axis=0)
    return jnp.dot(left, right, preferred_element_type=F32)


def load_kernel(codes_hbm, proj_hbm, gain_hbm, up_hbm, act_ref, w_ref, proj_ref, gain_ref, codes_ref, sems):
    pairs = ((codes_hbm, codes_ref), (proj_hbm, proj_ref), (gain_hbm, gain_ref), (up_hbm, w_ref))
    copies = [pltpu.make_async_copy(src, dst, sems.at[n]) for n, (src, dst) in enumerate(pairs)]
    for copy in copies:
        copy.start()
    for copy in copies[:3]:
        copy.wait()
    frames, rows, cols = codes_ref.shape
    codes = [codes_ref[t, r : r + 1, :] for t in range(frames) for r in range(rows)]
    act_ref[...] = latent_rows(codes, proj_ref[...], gain_ref[...]).astype(BF16)
    copies[3].wait()


def lanes_of(group, share, start=0):
    return pl.ds((group[0] - start) * share, group[1] * share)


def own_early_kernel(n, act_ref, w_ref, early_ref, late_ref):
    share = w_ref.shape[2]
    act = act_ref[...]
    for group in GROUPS:
        early_ref[:, lanes_of(group, share)] = early_products(act, n, w_ref, group)
    for group in GROUPS[:SPLIT]:
        late_ref[:, lanes_of(group, share)] = late_products(act, n, w_ref, group)


def own_late_kernel(n, act_ref, w_ref, after_ref, late_ref):
    share = w_ref.shape[2]
    act = act_ref[...]
    for group in GROUPS[SPLIT:]:
        late_ref[:, lanes_of(group, share, GROUPS[SPLIT][0])] = late_products(act, n, w_ref, group)


def combine(rows, cols, share, own, halo, h_ref):
    def taken(slot, tap):
        if slot in (0, rows + 1):
            row = 0 if slot == 0 else 1
            part = halo[:, tap * share : (tap + 1) * share]
            pieces = [part[(2 * t + row) * cols : (2 * t + row + 1) * cols] for t in range(2)]
        else:
            pieces = [own(tap, (t * rows + slot - 1) * cols) for t in range(2)]
        return jnp.concatenate(pieces, axis=0)

    for q in range(rows + 1):
        sums = [[], []]
        for c in range(3):
            x = taken(q, c) + taken(q + 1, 6 + c)
            sums[0].append(x + taken(q, 3 + c))
            sums[1].append(x + taken(q + 1, 3 + c))
        out = pl.ds(q * 2 * cols, 2 * cols)
        for py, (left, mid, right) in enumerate(sums):
            even = shifted(left, cols, 1) + (mid + right)
            odd = (left + mid) + shifted(right, cols, -1)
            h_ref[out, pl.ds(2 * py * share, share)] = even.astype(BF16)
            h_ref[out, pl.ds((2 * py + 1) * share, share)] = odd.astype(BF16)


def early_hidden_kernel(near_ref, far_ref, proj_ref, gain_ref, w_ref, own_ref, h_ref, act_ref):
    frames, rows, cols = near_ref.shape
    share = w_ref.shape[2]
    first = lax.axis_index("section") == 0
    place = lax.axis_index("rows")
    last = lax.axis_size("rows") - 1
    codes = []
    for t in range(frames):
        low = [ref[t, rows - 1 : rows, :] for ref in (near_ref, far_ref)]
        high = [ref[t, 0:1, :] for ref in (near_ref, far_ref)]
        codes += [jnp.where(first, low[0], low[1]), jnp.where(first, high[1], high[0])]
    act = latent_rows(codes, proj_ref[...], gain_ref[...])
    edge = lax.broadcasted_iota(jnp.int32, (frames, 2, cols, act.shape[1]), 1).reshape(act.shape)
    keep = jnp.where(edge == 0, (place > 0).astype(F32), (place < last).astype(F32))
    act = (act * keep).astype(BF16)
    act_ref[...] = act
    halo = jnp.concatenate([early_products(act, 2 * cols, w_ref, group) for group in GROUPS], axis=1)

    def own(tap, start):
        return own_ref[pl.ds(start, cols), pl.ds(tap * share, share)]

    combine(rows, cols, share, own, halo, h_ref)


def late_hidden_kernel(rows, cols, act_ref, w_ref, first_ref, rest_ref, h_ref):
    share = w_ref.shape[2]
    act = act_ref[...]
    halo = jnp.concatenate([late_products(act, 2 * cols, w_ref, group) for group in GROUPS], axis=1)
    cut = GROUPS[SPLIT][0]

    def own(tap, start):
        ref, k = (first_ref, tap) if tap < cut else (rest_ref, tap - cut)
        return ref[pl.ds(start, cols), pl.ds(k * share, share)]

    combine(rows, cols, share, own, halo, h_ref)


def part_starts(part):
    section = lax.axis_index("section")
    return [pl.multiple_of(k * part, part) for k in (section, 1 - section)]


def normalise(size, own_ref, other_ref, gain_ref):
    pairs = own_ref.shape[0] // size
    part = own_ref.shape[1] // 4
    gains = [0.5 * gain_ref[:, pl.ds(start, part)] for start in part_starts(part)]
    place = lax.axis_index("rows")
    last = lax.axis_size("rows") - 1
    rows = []
    for q in range(pairs):
        for py in range(2):
            cells = []
            for px in range(2):
                lanes = pl.ds((2 * py + px) * part, part)
                x = [ref[pl.ds(q * size, size), lanes].astype(F32) for ref in (own_ref, other_ref)]
                mean = jnp.sum(x[0] * x[0] + x[1] * x[1], axis=1, keepdims=True) / (2 * part)
                scale = lax.rsqrt(mean + EPS)
                if q == 0 and py == 0:
                    scale = jnp.where(place > 0, scale, 0.0)
                if q == pairs - 1 and py == 1:
                    scale = jnp.where(place < last, scale, 0.0)
                cells += [silu_of_half(x[s] * scale * gains[s]).astype(BF16) for s in range(2)]
            rows.append(jnp.concatenate(cells, axis=1))
    return rows


def out_products(rows, tap_ref, a, m):
    height = len(rows) - 2
    left = jnp.concatenate(
        [jnp.concatenate([rows[y + b][:m] for b in range(3)], axis=1) for y in range(height)], axis=0
    )
    part = tap_ref.shape[2] // 2
    starts = part_starts(part)
    lines = [[], [], [], []]
    for b in range(3):
        w = [
            jnp.concatenate([tap_ref[9 * a + 3 * b + c, :, pl.ds(start, part)] for start in starts], axis=1)
            for c in range(3)
        ]
        zero = jnp.zeros_like(w[0])
        for line, cells in zip(lines, ((w[1], w[2]), (w[0], w[1]), (zero, w[0]), (w[2], zero))):
            line += cells
    right = jnp.concatenate([jnp.concatenate(line, axis=1) for line in lines], axis=0)
    total = lax.dot_general(left, right, (((1,), (1,)), ((), ())), preferred_element_type=F32)
    return total.reshape(height, m, right.shape[0])


def mix(y, full, cols, ow, mix_ref):
    rows = full.shape[0]
    side = full[:, 2 * ow :]
    lane = lax.broadcasted_iota(jnp.int32, side.shape, 1)
    both = full[:, : 2 * ow] + jnp.where(lane < ow, shifted(side, cols, 1), shifted(side, cols, -1))
    mix_ref[y, pl.ds(0, rows, stride=2), :] = both
    mix_ref[y, pl.ds(1, rows, stride=2), :] = pltpu.roll(both, ow, 1)


def place_row(y, o_ref, mix_ref):
    rows, ow = o_ref.shape[2:]
    result = mix_ref[y][:, :ow].astype(BF16)
    for t in range(2):
        o_ref[t, y] = result[rows * t : rows * (t + 1)]


def early_out_kernel(cols, own_ref, other_ref, gain_ref, tap_ref, o_ref, acc_ref, mix_ref):
    size = 2 * cols
    rows = normalise(size, own_ref, other_ref, gain_ref)
    now, back, held = [out_products(rows, tap_ref, a, size) for a in (2, 1, 0)]
    height = now.shape[0]
    for y in range(height):
        full = jnp.concatenate([now[y, :cols], now[y, cols:] + back[y, :cols]], axis=0)
        mix(y, full, cols, o_ref.shape[3], mix_ref)
        acc_ref[y] = jnp.concatenate([held[y, :cols] + back[y, cols:], held[y, cols:]], axis=0)
    for y in range(height):
        place_row(y, o_ref, mix_ref)


def late_out_kernel(cols, own_ref, other_ref, gain_ref, tap_ref, early_ref, acc_ref, o_hbm, o_ref, mix_ref, sems):
    size = 2 * cols
    copies = [pltpu.make_async_copy(early_ref, o_hbm.at[pl.ds(0, 2)], sems.at[0])]
    copies[0].start()
    rows = normalise(size, own_ref, other_ref, gain_ref)
    now = out_products(rows, tap_ref, 2, size)
    back = out_products(rows, tap_ref, 1, -(-cols // 16) * 16)
    height = now.shape[0]
    for y in range(height):
        held = acc_ref[y]
        full = jnp.concatenate([held[:cols] + now[y, :cols], held[cols:] + now[y, cols:] + back[y, :cols]], axis=0)
        mix(y, full, cols, o_ref.shape[3], mix_ref)
    half = height // 2
    for k in range(2):
        for y in range(k * half, (k + 1) * half):
            place_row(y, o_ref, mix_ref)
        part = pl.ds(k * half, half)
        copies.append(
            pltpu.make_async_copy(o_ref.at[:, part], o_hbm.at[pl.ds(2, 2), part], sems.at[1 + k])
        )
        copies[-1].start()
    for copy in copies:
        copy.wait()


def params(mib):
    return pltpu.CompilerParams(vmem_limit_bytes=mib * MIB)


def cost(mflops):
    return pl.CostEstimate(flops=mflops * 10**6, bytes_accessed=10**7, transcendentals=0)


def vmem():
    return pl.BlockSpec(memory_space=pltpu.VMEM)


def in_space(space, *arrays):
    return tuple(pltpu.with_memory_space_constraint(x, space) for x in arrays)


def call(kernel, name, outs, ins, mib, mflops, scratch=(), in_specs=None, out_specs=None):
    results = pl.pallas_call(
        kernel,
        out_shape=outs,
        in_specs=in_specs or [vmem()] * len(ins),
        out_specs=out_specs or (vmem(),) * len(outs),
        scratch_shapes=list(scratch),
        compiler_params=params(mib),
        cost_estimate=cost(mflops),
        name=name,
    )(*ins)
    return results if out_specs else in_space(pltpu.VMEM, *results)


def body(codes, in_proj, gain_up, up_kernel, gain_res, out_kernel):
    frames, rows, cols = codes.shape
    size = 2 * cols
    width, share = up_kernel.shape[1:]
    ow = out_kernel.shape[1]
    pairs = rows + 1
    height = 2 * rows
    count = lax.axis_size("rows")
    joint = [(2 * i, 2 * i + 2) for i in range(count - 1)] + [(2 * i + 3, 2 * i + 1) for i in range(count - 1)]
    swap = [(0, 1), (1, 0)]
    near = lax.ppermute(codes, ("rows", "section"), joint)
    gain_res = gain_res.reshape(1, -1)
    up_kernel, codes, in_proj, gain_up = in_space(pltpu.HBM, up_kernel, codes, in_proj, gain_up.reshape(1, -1))
    (tap,) = in_space(pltpu.VMEM, out_kernel)
    hbm = pl.BlockSpec(memory_space=pltpu.HBM)
    hidden_shape = pltpu.VMEM((pairs * size, 4 * share), BF16)

    act, w, proj, gain = call(
        load_kernel,
        "load",
        (
            pltpu.VMEM((frames * rows * cols, width), BF16),
            pltpu.VMEM(up_kernel.shape, BF16),
            pltpu.VMEM(in_proj.shape, BF16),
            pltpu.VMEM(gain_up.shape, F32),
        ),
        (codes, in_proj, gain_up, up_kernel),
        6,
        2000,
        [pltpu.VMEM(codes.shape, jnp.int32), pltpu.SemaphoreType.DMA((4,))],
        in_specs=[hbm] * 4,
    )
    cut = GROUPS[SPLIT][0]
    own_early, own_first = call(
        functools.partial(own_early_kernel, rows * cols),
        "own_early",
        (pltpu.VMEM((2 * rows * cols, 9 * share), F32), pltpu.VMEM((2 * rows * cols, cut * share), F32)),
        (act, w),
        4,
        1000,
    )

    near, own_early = lax.optimization_barrier((near, own_early))
    far = lax.ppermute(near, "section", swap)
    near, far = in_space(pltpu.VMEM, near, far)
    (own_rest,) = call(
        functools.partial(own_late_kernel, rows * cols),
        "own_late",
        (pltpu.VMEM((2 * rows * cols, (9 - cut) * share), F32),),
        (act, w, near),
        4,
        1000,
    )
    far, own_rest = lax.optimization_barrier((far, own_rest))

    early, halo = call(
        early_hidden_kernel,
        "hidden_early",
        (hidden_shape, pltpu.VMEM((2 * frames * cols, width), BF16)),
        (near, far, proj, gain, w, own_early),
        8,
        1000,
    )
    early_other = lax.ppermute(early, "section", swap)
    (late,) = call(
        functools.partial(late_hidden_kernel, rows, cols),
        "hidden_late",
        (hidden_shape,),
        (halo, w, own_first, own_rest),
        8,
        1000,
    )
    late_other = lax.ppermute(late, "section", swap)
    early_other, late_other = in_space(pltpu.VMEM, early_other, late_other)

    mixed = pltpu.VMEM((height, 2 * size, 2 * ow), F32)
    out_early, held = call(
        functools.partial(early_out_kernel, cols),
        "out_early",
        (pltpu.VMEM((2, height, 2 * cols, ow), BF16), pltpu.VMEM((height, size, 4 * ow), F32)),
        (early, early_other, gain_res, tap),
        12,
        2000,
        [mixed],
    )
    return call(
        functools.partial(late_out_kernel, cols),
        "out_late",
        jax.ShapeDtypeStruct((frames, height, 2 * cols, ow), BF16),
        (late, late_other, gain_res, tap, out_early, held),
        12,
        1000,
        [pltpu.VMEM((2, height, 2 * cols, ow), BF16), mixed, pltpu.SemaphoreType.DMA((3,))],
        out_specs=hbm,
    )


def solution(mesh):
    in_specs = (
        P("clip", "rows", None),
        P(),
        P(),
        P(None, None, "section"),
        P(),
        P(None, "section", None),
    )
    out_specs = P("clip", "rows", None, "section")
    return jax.shard_map(body, mesh=mesh, in_specs=in_specs, out_specs=out_specs, check_vma=False)
```

```python
import functools

import jax
import jax.numpy as jnp
from jax import lax
from jax.experimental import pallas as pl
from jax.experimental.pallas import tpu as pltpu
from jax.sharding import PartitionSpec as P

BITS = 18
EPS = 1e-06
F32 = jnp.float32
BF16 = jnp.bfloat16
MIB = 1024 * 1024
GROUPS = ((0, 2), (2, 2), (4, 2), (6, 2), (8, 1))
SPLIT = 3


def silu_of_half(h):
    return h + h * jnp.tanh(h)


def latent_rows(rows, in_proj, gain):
    cols = rows[0].shape[1]
    count = len(rows)
    wide = jnp.concatenate([jnp.broadcast_to(row, (cols, cols)) for row in rows], axis=0)
    sub = lax.broadcasted_iota(jnp.int32, (count, cols, cols), 1).reshape(count * cols, cols)
    lane = lax.broadcasted_iota(jnp.int32, (count * cols, cols), 1)
    picked = jnp.where(sub == lane, wide, 0).astype(F32)
    column = jnp.sum(picked, axis=1, keepdims=True).astype(jnp.int32)
    spread = jnp.broadcast_to(column, (count * cols, BITS))
    shift = lax.broadcasted_iota(jnp.int32, (count * cols, BITS), 1)
    bits = ((jnp.right_shift(spread, shift) & 1) * 2 - 1).astype(F32).astype(BF16)
    latent = jnp.dot(bits, in_proj, preferred_element_type=F32)
    mean = jnp.mean(latent * latent, axis=1, keepdims=True)
    return silu_of_half(latent * lax.rsqrt(mean + EPS) * (0.5 * gain))


def shifted(x, cols, amount):
    rows, lanes = x.shape
    place = lax.broadcasted_iota(jnp.int32, (rows // cols, cols, lanes), 1).reshape(rows, lanes)
    moved = pltpu.roll(x, amount % rows, 0)
    return jnp.where(place == (0 if amount == 1 else cols - 1), 0.0, moved)


def weights(w_ref, a, group):
    return jnp.concatenate([w_ref[9 * a + group[0] + k] for k in range(group[1])], axis=1)


def early_products(act, n, w_ref, group):
    share = w_ref.shape[2]
    if group[1] == 1:
        both = jnp.concatenate([weights(w_ref, 2, group), weights(w_ref, 1, group)], axis=1)
        now = jnp.dot(act[: 2 * n], both, preferred_element_type=F32)
        now, back = now[:, :share], now[:n, share:]
    else:
        now = jnp.dot(act[: 2 * n], weights(w_ref, 2, group), preferred_element_type=F32)
        back = jnp.dot(act[:n], weights(w_ref, 1, group), preferred_element_type=F32)
    return jnp.concatenate([now[:n], now[n:] + back], axis=0)


def late_products(act, n, w_ref, group):
    left = jnp.concatenate([act[a * n : (a + 2) * n] for a in range(3)], axis=1)
    right = jnp.concatenate([weights(w_ref, a, group) for a in range(3)], axis=0)
    return jnp.dot(left, right, preferred_element_type=F32)


def latent_kernel(codes_hbm, proj_hbm, gain_hbm, act_ref, proj_ref, gain_ref, codes_ref, sems):
    pairs = ((codes_hbm, codes_ref), (proj_hbm, proj_ref), (gain_hbm, gain_ref))
    copies = [pltpu.make_async_copy(src, dst, sems.at[n]) for n, (src, dst) in enumerate(pairs)]
    for copy in copies:
        copy.start()
    for copy in copies:
        copy.wait()
    frames, rows, cols = codes_ref.shape
    codes = [codes_ref[t, r : r + 1, :] for t in range(frames) for r in range(rows)]
    act_ref[...] = latent_rows(codes, proj_ref[...], gain_ref[...]).astype(BF16)


def lanes_of(group, share, start=0):
    return pl.ds((group[0] - start) * share, group[1] * share)


def own_first_kernel(n, act_ref, w_ref, first_ref):
    share = w_ref.shape[2]
    act = act_ref[...]
    for group in GROUPS[:SPLIT]:
        first_ref[:, lanes_of(group, share)] = early_products(act, n, w_ref, group)


def own_rest_kernel(n, act_ref, w_ref, after_ref, rest_ref, late_ref):
    share = w_ref.shape[2]
    act = act_ref[...]
    for group in GROUPS[SPLIT:]:
        rest_ref[:, lanes_of(group, share, GROUPS[SPLIT][0])] = early_products(act, n, w_ref, group)
    for group in GROUPS:
        late_ref[:, lanes_of(group, share)] = late_products(act, n, w_ref, group)


def combine(rows, cols, share, own, halo, h_ref):
    def taken(slot, tap):
        if slot in (0, rows + 1):
            row = 0 if slot == 0 else 1
            part = halo[:, tap * share : (tap + 1) * share]
            pieces = [part[(2 * t + row) * cols : (2 * t + row + 1) * cols] for t in range(2)]
        else:
            pieces = [own(tap, (t * rows + slot - 1) * cols) for t in range(2)]
        return jnp.concatenate(pieces, axis=0)

    for q in range(rows + 1):
        sums = [[], []]
        for c in range(3):
            x = taken(q, c) + taken(q + 1, 6 + c)
            sums[0].append(x + taken(q, 3 + c))
            sums[1].append(x + taken(q + 1, 3 + c))
        out = pl.ds(q * 2 * cols, 2 * cols)
        for py, (left, mid, right) in enumerate(sums):
            even = shifted(left, cols, 1) + (mid + right)
            odd = (left + mid) + shifted(right, cols, -1)
            h_ref[out, pl.ds(2 * py * share, share)] = even.astype(BF16)
            h_ref[out, pl.ds((2 * py + 1) * share, share)] = odd.astype(BF16)


def early_hidden_kernel(near_ref, far_ref, proj_ref, gain_ref, w_ref, first_ref, rest_ref, h_ref, act_ref):
    frames, rows, cols = near_ref.shape
    share = w_ref.shape[2]
    first = lax.axis_index("section") == 0
    place = lax.axis_index("rows")
    last = lax.axis_size("rows") - 1
    codes = []
    for t in range(frames):
        low = [ref[t, rows - 1 : rows, :] for ref in (near_ref, far_ref)]
        high = [ref[t, 0:1, :] for ref in (near_ref, far_ref)]
        codes += [jnp.where(first, low[0], low[1]), jnp.where(first, high[1], high[0])]
    act = latent_rows(codes, proj_ref[...], gain_ref[...])
    edge = lax.broadcasted_iota(jnp.int32, (frames, 2, cols, act.shape[1]), 1).reshape(act.shape)
    keep = jnp.where(edge == 0, (place > 0).astype(F32), (place < last).astype(F32))
    act = (act * keep).astype(BF16)
    act_ref[...] = act
    halo = jnp.concatenate([early_products(act, 2 * cols, w_ref, group) for group in GROUPS], axis=1)

    cut = GROUPS[SPLIT][0]

    def own(tap, start):
        ref, k = (first_ref, tap) if tap < cut else (rest_ref, tap - cut)
        return ref[pl.ds(start, cols), pl.ds(k * share, share)]

    combine(rows, cols, share, own, halo, h_ref)


def late_hidden_kernel(rows, cols, act_ref, w_ref, own_ref, h_ref):
    share = w_ref.shape[2]
    act = act_ref[...]
    halo = jnp.concatenate([late_products(act, 2 * cols, w_ref, group) for group in GROUPS], axis=1)

    def own(tap, start):
        return own_ref[pl.ds(start, cols), pl.ds(tap * share, share)]

    combine(rows, cols, share, own, halo, h_ref)


def part_starts(part):
    section = lax.axis_index("section")
    return [pl.multiple_of(k * part, part) for k in (section, 1 - section)]


def normalise(size, own_ref, other_ref, gain_ref):
    pairs = own_ref.shape[0] // size
    part = own_ref.shape[1] // 4
    gains = [0.5 * gain_ref[:, pl.ds(start, part)] for start in part_starts(part)]
    place = lax.axis_index("rows")
    last = lax.axis_size("rows") - 1
    rows = []
    for q in range(pairs):
        for py in range(2):
            cells = []
            for px in range(2):
                lanes = pl.ds((2 * py + px) * part, part)
                x = [ref[pl.ds(q * size, size), lanes].astype(F32) for ref in (own_ref, other_ref)]
                mean = jnp.sum(x[0] * x[0] + x[1] * x[1], axis=1, keepdims=True) / (2 * part)
                scale = lax.rsqrt(mean + EPS)
                if q == 0 and py == 0:
                    scale = jnp.where(place > 0, scale, 0.0)
                if q == pairs - 1 and py == 1:
                    scale = jnp.where(place < last, scale, 0.0)
                cells += [silu_of_half(x[s] * scale * gains[s]).astype(BF16) for s in range(2)]
            rows.append(jnp.concatenate(cells, axis=1))
    return rows


def out_products(rows, tap_ref, a, m):
    height = len(rows) - 2
    left = jnp.concatenate(
        [jnp.concatenate([rows[y + b][:m] for b in range(3)], axis=1) for y in range(height)], axis=0
    )
    part = tap_ref.shape[2] // 2
    starts = part_starts(part)
    lines = [[], [], [], []]
    for b in range(3):
        w = [
            jnp.concatenate([tap_ref[9 * a + 3 * b + c, :, pl.ds(start, part)] for start in starts], axis=1)
            for c in range(3)
        ]
        zero = jnp.zeros_like(w[0])
        for line, cells in zip(lines, ((w[1], w[2]), (w[0], w[1]), (zero, w[0]), (w[2], zero))):
            line += cells
    right = jnp.concatenate([jnp.concatenate(line, axis=1) for line in lines], axis=0)
    total = lax.dot_general(left, right, (((1,), (1,)), ((), ())), preferred_element_type=F32)
    return total.reshape(height, m, right.shape[0])


def mix(y, full, cols, ow, mix_ref):
    rows = full.shape[0]
    side = full[:, 2 * ow :]
    lane = lax.broadcasted_iota(jnp.int32, side.shape, 1)
    both = full[:, : 2 * ow] + jnp.where(lane < ow, shifted(side, cols, 1), shifted(side, cols, -1))
    mix_ref[y, pl.ds(0, rows, stride=2), :] = both
    mix_ref[y, pl.ds(1, rows, stride=2), :] = pltpu.roll(both, ow, 1)


def place_row(y, o_ref, mix_ref):
    rows, ow = o_ref.shape[2:]
    result = mix_ref[y][:, :ow].astype(BF16)
    for t in range(2):
        o_ref[t, y] = result[rows * t : rows * (t + 1)]


def early_out_kernel(cols, own_ref, other_ref, gain_ref, tap_ref, o_ref, acc_ref, mix_ref):
    size = 2 * cols
    rows = normalise(size, own_ref, other_ref, gain_ref)
    now, back, held = [out_products(rows, tap_ref, a, size) for a in (2, 1, 0)]
    height = now.shape[0]
    for y in range(height):
        full = jnp.concatenate([now[y, :cols], now[y, cols:] + back[y, :cols]], axis=0)
        mix(y, full, cols, o_ref.shape[3], mix_ref)
        acc_ref[y] = jnp.concatenate([held[y, :cols] + back[y, cols:], held[y, cols:]], axis=0)
    for y in range(height):
        place_row(y, o_ref, mix_ref)


def late_out_kernel(cols, own_ref, other_ref, gain_ref, tap_ref, early_ref, acc_ref, o_hbm, o_ref, mix_ref, sems):
    size = 2 * cols
    copies = [pltpu.make_async_copy(early_ref, o_hbm.at[pl.ds(0, 2)], sems.at[0])]
    copies[0].start()
    rows = normalise(size, own_ref, other_ref, gain_ref)
    now = out_products(rows, tap_ref, 2, size)
    back = out_products(rows, tap_ref, 1, -(-cols // 16) * 16)
    height = now.shape[0]
    for y in range(height):
        held = acc_ref[y]
        full = jnp.concatenate([held[:cols] + now[y, :cols], held[cols:] + now[y, cols:] + back[y, :cols]], axis=0)
        mix(y, full, cols, o_ref.shape[3], mix_ref)
    half = height // 2
    for k in range(2):
        for y in range(k * half, (k + 1) * half):
            place_row(y, o_ref, mix_ref)
        part = pl.ds(k * half, half)
        copies.append(
            pltpu.make_async_copy(o_ref.at[:, part], o_hbm.at[pl.ds(2, 2), part], sems.at[1 + k])
        )
        copies[-1].start()
    for copy in copies:
        copy.wait()


def params(mib):
    return pltpu.CompilerParams(vmem_limit_bytes=mib * MIB)


def cost(mflops):
    return pl.CostEstimate(flops=mflops * 10**6, bytes_accessed=10**7, transcendentals=0)


def vmem():
    return pl.BlockSpec(memory_space=pltpu.VMEM)


def in_space(space, *arrays):
    return tuple(pltpu.with_memory_space_constraint(x, space) for x in arrays)


def call(kernel, name, outs, ins, mib, mflops, scratch=(), in_specs=None, out_specs=None):
    results = pl.pallas_call(
        kernel,
        out_shape=outs,
        in_specs=in_specs or [vmem()] * len(ins),
        out_specs=out_specs or (vmem(),) * len(outs),
        scratch_shapes=list(scratch),
        compiler_params=params(mib),
        cost_estimate=cost(mflops),
        name=name,
    )(*ins)
    return results if out_specs else in_space(pltpu.VMEM, *results)


def body(codes, in_proj, gain_up, up_kernel, gain_res, out_kernel):
    frames, rows, cols = codes.shape
    size = 2 * cols
    width, share = up_kernel.shape[1:]
    ow = out_kernel.shape[1]
    pairs = rows + 1
    height = 2 * rows
    count = lax.axis_size("rows")
    joint = [(2 * i, 2 * i + 2) for i in range(count - 1)] + [(2 * i + 3, 2 * i + 1) for i in range(count - 1)]
    swap = [(0, 1), (1, 0)]
    near = lax.ppermute(codes, ("rows", "section"), joint)
    gain_res = gain_res.reshape(1, -1)
    w, tap = in_space(pltpu.VMEM, up_kernel, out_kernel)
    codes, in_proj, gain_up = in_space(pltpu.HBM, codes, in_proj, gain_up.reshape(1, -1))
    hbm = pl.BlockSpec(memory_space=pltpu.HBM)
    hidden_shape = pltpu.VMEM((pairs * size, 4 * share), BF16)

    act, proj, gain = call(
        latent_kernel,
        "latent",
        (
            pltpu.VMEM((frames * rows * cols, width), BF16),
            pltpu.VMEM(in_proj.shape, BF16),
            pltpu.VMEM(gain_up.shape, F32),
        ),
        (codes, in_proj, gain_up),
        4,
        1000,
        [pltpu.VMEM(codes.shape, jnp.int32), pltpu.SemaphoreType.DMA((3,))],
        in_specs=[hbm] * 3,
    )
    cut = GROUPS[SPLIT][0]
    own_rows = 2 * rows * cols
    (own_first,) = call(
        functools.partial(own_first_kernel, rows * cols),
        "own_first",
        (pltpu.VMEM((own_rows, cut * share), F32),),
        (act, w),
        4,
        1000,
    )

    near, own_first = lax.optimization_barrier((near, own_first))
    far = lax.ppermute(near, "section", swap)
    near, far = in_space(pltpu.VMEM, near, far)
    own_rest, own_late = call(
        functools.partial(own_rest_kernel, rows * cols),
        "own_rest",
        (pltpu.VMEM((own_rows, (9 - cut) * share), F32), pltpu.VMEM((own_rows, 9 * share), F32)),
        (act, w, near),
        4,
        1000,
    )
    far, own_rest, own_late = lax.optimization_barrier((far, own_rest, own_late))

    early, halo = call(
        early_hidden_kernel,
        "hidden_early",
        (hidden_shape, pltpu.VMEM((2 * frames * cols, width), BF16)),
        (near, far, proj, gain, w, own_first, own_rest),
        8,
        1000,
    )
    early_other = lax.ppermute(early, "section", swap)
    (late,) = call(
        functools.partial(late_hidden_kernel, rows, cols),
        "hidden_late",
        (hidden_shape,),
        (halo, w, own_late),
        8,
        1000,
    )
    late_other = lax.ppermute(late, "section", swap)
    early_other, late_other = in_space(pltpu.VMEM, early_other, late_other)

    mixed = pltpu.VMEM((height, 2 * size, 2 * ow), F32)
    out_early, held = call(
        functools.partial(early_out_kernel, cols),
        "out_early",
        (pltpu.VMEM((2, height, 2 * cols, ow), BF16), pltpu.VMEM((height, size, 4 * ow), F32)),
        (early, early_other, gain_res, tap),
        12,
        2000,
        [mixed],
    )
    return call(
        functools.partial(late_out_kernel, cols),
        "out_late",
        jax.ShapeDtypeStruct((frames, height, 2 * cols, ow), BF16),
        (late, late_other, gain_res, tap, out_early, held),
        12,
        1000,
        [pltpu.VMEM((2, height, 2 * cols, ow), BF16), mixed, pltpu.SemaphoreType.DMA((3,))],
        out_specs=hbm,
    )


def solution(mesh):
    in_specs = (
        P("clip", "rows", None),
        P(),
        P(),
        P(None, None, "section"),
        P(),
        P(None, "section", None),
    )
    out_specs = P("clip", "rows", None, "section")
    return jax.shard_map(body, mesh=mesh, in_specs=in_specs, out_specs=out_specs, check_vma=False)
```

```python
import functools

import jax
import jax.numpy as jnp
from jax import lax
from jax.experimental import pallas as pl
from jax.experimental.pallas import tpu as pltpu
from jax.sharding import PartitionSpec as P

BITS = 18
EPS = 1e-06
F32 = jnp.float32
BF16 = jnp.bfloat16
MIB = 1024 * 1024
GROUPS = ((0, 2), (2, 2), (4, 2), (6, 2), (8, 1))
SPLIT = 3


def silu_of_half(h):
    return h + h * jnp.tanh(h)


def latent_rows(rows, in_proj, gain):
    cols = rows[0].shape[1]
    count = len(rows)
    wide = jnp.concatenate([jnp.broadcast_to(row, (cols, cols)) for row in rows], axis=0)
    sub = lax.broadcasted_iota(jnp.int32, (count, cols, cols), 1).reshape(count * cols, cols)
    lane = lax.broadcasted_iota(jnp.int32, (count * cols, cols), 1)
    picked = jnp.where(sub == lane, wide, 0).astype(F32)
    column = jnp.sum(picked, axis=1, keepdims=True).astype(jnp.int32)
    spread = jnp.broadcast_to(column, (count * cols, BITS))
    shift = lax.broadcasted_iota(jnp.int32, (count * cols, BITS), 1)
    bits = ((jnp.right_shift(spread, shift) & 1) * 2 - 1).astype(F32).astype(BF16)
    latent = jnp.dot(bits, in_proj, preferred_element_type=F32)
    mean = jnp.mean(latent * latent, axis=1, keepdims=True)
    return silu_of_half(latent * lax.rsqrt(mean + EPS) * (0.5 * gain))


def shifted(x, cols, amount):
    rows, lanes = x.shape
    place = lax.broadcasted_iota(jnp.int32, (rows // cols, cols, lanes), 1).reshape(rows, lanes)
    moved = pltpu.roll(x, amount % rows, 0)
    return jnp.where(place == (0 if amount == 1 else cols - 1), 0.0, moved)


def weights(w_ref, a, group):
    return jnp.concatenate([w_ref[9 * a + group[0] + k] for k in range(group[1])], axis=1)


def early_products(act, n, w_ref, group):
    share = w_ref.shape[2]
    if group[1] == 1:
        both = jnp.concatenate([weights(w_ref, 2, group), weights(w_ref, 1, group)], axis=1)
        now = jnp.dot(act[: 2 * n], both, preferred_element_type=F32)
        now, back = now[:, :share], now[:n, share:]
    else:
        now = jnp.dot(act[: 2 * n], weights(w_ref, 2, group), preferred_element_type=F32)
        back = jnp.dot(act[:n], weights(w_ref, 1, group), preferred_element_type=F32)
    return jnp.concatenate([now[:n], now[n:] + back], axis=0)


def late_products(act, n, w_ref, group):
    left = jnp.concatenate([act[a * n : (a + 2) * n] for a in range(3)], axis=1)
    right = jnp.concatenate([weights(w_ref, a, group) for a in range(3)], axis=0)
    return jnp.dot(left, right, preferred_element_type=F32)


def latent_kernel(codes_hbm, proj_hbm, gain_hbm, act_ref, proj_ref, gain_ref, codes_ref, sems):
    pairs = ((codes_hbm, codes_ref), (proj_hbm, proj_ref), (gain_hbm, gain_ref))
    copies = [pltpu.make_async_copy(src, dst, sems.at[n]) for n, (src, dst) in enumerate(pairs)]
    for copy in copies:
        copy.start()
    for copy in copies:
        copy.wait()
    frames, rows, cols = codes_ref.shape
    codes = [codes_ref[t, r : r + 1, :] for t in range(frames) for r in range(rows)]
    act_ref[...] = latent_rows(codes, proj_ref[...], gain_ref[...]).astype(BF16)


def lanes_of(group, share, start=0):
    return pl.ds((group[0] - start) * share, group[1] * share)


def own_first_kernel(n, act_ref, w_ref, first_ref):
    share = w_ref.shape[2]
    act = act_ref[...]
    for group in GROUPS[:SPLIT]:
        first_ref[:, lanes_of(group, share)] = early_products(act, n, w_ref, group)


def own_rest_kernel(n, act_ref, w_ref, after_ref, rest_ref, late_ref):
    share = w_ref.shape[2]
    act = act_ref[...]
    for group in GROUPS[SPLIT:]:
        rest_ref[:, lanes_of(group, share, GROUPS[SPLIT][0])] = early_products(act, n, w_ref, group)
    for group in GROUPS:
        late_ref[:, lanes_of(group, share)] = late_products(act, n, w_ref, group)


def combine(rows, cols, share, own, halo, h_ref):
    def taken(slot, tap):
        if slot in (0, rows + 1):
            row = 0 if slot == 0 else 1
            part = halo[:, tap * share : (tap + 1) * share]
            pieces = [part[(2 * t + row) * cols : (2 * t + row + 1) * cols] for t in range(2)]
        else:
            pieces = [own(tap, (t * rows + slot - 1) * cols) for t in range(2)]
        return jnp.concatenate(pieces, axis=0)

    for q in range(rows + 1):
        sums = [[], []]
        for c in range(3):
            x = taken(q, c) + taken(q + 1, 6 + c)
            sums[0].append(x + taken(q, 3 + c))
            sums[1].append(x + taken(q + 1, 3 + c))
        out = pl.ds(q * 2 * cols, 2 * cols)
        for py, (left, mid, right) in enumerate(sums):
            even = shifted(left, cols, 1) + (mid + right)
            odd = (left + mid) + shifted(right, cols, -1)
            h_ref[out, pl.ds(2 * py * share, share)] = even.astype(BF16)
            h_ref[out, pl.ds((2 * py + 1) * share, share)] = odd.astype(BF16)


def early_hidden_kernel(near_ref, far_ref, proj_ref, gain_ref, w_ref, first_ref, rest_ref, h_ref, act_ref):
    frames, rows, cols = near_ref.shape
    share = w_ref.shape[2]
    first = lax.axis_index("section") == 0
    place = lax.axis_index("rows")
    last = lax.axis_size("rows") - 1
    codes = []
    for t in range(frames):
        low = [ref[t, rows - 1 : rows, :] for ref in (near_ref, far_ref)]
        high = [ref[t, 0:1, :] for ref in (near_ref, far_ref)]
        codes += [jnp.where(first, low[0], low[1]), jnp.where(first, high[1], high[0])]
    act = latent_rows(codes, proj_ref[...], gain_ref[...])
    edge = lax.broadcasted_iota(jnp.int32, (frames, 2, cols, act.shape[1]), 1).reshape(act.shape)
    keep = jnp.where(edge == 0, (place > 0).astype(F32), (place < last).astype(F32))
    act = (act * keep).astype(BF16)
    act_ref[...] = act
    halo = jnp.concatenate([early_products(act, 2 * cols, w_ref, group) for group in GROUPS], axis=1)

    cut = GROUPS[SPLIT][0]

    def own(tap, start):
        ref, k = (first_ref, tap) if tap < cut else (rest_ref, tap - cut)
        return ref[pl.ds(start, cols), pl.ds(k * share, share)]

    combine(rows, cols, share, own, halo, h_ref)


def late_hidden_kernel(rows, cols, act_ref, w_ref, own_ref, h_ref):
    share = w_ref.shape[2]
    act = act_ref[...]
    halo = jnp.concatenate([late_products(act, 2 * cols, w_ref, group) for group in GROUPS], axis=1)

    def own(tap, start):
        return own_ref[pl.ds(start, cols), pl.ds(tap * share, share)]

    combine(rows, cols, share, own, halo, h_ref)


def part_starts(part):
    section = lax.axis_index("section")
    return [pl.multiple_of(k * part, part) for k in (section, 1 - section)]


def normalise(size, own_ref, other_ref, gain_ref):
    pairs = own_ref.shape[0] // size
    part = own_ref.shape[1] // 4
    gains = [0.5 * gain_ref[:, pl.ds(start, part)] for start in part_starts(part)]
    place = lax.axis_index("rows")
    last = lax.axis_size("rows") - 1
    rows = []
    for q in range(pairs):
        for py in range(2):
            cells = []
            for px in range(2):
                lanes = pl.ds((2 * py + px) * part, part)
                x = [ref[pl.ds(q * size, size), lanes].astype(F32) for ref in (own_ref, other_ref)]
                mean = jnp.sum(x[0] * x[0] + x[1] * x[1], axis=1, keepdims=True) / (2 * part)
                scale = lax.rsqrt(mean + EPS)
                if q == 0 and py == 0:
                    scale = jnp.where(place > 0, scale, 0.0)
                if q == pairs - 1 and py == 1:
                    scale = jnp.where(place < last, scale, 0.0)
                cells += [silu_of_half(x[s] * scale * gains[s]).astype(BF16) for s in range(2)]
            rows.append(jnp.concatenate(cells, axis=1))
    return rows


def out_products(rows, tap_ref, a, m):
    height = len(rows) - 2
    left = jnp.concatenate(
        [jnp.concatenate([rows[y + b][:m] for b in range(3)], axis=1) for y in range(height)], axis=0
    )
    part = tap_ref.shape[2] // 2
    starts = part_starts(part)
    lines = [[], [], [], []]
    for b in range(3):
        w = [
            jnp.concatenate([tap_ref[9 * a + 3 * b + c, :, pl.ds(start, part)] for start in starts], axis=1)
            for c in range(3)
        ]
        zero = jnp.zeros_like(w[0])
        for line, cells in zip(lines, ((w[1], w[2]), (w[0], w[1]), (zero, w[0]), (w[2], zero))):
            line += cells
    right = jnp.concatenate([jnp.concatenate(line, axis=1) for line in lines], axis=0)
    total = lax.dot_general(left, right, (((1,), (1,)), ((), ())), preferred_element_type=F32)
    return total.reshape(height, m, right.shape[0])


def mix(y, full, cols, ow, mix_ref):
    rows = full.shape[0]
    side = full[:, 2 * ow :]
    lane = lax.broadcasted_iota(jnp.int32, side.shape, 1)
    both = full[:, : 2 * ow] + jnp.where(lane < ow, shifted(side, cols, 1), shifted(side, cols, -1))
    mix_ref[y, pl.ds(0, rows, stride=2), :] = both
    mix_ref[y, pl.ds(1, rows, stride=2), :] = pltpu.roll(both, ow, 1)


def place_row(y, o_ref, mix_ref):
    rows, ow = o_ref.shape[2:]
    result = mix_ref[y][:, :ow].astype(BF16)
    for t in range(2):
        o_ref[t, y] = result[rows * t : rows * (t + 1)]


def early_out_kernel(cols, own_ref, other_ref, gain_ref, tap_ref, o_ref, acc_ref, mix_ref):
    size = 2 * cols
    rows = normalise(size, own_ref, other_ref, gain_ref)
    now, back, held = [out_products(rows, tap_ref, a, size) for a in (2, 1, 0)]
    height = now.shape[0]
    for y in range(height):
        full = jnp.concatenate([now[y, :cols], now[y, cols:] + back[y, :cols]], axis=0)
        mix(y, full, cols, o_ref.shape[3], mix_ref)
        acc_ref[y] = jnp.concatenate([held[y, :cols] + back[y, cols:], held[y, cols:]], axis=0)
    for y in range(height):
        place_row(y, o_ref, mix_ref)


def late_out_kernel(cols, own_ref, other_ref, gain_ref, tap_ref, early_ref, acc_ref, o_hbm, o_ref, mix_ref, sems):
    size = 2 * cols
    copies = [pltpu.make_async_copy(early_ref, o_hbm.at[pl.ds(0, 2)], sems.at[0])]
    copies[0].start()
    rows = normalise(size, own_ref, other_ref, gain_ref)
    now = out_products(rows, tap_ref, 2, size)
    back = out_products(rows, tap_ref, 1, -(-cols // 16) * 16)
    height = now.shape[0]
    for y in range(height):
        held = acc_ref[y]
        full = jnp.concatenate([held[:cols] + now[y, :cols], held[cols:] + now[y, cols:] + back[y, :cols]], axis=0)
        mix(y, full, cols, o_ref.shape[3], mix_ref)
    half = height // 2
    for k in range(2):
        for y in range(k * half, (k + 1) * half):
            place_row(y, o_ref, mix_ref)
        part = pl.ds(k * half, half)
        copies.append(
            pltpu.make_async_copy(o_ref.at[:, part], o_hbm.at[pl.ds(2, 2), part], sems.at[1 + k])
        )
        copies[-1].start()
    for copy in copies:
        copy.wait()


def params(mib):
    return pltpu.CompilerParams(vmem_limit_bytes=mib * MIB)


def cost(mflops):
    return pl.CostEstimate(flops=mflops * 10**6, bytes_accessed=10**7, transcendentals=0)


def vmem():
    return pl.BlockSpec(memory_space=pltpu.VMEM)


def in_space(space, *arrays):
    return tuple(pltpu.with_memory_space_constraint(x, space) for x in arrays)


def call(kernel, name, outs, ins, mib, mflops, scratch=(), in_specs=None, out_specs=None):
    results = pl.pallas_call(
        kernel,
        out_shape=outs,
        in_specs=in_specs or [vmem()] * len(ins),
        out_specs=out_specs or (vmem(),) * len(outs),
        scratch_shapes=list(scratch),
        compiler_params=params(mib),
        cost_estimate=cost(mflops),
        name=name,
    )(*ins)
    return results if out_specs else in_space(pltpu.VMEM, *results)


def body(codes, in_proj, gain_up, up_kernel, gain_res, out_kernel):
    frames, rows, cols = codes.shape
    size = 2 * cols
    width, share = up_kernel.shape[1:]
    ow = out_kernel.shape[1]
    pairs = rows + 1
    height = 2 * rows
    count = lax.axis_size("rows")
    joint = [pair for i in range(count - 1) for pair in ((2 * i + 1, 2 * i + 2), (2 * i + 2, 2 * i + 1))]
    swap = [(0, 1), (1, 0)]
    near = lax.ppermute(codes, ("rows", "section"), joint)
    gain_res = gain_res.reshape(1, -1)
    w, tap = in_space(pltpu.VMEM, up_kernel, out_kernel)
    codes, in_proj, gain_up = in_space(pltpu.HBM, codes, in_proj, gain_up.reshape(1, -1))
    hbm = pl.BlockSpec(memory_space=pltpu.HBM)
    hidden_shape = pltpu.VMEM((pairs * size, 4 * share), BF16)

    act, proj, gain = call(
        latent_kernel,
        "latent",
        (
            pltpu.VMEM((frames * rows * cols, width), BF16),
            pltpu.VMEM(in_proj.shape, BF16),
            pltpu.VMEM(gain_up.shape, F32),
        ),
        (codes, in_proj, gain_up),
        4,
        1000,
        [pltpu.VMEM(codes.shape, jnp.int32), pltpu.SemaphoreType.DMA((3,))],
        in_specs=[hbm] * 3,
    )
    cut = GROUPS[SPLIT][0]
    own_rows = 2 * rows * cols
    (own_first,) = call(
        functools.partial(own_first_kernel, rows * cols),
        "own_first",
        (pltpu.VMEM((own_rows, cut * share), F32),),
        (act, w),
        4,
        1000,
    )

    near, own_first = lax.optimization_barrier((near, own_first))
    far = lax.ppermute(near, "section", swap)
    near, far = in_space(pltpu.VMEM, near, far)
    own_rest, own_late = call(
        functools.partial(own_rest_kernel, rows * cols),
        "own_rest",
        (pltpu.VMEM((own_rows, (9 - cut) * share), F32), pltpu.VMEM((own_rows, 9 * share), F32)),
        (act, w, near),
        4,
        1000,
    )
    far, own_rest, own_late = lax.optimization_barrier((far, own_rest, own_late))

    early, halo = call(
        early_hidden_kernel,
        "hidden_early",
        (hidden_shape, pltpu.VMEM((2 * frames * cols, width), BF16)),
        (near, far, proj, gain, w, own_first, own_rest),
        8,
        1000,
    )
    early_other = lax.ppermute(early, "section", swap)
    (late,) = call(
        functools.partial(late_hidden_kernel, rows, cols),
        "hidden_late",
        (hidden_shape,),
        (halo, w, own_late),
        8,
        1000,
    )
    late_other = lax.ppermute(late, "section", swap)
    early_other, late_other = in_space(pltpu.VMEM, early_other, late_other)

    mixed = pltpu.VMEM((height, 2 * size, 2 * ow), F32)
    out_early, held = call(
        functools.partial(early_out_kernel, cols),
        "out_early",
        (pltpu.VMEM((2, height, 2 * cols, ow), BF16), pltpu.VMEM((height, size, 4 * ow), F32)),
        (early, early_other, gain_res, tap),
        12,
        2000,
        [mixed],
    )
    return call(
        functools.partial(late_out_kernel, cols),
        "out_late",
        jax.ShapeDtypeStruct((frames, height, 2 * cols, ow), BF16),
        (late, late_other, gain_res, tap, out_early, held),
        12,
        1000,
        [pltpu.VMEM((2, height, 2 * cols, ow), BF16), mixed, pltpu.SemaphoreType.DMA((3,))],
        out_specs=hbm,
    )


def solution(mesh):
    in_specs = (
        P("clip", "rows", None),
        P(),
        P(),
        P(None, None, "section"),
        P(),
        P(None, "section", None),
    )
    out_specs = P("clip", "rows", None, "section")
    return jax.shard_map(body, mesh=mesh, in_specs=in_specs, out_specs=out_specs, check_vma=False)
```

```python
import functools

import jax
import jax.numpy as jnp
from jax import lax
from jax.experimental import pallas as pl
from jax.experimental.pallas import tpu as pltpu
from jax.sharding import PartitionSpec as P

BITS = 18
EPS = 1e-06
F32 = jnp.float32
BF16 = jnp.bfloat16
MIB = 1024 * 1024
GROUPS = ((0, 2), (2, 2), (4, 2), (6, 2), (8, 1))
SPLIT = 2


def silu_of_half(h):
    return h + h * jnp.tanh(h)


def latent_rows(rows, in_proj, gain):
    cols = rows[0].shape[1]
    count = len(rows)
    wide = jnp.concatenate([jnp.broadcast_to(row, (cols, cols)) for row in rows], axis=0)
    sub = lax.broadcasted_iota(jnp.int32, (count, cols, cols), 1).reshape(count * cols, cols)
    lane = lax.broadcasted_iota(jnp.int32, (count * cols, cols), 1)
    picked = jnp.where(sub == lane, wide, 0).astype(F32)
    column = jnp.sum(picked, axis=1, keepdims=True).astype(jnp.int32)
    spread = jnp.broadcast_to(column, (count * cols, BITS))
    shift = lax.broadcasted_iota(jnp.int32, (count * cols, BITS), 1)
    bits = ((jnp.right_shift(spread, shift) & 1) * 2 - 1).astype(F32).astype(BF16)
    latent = jnp.dot(bits, in_proj, preferred_element_type=F32)
    mean = jnp.mean(latent * latent, axis=1, keepdims=True)
    return silu_of_half(latent * lax.rsqrt(mean + EPS) * (0.5 * gain))


def shifted(x, cols, amount):
    rows, lanes = x.shape
    place = lax.broadcasted_iota(jnp.int32, (rows // cols, cols, lanes), 1).reshape(rows, lanes)
    moved = pltpu.roll(x, amount % rows, 0)
    return jnp.where(place == (0 if amount == 1 else cols - 1), 0.0, moved)


def weights(w_ref, a, group):
    return jnp.concatenate([w_ref[9 * a + group[0] + k] for k in range(group[1])], axis=1)


def products(act, n, w_ref, group):
    share = w_ref.shape[2]
    if group[1] == 1:
        both = jnp.concatenate([weights(w_ref, 2, group), weights(w_ref, 1, group)], axis=1)
        now = jnp.dot(act, both, preferred_element_type=F32)
        now, back = now[:, :share], now[: 3 * n, share:]
    else:
        now = jnp.dot(act, weights(w_ref, 2, group), preferred_element_type=F32)
        back = jnp.dot(act[: 3 * n], weights(w_ref, 1, group), preferred_element_type=F32)
    oldest = jnp.dot(act[: 2 * n], weights(w_ref, 0, group), preferred_element_type=F32)
    return jnp.concatenate([now[:n], now[n : 2 * n] + back[:n], now[2 * n :] + back[n:] + oldest], axis=0)


def latent_kernel(codes_hbm, proj_hbm, gain_hbm, act_ref, proj_ref, gain_ref, codes_ref, sems):
    pairs = ((codes_hbm, codes_ref), (proj_hbm, proj_ref), (gain_hbm, gain_ref))
    copies = [pltpu.make_async_copy(src, dst, sems.at[n]) for n, (src, dst) in enumerate(pairs)]
    for copy in copies:
        copy.start()
    for copy in copies:
        copy.wait()
    frames, rows, cols = codes_ref.shape
    codes = [codes_ref[t, r : r + 1, :] for t in range(frames) for r in range(rows)]
    act_ref[...] = latent_rows(codes, proj_ref[...], gain_ref[...]).astype(BF16)


def lanes_of(group, share, start=0):
    return pl.ds((group[0] - start) * share, group[1] * share)


def own_first_kernel(n, act_ref, w_ref, first_ref):
    for group in GROUPS[:SPLIT]:
        first_ref[:, lanes_of(group, w_ref.shape[2])] = products(act_ref[...], n, w_ref, group)


def of_row(part, frames, stride, start, cols):
    return jnp.concatenate([part[t * stride + start : t * stride + start + cols] for t in range(frames)], axis=0)


def put_hidden(upper, lower, cols, share, q, h_ref):
    size = upper(0).shape[0]
    sums = [[], []]
    for c in range(3):
        x = upper(c) + lower(6 + c)
        sums[0].append(x + upper(3 + c))
        sums[1].append(x + lower(3 + c))
    out = pl.ds(q * size, size)
    for py, (left, mid, right) in enumerate(sums):
        even = shifted(left, cols, 1) + (mid + right)
        odd = (left + mid) + shifted(right, cols, -1)
        h_ref[out, pl.ds(2 * py * share, share)] = even.astype(BF16)
        h_ref[out, pl.ds((2 * py + 1) * share, share)] = odd.astype(BF16)


def own_rest_kernel(frames, cols, act_ref, w_ref, first_ref, after_ref, h_ref, edge_ref):
    share = w_ref.shape[2]
    n = act_ref.shape[0] // frames
    rows = n // cols
    act = act_ref[...]
    done = [first_ref[...]] + [products(act, n, w_ref, group) for group in GROUPS[SPLIT:]]
    taken = []
    for part in done:
        taken += [part[:, k * share : (k + 1) * share] for k in range(part.shape[1] // share)]

    def row(r):
        return lambda tap: of_row(taken[tap], frames, n, r * cols, cols)

    for q in range(rows - 1):
        put_hidden(row(q), row(q + 1), cols, share, q, h_ref)
    for k in range(6):
        edge_ref[0, :, pl.ds(k * share, share)] = row(0)(3 + k)
        edge_ref[1, :, pl.ds(k * share, share)] = row(rows - 1)(k)


def halo_kernel(near_ref, far_ref, proj_ref, gain_ref, w_ref, edge_ref, h_ref):
    frames, rows, cols = near_ref.shape
    share = w_ref.shape[2]
    first = lax.axis_index("section") == 0
    place = lax.axis_index("rows")
    last = lax.axis_size("rows") - 1
    codes = []
    for t in range(frames):
        low = [ref[t, rows - 1 : rows, :] for ref in (near_ref, far_ref)]
        high = [ref[t, 0:1, :] for ref in (near_ref, far_ref)]
        codes += [jnp.where(first, low[0], low[1]), jnp.where(first, high[1], high[0])]
    act = latent_rows(codes, proj_ref[...], gain_ref[...])
    side = lax.broadcasted_iota(jnp.int32, (frames, 2, cols, act.shape[1]), 1).reshape(act.shape)
    keep = jnp.where(side == 0, (place > 0).astype(F32), (place < last).astype(F32))
    act = (act * keep).astype(BF16)
    halo = jnp.concatenate([products(act, 2 * cols, w_ref, group) for group in GROUPS], axis=1)

    def outer(e):
        return lambda tap: of_row(halo[:, tap * share : (tap + 1) * share], frames, 2 * cols, e * cols, cols)

    put_hidden(outer(0), lambda tap: edge_ref[0, :, pl.ds((tap - 3) * share, share)], cols, share, 0, h_ref)
    put_hidden(lambda tap: edge_ref[1, :, pl.ds(tap * share, share)], outer(1), cols, share, 1, h_ref)


def part_starts(part):
    section = lax.axis_index("section")
    return [pl.multiple_of(k * part, part) for k in (section, 1 - section)]


def normalise(size, own_ref, other_ref, gain_ref, keeps):
    part = own_ref.shape[1] // 4
    gains = [0.5 * gain_ref[:, pl.ds(start, part)] for start in part_starts(part)]
    rows = []
    for j, keep in enumerate(keeps):
        cells = []
        for px in range(2):
            lanes = pl.ds((2 * (j % 2) + px) * part, part)
            x = [ref[pl.ds(j // 2 * size, size), lanes].astype(F32) for ref in (own_ref, other_ref)]
            mean = jnp.sum(x[0] * x[0] + x[1] * x[1], axis=1, keepdims=True) / (2 * part)
            scale = lax.rsqrt(mean + EPS)
            if keep is not None:
                scale = jnp.where(keep, scale, 0.0)
            cells += [silu_of_half(x[s] * scale * gains[s]).astype(BF16) for s in range(2)]
        rows.append(jnp.concatenate(cells, axis=1))
    return rows


def out_products(windows, tap_ref, a, m):
    left = jnp.concatenate([jnp.concatenate([row[:m] for row in window], axis=1) for window in windows], axis=0)
    part = tap_ref.shape[2] // 2
    starts = part_starts(part)
    lines = [[], [], [], []]
    for b in range(3):
        w = [
            jnp.concatenate([tap_ref[9 * a + 3 * b + c, :, pl.ds(start, part)] for start in starts], axis=1)
            for c in range(3)
        ]
        zero = jnp.zeros_like(w[0])
        for line, cells in zip(lines, ((w[1], w[2]), (w[0], w[1]), (zero, w[0]), (w[2], zero))):
            line += cells
    right = jnp.concatenate([jnp.concatenate(line, axis=1) for line in lines], axis=0)
    total = lax.dot_general(left, right, (((1,), (1,)), ((), ())), preferred_element_type=F32)
    return total.reshape(len(windows), m, right.shape[0])


def out_rows(windows, tap_ref, frames, cols, mix_ref, o_ref):
    size = frames * cols
    height = len(windows)
    rows, ow = o_ref.shape[2:]
    now, back, oldest = [out_products(windows, tap_ref, a, -(-(frames - 2 + a) * cols // 16) * 16) for a in (2, 1, 0)]
    for y in range(height):
        full = jnp.concatenate(
            [
                now[y, :cols],
                now[y, cols : 2 * cols] + back[y, :cols],
                now[y, 2 * cols :] + back[y, cols : size - cols] + oldest[y, : size - 2 * cols],
            ],
            axis=0,
        )
        side = full[:, 2 * ow :]
        lane = lax.broadcasted_iota(jnp.int32, side.shape, 1)
        both = full[:, : 2 * ow] + jnp.where(lane < ow, shifted(side, cols, 1), shifted(side, cols, -1))
        mix_ref[y, pl.ds(0, size, stride=2), :] = both
        mix_ref[y, pl.ds(1, size, stride=2), :] = pltpu.roll(both, ow, 1)
    for y in range(height):
        result = mix_ref[y][:, :ow].astype(BF16)
        for t in range(frames):
            o_ref[t, y] = result[rows * t : rows * (t + 1)]


def inner_out_kernel(frames, cols, own_ref, other_ref, gain_ref, tap_ref, o_ref, norm_ref, mix_ref):
    size = frames * cols
    count = own_ref.shape[0] // size * 2
    rows = normalise(size, own_ref, other_ref, gain_ref, [None] * count)
    for k, j in enumerate((0, 1, count - 2, count - 1)):
        norm_ref[k] = rows[j]
    out_rows([rows[y : y + 3] for y in range(count - 2)], tap_ref, frames, cols, mix_ref, o_ref)


def edge_out_kernel(frames, cols, own_ref, other_ref, gain_ref, tap_ref, norm_ref, inner_ref, o_hbm, o_ref, mix_ref, sems):
    size = frames * cols
    inner = inner_ref.shape[1]
    copies = [pltpu.make_async_copy(inner_ref, o_hbm.at[:, pl.ds(2, inner)], sems.at[0])]
    copies[0].start()
    place = lax.axis_index("rows")
    last = lax.axis_size("rows") - 1
    edge = normalise(size, own_ref, other_ref, gain_ref, (place > 0, None, None, place < last))
    top = edge[:2] + [norm_ref[0], norm_ref[1]]
    bottom = [norm_ref[2], norm_ref[3]] + edge[2:]
    windows = [side[y : y + 3] for side in (top, bottom) for y in range(2)]
    out_rows(windows, tap_ref, frames, cols, mix_ref, o_ref)
    for k, start in enumerate((0, inner + 2)):
        copies.append(
            pltpu.make_async_copy(o_ref.at[:, pl.ds(2 * k, 2)], o_hbm.at[:, pl.ds(start, 2)], sems.at[1 + k])
        )
        copies[-1].start()
    for copy in copies:
        copy.wait()


def params(mib):
    return pltpu.CompilerParams(vmem_limit_bytes=mib * MIB)


def cost(mflops):
    return pl.CostEstimate(flops=mflops * 10**6, bytes_accessed=10**7, transcendentals=0)


def vmem():
    return pl.BlockSpec(memory_space=pltpu.VMEM)


def in_space(space, *arrays):
    return tuple(pltpu.with_memory_space_constraint(x, space) for x in arrays)


def call(kernel, name, outs, ins, mib, mflops, scratch=(), in_specs=None, out_specs=None):
    results = pl.pallas_call(
        kernel,
        out_shape=outs,
        in_specs=in_specs or [vmem()] * len(ins),
        out_specs=out_specs or (vmem(),) * len(outs),
        scratch_shapes=list(scratch),
        compiler_params=params(mib),
        cost_estimate=cost(mflops),
        name=name,
    )(*ins)
    return results if out_specs else in_space(pltpu.VMEM, *results)


def body(codes, in_proj, gain_up, up_kernel, gain_res, out_kernel):
    frames, rows, cols = codes.shape
    size = frames * cols
    width, share = up_kernel.shape[1:]
    ow = out_kernel.shape[1]
    height = 2 * rows
    inner = height - 4
    count = lax.axis_size("rows")
    joint = [pair for i in range(count - 1) for pair in ((2 * i + 1, 2 * i + 2), (2 * i + 2, 2 * i + 1))]
    swap = [(0, 1), (1, 0)]
    near = lax.ppermute(codes, ("rows", "section"), joint)
    gain_res = gain_res.reshape(1, -1)
    w, tap = in_space(pltpu.VMEM, up_kernel, out_kernel)
    codes, in_proj, gain_up = in_space(pltpu.HBM, codes, in_proj, gain_up.reshape(1, -1))
    hbm = pl.BlockSpec(memory_space=pltpu.HBM)

    act, proj, gain = call(
        latent_kernel,
        "latent",
        (
            pltpu.VMEM((frames * rows * cols, width), BF16),
            pltpu.VMEM(in_proj.shape, BF16),
            pltpu.VMEM(gain_up.shape, F32),
        ),
        (codes, in_proj, gain_up),
        4,
        1000,
        [pltpu.VMEM(codes.shape, jnp.int32), pltpu.SemaphoreType.DMA((3,))],
        in_specs=[hbm] * 3,
    )
    cut = GROUPS[SPLIT][0]
    (own_first,) = call(
        functools.partial(own_first_kernel, rows * cols),
        "own_first",
        (pltpu.VMEM((rows * size, cut * share), F32),),
        (act, w),
        6,
        1000,
    )

    near, own_first = lax.optimization_barrier((near, own_first))
    far = lax.ppermute(near, "section", swap)
    near, far, own_first = in_space(pltpu.VMEM, near, far, own_first)
    inner_own, edge = call(
        functools.partial(own_rest_kernel, frames, cols),
        "own_rest",
        (pltpu.VMEM(((rows - 1) * size, 4 * share), BF16), pltpu.VMEM((2, size, 6 * share), F32)),
        (act, w, own_first, near),
        8,
        1000,
    )
    far, inner_own, edge = lax.optimization_barrier((far, inner_own, edge))
    inner_other = lax.ppermute(inner_own, "section", swap)
    far, inner_own, edge = in_space(pltpu.VMEM, far, inner_own, edge)
    (edge_own,) = call(
        halo_kernel,
        "halo",
        (pltpu.VMEM((2 * size, 4 * share), BF16),),
        (near, far, proj, gain, w, edge),
        8,
        3000,
    )
    edge_other = lax.ppermute(edge_own, "section", swap)
    inner_other, edge_other = in_space(pltpu.VMEM, inner_other, edge_other)

    mixed = pltpu.VMEM((max(inner, 4), 2 * size, 2 * ow), F32)
    out_inner, norm = call(
        functools.partial(inner_out_kernel, frames, cols),
        "out_inner",
        (pltpu.VMEM((frames, inner, 2 * cols, ow), BF16), pltpu.VMEM((4, size, 4 * share), BF16)),
        (inner_own, inner_other, gain_res, tap),
        12,
        2000,
        [mixed],
    )
    return call(
        functools.partial(edge_out_kernel, frames, cols),
        "out_edge",
        jax.ShapeDtypeStruct((frames, height, 2 * cols, ow), BF16),
        (edge_own, edge_other, gain_res, tap, norm, out_inner),
        12,
        1000,
        [pltpu.VMEM((frames, 4, 2 * cols, ow), BF16), mixed, pltpu.SemaphoreType.DMA((3,))],
        out_specs=hbm,
    )


def solution(mesh):
    in_specs = (
        P("clip", "rows", None),
        P(),
        P(),
        P(None, None, "section"),
        P(),
        P(None, "section", None),
    )
    out_specs = P("clip", "rows", None, "section")
    return jax.shard_map(body, mesh=mesh, in_specs=in_specs, out_specs=out_specs, check_vma=False)
```

```python
import functools

import jax
import jax.numpy as jnp
from jax import lax
from jax.experimental import pallas as pl
from jax.experimental.pallas import tpu as pltpu
from jax.sharding import PartitionSpec as P

BITS = 18
EPS = 1e-06
F32 = jnp.float32
BF16 = jnp.bfloat16
MIB = 1024 * 1024
GROUPS = ((0, 2), (2, 2), (4, 2), (6, 2), (8, 1))
SPLIT = 2


def silu_of_half(h):
    return h + h * jnp.tanh(h)


def latent_rows(rows, in_proj, gain):
    cols = rows[0].shape[1]
    count = len(rows)
    wide = jnp.concatenate([jnp.broadcast_to(row, (cols, cols)) for row in rows], axis=0)
    sub = lax.broadcasted_iota(jnp.int32, (count, cols, cols), 1).reshape(count * cols, cols)
    lane = lax.broadcasted_iota(jnp.int32, (count * cols, cols), 1)
    picked = jnp.where(sub == lane, wide, 0).astype(F32)
    column = jnp.sum(picked, axis=1, keepdims=True).astype(jnp.int32)
    spread = jnp.broadcast_to(column, (count * cols, BITS))
    shift = lax.broadcasted_iota(jnp.int32, (count * cols, BITS), 1)
    bits = ((jnp.right_shift(spread, shift) & 1) * 2 - 1).astype(F32).astype(BF16)
    latent = jnp.dot(bits, in_proj, preferred_element_type=F32)
    mean = jnp.mean(latent * latent, axis=1, keepdims=True)
    return silu_of_half(latent * lax.rsqrt(mean + EPS) * (0.5 * gain))


def shifted(x, cols, amount):
    rows, lanes = x.shape
    place = lax.broadcasted_iota(jnp.int32, (rows // cols, cols, lanes), 1).reshape(rows, lanes)
    moved = pltpu.roll(x, amount % rows, 0)
    return jnp.where(place == (0 if amount == 1 else cols - 1), 0.0, moved)


def weights(w_ref, a, group):
    return jnp.concatenate([w_ref[9 * a + group[0] + k] for k in range(group[1])], axis=1)


def products(act, n, w_ref, group):
    share = w_ref.shape[2]
    if group[1] == 1:
        both = jnp.concatenate([weights(w_ref, 2, group), weights(w_ref, 1, group)], axis=1)
        now = jnp.dot(act, both, preferred_element_type=F32)
        now, back = now[:, :share], now[: 3 * n, share:]
    else:
        now = jnp.dot(act, weights(w_ref, 2, group), preferred_element_type=F32)
        back = jnp.dot(act[: 3 * n], weights(w_ref, 1, group), preferred_element_type=F32)
    oldest = jnp.dot(act[: 2 * n], weights(w_ref, 0, group), preferred_element_type=F32)
    return jnp.concatenate([now[:n], now[n : 2 * n] + back[:n], now[2 * n :] + back[n:] + oldest], axis=0)


def latent_kernel(codes_hbm, proj_hbm, gain_hbm, act_ref, proj_ref, gain_ref, codes_ref, sems):
    pairs = ((codes_hbm, codes_ref), (proj_hbm, proj_ref), (gain_hbm, gain_ref))
    copies = [pltpu.make_async_copy(src, dst, sems.at[n]) for n, (src, dst) in enumerate(pairs)]
    for copy in copies:
        copy.start()
    for copy in copies:
        copy.wait()
    frames, rows, cols = codes_ref.shape
    codes = [codes_ref[t, r : r + 1, :] for t in range(frames) for r in range(rows)]
    act_ref[...] = latent_rows(codes, proj_ref[...], gain_ref[...]).astype(BF16)


def lanes_of(group, share, start=0):
    return pl.ds((group[0] - start) * share, group[1] * share)


def own_first_kernel(n, act_ref, w_ref, first_ref):
    for group in GROUPS[:SPLIT]:
        first_ref[:, lanes_of(group, w_ref.shape[2])] = products(act_ref[...], n, w_ref, group)


def of_row(part, frames, stride, start, cols):
    return jnp.concatenate([part[t * stride + start : t * stride + start + cols] for t in range(frames)], axis=0)


def put_hidden(upper, lower, cols, share, q, h_ref):
    size = upper(0).shape[0]
    sums = [[], []]
    for c in range(3):
        x = upper(c) + lower(6 + c)
        sums[0].append(x + upper(3 + c))
        sums[1].append(x + lower(3 + c))
    out = pl.ds(q * size, size)
    for py, (left, mid, right) in enumerate(sums):
        even = shifted(left, cols, 1) + (mid + right)
        odd = (left + mid) + shifted(right, cols, -1)
        h_ref[out, pl.ds(2 * py * share, share)] = even.astype(BF16)
        h_ref[out, pl.ds((2 * py + 1) * share, share)] = odd.astype(BF16)


def own_rest_kernel(frames, cols, act_ref, w_ref, first_ref, after_ref, h_ref, edge_ref):
    share = w_ref.shape[2]
    n = act_ref.shape[0] // frames
    rows = n // cols
    act = act_ref[...]
    done = [first_ref[...]] + [products(act, n, w_ref, group) for group in GROUPS[SPLIT:]]
    taken = []
    for part in done:
        taken += [part[:, k * share : (k + 1) * share] for k in range(part.shape[1] // share)]

    def row(r):
        return lambda tap: of_row(taken[tap], frames, n, r * cols, cols)

    for q in range(rows - 1):
        put_hidden(row(q), row(q + 1), cols, share, q, h_ref)
    for k in range(6):
        edge_ref[0, :, pl.ds(k * share, share)] = row(0)(3 + k)
        edge_ref[1, :, pl.ds(k * share, share)] = row(rows - 1)(k)


def halo_kernel(near_ref, far_ref, proj_ref, gain_ref, w_ref, edge_ref, h_ref):
    frames, rows, cols = near_ref.shape
    share = w_ref.shape[2]
    first = lax.axis_index("section") == 0
    place = lax.axis_index("rows")
    last = lax.axis_size("rows") - 1
    codes = []
    for t in range(frames):
        low = [ref[t, rows - 1 : rows, :] for ref in (near_ref, far_ref)]
        high = [ref[t, 0:1, :] for ref in (near_ref, far_ref)]
        codes += [jnp.where(first, low[0], low[1]), jnp.where(first, high[1], high[0])]
    act = latent_rows(codes, proj_ref[...], gain_ref[...])
    side = lax.broadcasted_iota(jnp.int32, (frames, 2, cols, act.shape[1]), 1).reshape(act.shape)
    keep = jnp.where(side == 0, (place > 0).astype(F32), (place < last).astype(F32))
    act = (act * keep).astype(BF16)
    halo = jnp.concatenate([products(act, 2 * cols, w_ref, group) for group in GROUPS], axis=1)

    def outer(e):
        return lambda tap: of_row(halo[:, tap * share : (tap + 1) * share], frames, 2 * cols, e * cols, cols)

    put_hidden(outer(0), lambda tap: edge_ref[0, :, pl.ds((tap - 3) * share, share)], cols, share, 0, h_ref)
    put_hidden(lambda tap: edge_ref[1, :, pl.ds(tap * share, share)], outer(1), cols, share, 1, h_ref)


def part_starts(part):
    section = lax.axis_index("section")
    return [pl.multiple_of(k * part, part) for k in (section, 1 - section)]


def normalise(size, own_ref, other_ref, gain_ref, keeps):
    part = own_ref.shape[1] // 4
    gains = [0.5 * gain_ref[:, pl.ds(start, part)] for start in part_starts(part)]
    rows = []
    for j, keep in enumerate(keeps):
        cells = []
        for px in range(2):
            lanes = pl.ds((2 * (j % 2) + px) * part, part)
            x = [ref[pl.ds(j // 2 * size, size), lanes].astype(F32) for ref in (own_ref, other_ref)]
            mean = jnp.sum(x[0] * x[0] + x[1] * x[1], axis=1, keepdims=True) / (2 * part)
            scale = lax.rsqrt(mean + EPS)
            if keep is not None:
                scale = jnp.where(keep, scale, 0.0)
            cells += [silu_of_half(x[s] * scale * gains[s]).astype(BF16) for s in range(2)]
        rows.append(jnp.concatenate(cells, axis=1))
    return rows


def out_products(windows, tap_ref, a, m):
    left = jnp.concatenate([jnp.concatenate([row[:m] for row in window], axis=1) for window in windows], axis=0)
    part = tap_ref.shape[2] // 2
    starts = part_starts(part)
    lines = [[], [], [], []]
    for b in range(3):
        w = [
            jnp.concatenate([tap_ref[9 * a + 3 * b + c, :, pl.ds(start, part)] for start in starts], axis=1)
            for c in range(3)
        ]
        zero = jnp.zeros_like(w[0])
        for line, cells in zip(lines, ((w[1], w[2]), (w[0], w[1]), (zero, w[0]), (w[2], zero))):
            line += cells
    right = jnp.concatenate([jnp.concatenate(line, axis=1) for line in lines], axis=0)
    total = lax.dot_general(left, right, (((1,), (1,)), ((), ())), preferred_element_type=F32)
    return total.reshape(len(windows), m, right.shape[0])


def out_rows(windows, tap_ref, frames, cols, mix_ref, o_ref):
    size = frames * cols
    height = len(windows)
    rows, ow = o_ref.shape[2:]
    now, back, oldest = [out_products(windows, tap_ref, a, -(-(frames - 2 + a) * cols // 16) * 16) for a in (2, 1, 0)]
    for y in range(height):
        full = jnp.concatenate(
            [
                now[y, :cols],
                now[y, cols : 2 * cols] + back[y, :cols],
                now[y, 2 * cols :] + back[y, cols : size - cols] + oldest[y, : size - 2 * cols],
            ],
            axis=0,
        )
        side = full[:, 2 * ow :]
        lane = lax.broadcasted_iota(jnp.int32, side.shape, 1)
        both = full[:, : 2 * ow] + jnp.where(lane < ow, shifted(side, cols, 1), shifted(side, cols, -1))
        mix_ref[y, pl.ds(0, size, stride=2), :] = both
        mix_ref[y, pl.ds(1, size, stride=2), :] = pltpu.roll(both, ow, 1)
    for y in range(height):
        result = mix_ref[y][:, :ow].astype(BF16)
        for t in range(frames):
            o_ref[t, y] = result[rows * t : rows * (t + 1)]


def inner_out_kernel(frames, cols, own_ref, other_ref, gain_ref, tap_ref, o_ref, norm_ref, mix_ref):
    size = frames * cols
    count = own_ref.shape[0] // size * 2
    rows = normalise(size, own_ref, other_ref, gain_ref, [None] * count)
    for k, j in enumerate((0, 1, count - 2, count - 1)):
        norm_ref[k] = rows[j]
    out_rows([rows[y : y + 3] for y in range(count - 2)], tap_ref, frames, cols, mix_ref, o_ref)


def edge_out_kernel(frames, cols, own_ref, other_ref, gain_ref, tap_ref, norm_ref, inner_ref, o_hbm, o_ref, mix_ref, sems):
    size = frames * cols
    inner = inner_ref.shape[1]
    copies = [pltpu.make_async_copy(inner_ref, o_hbm.at[:, pl.ds(2, inner)], sems.at[0])]
    copies[0].start()
    place = lax.axis_index("rows")
    last = lax.axis_size("rows") - 1
    edge = normalise(size, own_ref, other_ref, gain_ref, (place > 0, None, None, place < last))
    top = edge[:2] + [norm_ref[0], norm_ref[1]]
    bottom = [norm_ref[2], norm_ref[3]] + edge[2:]
    windows = [side[y : y + 3] for side in (top, bottom) for y in range(2)]
    out_rows(windows, tap_ref, frames, cols, mix_ref, o_ref)
    for k, start in enumerate((0, inner + 2)):
        copies.append(
            pltpu.make_async_copy(o_ref.at[:, pl.ds(2 * k, 2)], o_hbm.at[:, pl.ds(start, 2)], sems.at[1 + k])
        )
        copies[-1].start()
    for copy in copies:
        copy.wait()


def params(mib):
    return pltpu.CompilerParams(vmem_limit_bytes=mib * MIB)


def cost(mflops):
    return pl.CostEstimate(flops=mflops * 10**6, bytes_accessed=10**7, transcendentals=0)


def vmem():
    return pl.BlockSpec(memory_space=pltpu.VMEM)


def in_space(space, *arrays):
    return tuple(pltpu.with_memory_space_constraint(x, space) for x in arrays)


def call(kernel, name, outs, ins, mib, mflops, scratch=(), in_specs=None, out_specs=None):
    results = pl.pallas_call(
        kernel,
        out_shape=outs,
        in_specs=in_specs or [vmem()] * len(ins),
        out_specs=out_specs or (vmem(),) * len(outs),
        scratch_shapes=list(scratch),
        compiler_params=params(mib),
        cost_estimate=cost(mflops),
        name=name,
    )(*ins)
    return results if out_specs else in_space(pltpu.VMEM, *results)


def body(codes, in_proj, gain_up, up_kernel, gain_res, out_kernel):
    frames, rows, cols = codes.shape
    size = frames * cols
    width, share = up_kernel.shape[1:]
    ow = out_kernel.shape[1]
    height = 2 * rows
    inner = height - 4
    count = lax.axis_size("rows")
    joint = [pair for i in range(count - 1) for pair in ((2 * i + 1, 2 * i + 2), (2 * i + 2, 2 * i + 1))]
    swap = [(0, 1), (1, 0)]
    near = lax.ppermute(codes, ("rows", "section"), joint)
    gain_res = gain_res.reshape(1, -1)
    w, tap = in_space(pltpu.VMEM, up_kernel, out_kernel)
    codes, in_proj, gain_up = in_space(pltpu.HBM, codes, in_proj, gain_up.reshape(1, -1))
    hbm = pl.BlockSpec(memory_space=pltpu.HBM)

    act, proj, gain = call(
        latent_kernel,
        "latent",
        (
            pltpu.VMEM((frames * rows * cols, width), BF16),
            pltpu.VMEM(in_proj.shape, BF16),
            pltpu.VMEM(gain_up.shape, F32),
        ),
        (codes, in_proj, gain_up),
        4,
        1000,
        [pltpu.VMEM(codes.shape, jnp.int32), pltpu.SemaphoreType.DMA((3,))],
        in_specs=[hbm] * 3,
    )
    cut = GROUPS[SPLIT][0]
    (own_first,) = call(
        functools.partial(own_first_kernel, rows * cols),
        "own_first",
        (pltpu.VMEM((rows * size, cut * share), F32),),
        (act, w),
        6,
        1000,
    )

    near, own_first = lax.optimization_barrier((near, own_first))
    far = lax.ppermute(near, "section", swap)
    near, far, own_first = in_space(pltpu.VMEM, near, far, own_first)
    inner_own, edge = call(
        functools.partial(own_rest_kernel, frames, cols),
        "own_rest",
        (pltpu.VMEM(((rows - 1) * size, 4 * share), BF16), pltpu.VMEM((2, size, 6 * share), F32)),
        (act, w, own_first, near),
        8,
        1000,
    )
    inner_other = lax.ppermute(inner_own, "section", swap)
    far, edge = lax.optimization_barrier((far, edge))
    far, edge = in_space(pltpu.VMEM, far, edge)
    (edge_own,) = call(
        halo_kernel,
        "halo",
        (pltpu.VMEM((2 * size, 4 * share), BF16),),
        (near, far, proj, gain, w, edge),
        8,
        20000,
    )
    edge_other = lax.ppermute(edge_own, "section", swap)
    inner_other, edge_other = in_space(pltpu.VMEM, inner_other, edge_other)

    mixed = pltpu.VMEM((max(inner, 4), 2 * size, 2 * ow), F32)
    out_inner, norm = call(
        functools.partial(inner_out_kernel, frames, cols),
        "out_inner",
        (pltpu.VMEM((frames, inner, 2 * cols, ow), BF16), pltpu.VMEM((4, size, 4 * share), BF16)),
        (inner_own, inner_other, gain_res, tap),
        12,
        2000,
        [mixed],
    )
    return call(
        functools.partial(edge_out_kernel, frames, cols),
        "out_edge",
        jax.ShapeDtypeStruct((frames, height, 2 * cols, ow), BF16),
        (edge_own, edge_other, gain_res, tap, norm, out_inner),
        12,
        1000,
        [pltpu.VMEM((frames, 4, 2 * cols, ow), BF16), mixed, pltpu.SemaphoreType.DMA((3,))],
        out_specs=hbm,
    )


def solution(mesh):
    in_specs = (
        P("clip", "rows", None),
        P(),
        P(),
        P(None, None, "section"),
        P(),
        P(None, "section", None),
    )
    out_specs = P("clip", "rows", None, "section")
    return jax.shard_map(body, mesh=mesh, in_specs=in_specs, out_specs=out_specs, check_vma=False)
```

```python
import functools

import jax
import jax.numpy as jnp
from jax import lax
from jax.experimental import pallas as pl
from jax.experimental.pallas import tpu as pltpu
from jax.sharding import PartitionSpec as P

BITS = 18
EPS = 1e-06
F32 = jnp.float32
BF16 = jnp.bfloat16
MIB = 1024 * 1024
GROUPS = ((0, 2), (2, 2), (4, 2), (6, 2), (8, 1))
SPLIT = 3


def silu_of_half(h):
    return h + h * jnp.tanh(h)


def latent_rows(rows, in_proj, gain):
    cols = rows[0].shape[1]
    count = len(rows)
    wide = jnp.concatenate([jnp.broadcast_to(row, (cols, cols)) for row in rows], axis=0)
    sub = lax.broadcasted_iota(jnp.int32, (count, cols, cols), 1).reshape(count * cols, cols)
    lane = lax.broadcasted_iota(jnp.int32, (count * cols, cols), 1)
    picked = jnp.where(sub == lane, wide, 0).astype(F32)
    column = jnp.sum(picked, axis=1, keepdims=True).astype(jnp.int32)
    spread = jnp.broadcast_to(column, (count * cols, BITS))
    shift = lax.broadcasted_iota(jnp.int32, (count * cols, BITS), 1)
    bits = ((jnp.right_shift(spread, shift) & 1) * 2 - 1).astype(F32).astype(BF16)
    latent = jnp.dot(bits, in_proj, preferred_element_type=F32)
    mean = jnp.mean(latent * latent, axis=1, keepdims=True)
    return silu_of_half(latent * lax.rsqrt(mean + EPS) * (0.5 * gain))


def shifted(x, cols, amount):
    rows, lanes = x.shape
    place = lax.broadcasted_iota(jnp.int32, (rows // cols, cols, lanes), 1).reshape(rows, lanes)
    moved = pltpu.roll(x, amount % rows, 0)
    return jnp.where(place == (0 if amount == 1 else cols - 1), 0.0, moved)


def weights(w_ref, a, group):
    return jnp.concatenate([w_ref[9 * a + group[0] + k] for k in range(group[1])], axis=1)


def products(act, n, w_ref, group):
    share = w_ref.shape[2]
    if group[1] == 1:
        both = jnp.concatenate([weights(w_ref, 2, group), weights(w_ref, 1, group)], axis=1)
        now = jnp.dot(act, both, preferred_element_type=F32)
        now, back = now[:, :share], now[: 3 * n, share:]
    else:
        now = jnp.dot(act, weights(w_ref, 2, group), preferred_element_type=F32)
        back = jnp.dot(act[: 3 * n], weights(w_ref, 1, group), preferred_element_type=F32)
    oldest = jnp.dot(act[: 2 * n], weights(w_ref, 0, group), preferred_element_type=F32)
    return jnp.concatenate([now[:n], now[n : 2 * n] + back[:n], now[2 * n :] + back[n:] + oldest], axis=0)


def open_kernel(mark_ref):
    mark_ref[...] = jnp.zeros_like(mark_ref)


def latent_kernel(codes_ref, proj_ref, gain_ref, mark_ref, act_ref):
    frames, rows, cols = codes_ref.shape
    codes = [codes_ref[t, r : r + 1, :] for t in range(frames) for r in range(rows)]
    act_ref[...] = latent_rows(codes, proj_ref[...], gain_ref[...]).astype(BF16)


def lanes_of(group, share, start=0):
    return pl.ds((group[0] - start) * share, group[1] * share)


def own_first_kernel(n, act_ref, w_ref, first_ref):
    for group in GROUPS[:SPLIT]:
        first_ref[:, lanes_of(group, w_ref.shape[2])] = products(act_ref[...], n, w_ref, group)


def of_row(part, frames, stride, start, cols):
    return jnp.concatenate([part[t * stride + start : t * stride + start + cols] for t in range(frames)], axis=0)


def put_hidden(upper, lower, cols, share, q, h_ref):
    size = upper(0).shape[0]
    sums = [[], []]
    for c in range(3):
        x = upper(c) + lower(6 + c)
        sums[0].append(x + upper(3 + c))
        sums[1].append(x + lower(3 + c))
    out = pl.ds(q * size, size)
    for py, (left, mid, right) in enumerate(sums):
        even = shifted(left, cols, 1) + (mid + right)
        odd = (left + mid) + shifted(right, cols, -1)
        h_ref[out, pl.ds(2 * py * share, share)] = even.astype(BF16)
        h_ref[out, pl.ds((2 * py + 1) * share, share)] = odd.astype(BF16)


def own_rest_kernel(frames, cols, act_ref, w_ref, first_ref, after_ref, h_ref, edge_ref):
    share = w_ref.shape[2]
    n = act_ref.shape[0] // frames
    rows = n // cols
    act = act_ref[...]
    done = [first_ref[...]] + [products(act, n, w_ref, group) for group in GROUPS[SPLIT:]]
    taken = []
    for part in done:
        taken += [part[:, k * share : (k + 1) * share] for k in range(part.shape[1] // share)]

    def row(r):
        return lambda tap: of_row(taken[tap], frames, n, r * cols, cols)

    for q in range(rows - 1):
        put_hidden(row(q), row(q + 1), cols, share, q, h_ref)
    for k in range(6):
        edge_ref[0, :, pl.ds(k * share, share)] = row(0)(3 + k)
        edge_ref[1, :, pl.ds(k * share, share)] = row(rows - 1)(k)


def halo_kernel(near_ref, far_ref, proj_ref, gain_ref, w_ref, edge_ref, h_ref):
    frames, rows, cols = near_ref.shape
    share = w_ref.shape[2]
    first = lax.axis_index("section") == 0
    place = lax.axis_index("rows")
    last = lax.axis_size("rows") - 1
    codes = []
    for t in range(frames):
        low = [ref[t, rows - 1 : rows, :] for ref in (near_ref, far_ref)]
        high = [ref[t, 0:1, :] for ref in (near_ref, far_ref)]
        codes += [jnp.where(first, low[0], low[1]), jnp.where(first, high[1], high[0])]
    act = latent_rows(codes, proj_ref[...], gain_ref[...])
    side = lax.broadcasted_iota(jnp.int32, (frames, 2, cols, act.shape[1]), 1).reshape(act.shape)
    keep = jnp.where(side == 0, (place > 0).astype(F32), (place < last).astype(F32))
    act = (act * keep).astype(BF16)
    halo = jnp.concatenate([products(act, 2 * cols, w_ref, group) for group in GROUPS], axis=1)

    def outer(e):
        return lambda tap: of_row(halo[:, tap * share : (tap + 1) * share], frames, 2 * cols, e * cols, cols)

    put_hidden(outer(0), lambda tap: edge_ref[0, :, pl.ds((tap - 3) * share, share)], cols, share, 0, h_ref)
    put_hidden(lambda tap: edge_ref[1, :, pl.ds(tap * share, share)], outer(1), cols, share, 1, h_ref)


def part_starts(part):
    section = lax.axis_index("section")
    return [pl.multiple_of(k * part, part) for k in (section, 1 - section)]


def normalise(size, own_ref, other_ref, gain_ref, keeps):
    part = own_ref.shape[1] // 4
    gains = [0.5 * gain_ref[:, pl.ds(start, part)] for start in part_starts(part)]
    rows = []
    for j, keep in enumerate(keeps):
        cells = []
        for px in range(2):
            lanes = pl.ds((2 * (j % 2) + px) * part, part)
            x = [ref[pl.ds(j // 2 * size, size), lanes].astype(F32) for ref in (own_ref, other_ref)]
            mean = jnp.sum(x[0] * x[0] + x[1] * x[1], axis=1, keepdims=True) / (2 * part)
            scale = lax.rsqrt(mean + EPS)
            if keep is not None:
                scale = jnp.where(keep, scale, 0.0)
            cells += [silu_of_half(x[s] * scale * gains[s]).astype(BF16) for s in range(2)]
        rows.append(jnp.concatenate(cells, axis=1))
    return rows


def out_products(windows, tap_ref, a, m):
    left = jnp.concatenate([jnp.concatenate([row[:m] for row in window], axis=1) for window in windows], axis=0)
    part = tap_ref.shape[2] // 2
    starts = part_starts(part)
    lines = [[], [], [], []]
    for b in range(3):
        w = [
            jnp.concatenate([tap_ref[9 * a + 3 * b + c, :, pl.ds(start, part)] for start in starts], axis=1)
            for c in range(3)
        ]
        zero = jnp.zeros_like(w[0])
        for line, cells in zip(lines, ((w[1], w[2]), (w[0], w[1]), (zero, w[0]), (w[2], zero))):
            line += cells
    right = jnp.concatenate([jnp.concatenate(line, axis=1) for line in lines], axis=0)
    total = lax.dot_general(left, right, (((1,), (1,)), ((), ())), preferred_element_type=F32)
    return total.reshape(len(windows), m, right.shape[0])


def out_rows(windows, tap_ref, frames, cols, mix_ref, o_ref):
    size = frames * cols
    height = len(windows)
    rows, ow = o_ref.shape[2:]
    now, back, oldest = [out_products(windows, tap_ref, a, -(-(frames - 2 + a) * cols // 16) * 16) for a in (2, 1, 0)]
    for y in range(height):
        full = jnp.concatenate(
            [
                now[y, :cols],
                now[y, cols : 2 * cols] + back[y, :cols],
                now[y, 2 * cols :] + back[y, cols : size - cols] + oldest[y, : size - 2 * cols],
            ],
            axis=0,
        )
        side = full[:, 2 * ow :]
        lane = lax.broadcasted_iota(jnp.int32, side.shape, 1)
        both = full[:, : 2 * ow] + jnp.where(lane < ow, shifted(side, cols, 1), shifted(side, cols, -1))
        mix_ref[y, pl.ds(0, size, stride=2), :] = both
        mix_ref[y, pl.ds(1, size, stride=2), :] = pltpu.roll(both, ow, 1)
    for y in range(height):
        result = mix_ref[y][:, :ow].astype(BF16)
        for t in range(frames):
            o_ref[t, y] = result[rows * t : rows * (t + 1)]


def inner_out_kernel(frames, cols, own_ref, other_ref, gain_ref, tap_ref, o_ref, norm_ref, mix_ref):
    size = frames * cols
    count = own_ref.shape[0] // size * 2
    rows = normalise(size, own_ref, other_ref, gain_ref, [None] * count)
    for k, j in enumerate((0, 1, count - 2, count - 1)):
        norm_ref[k] = rows[j]
    out_rows([rows[y : y + 3] for y in range(count - 2)], tap_ref, frames, cols, mix_ref, o_ref)


def edge_out_kernel(frames, cols, own_ref, other_ref, gain_ref, tap_ref, norm_ref, inner_ref, o_hbm, o_ref, mix_ref, sems):
    size = frames * cols
    inner = inner_ref.shape[1]
    copies = [pltpu.make_async_copy(inner_ref, o_hbm.at[:, pl.ds(2, inner)], sems.at[0])]
    copies[0].start()
    place = lax.axis_index("rows")
    last = lax.axis_size("rows") - 1
    edge = normalise(size, own_ref, other_ref, gain_ref, (place > 0, None, None, place < last))
    top = edge[:2] + [norm_ref[0], norm_ref[1]]
    bottom = [norm_ref[2], norm_ref[3]] + edge[2:]
    windows = [side[y : y + 3] for side in (top, bottom) for y in range(2)]
    out_rows(windows, tap_ref, frames, cols, mix_ref, o_ref)
    for k, start in enumerate((0, inner + 2)):
        copies.append(
            pltpu.make_async_copy(o_ref.at[:, pl.ds(2 * k, 2)], o_hbm.at[:, pl.ds(start, 2)], sems.at[1 + k])
        )
        copies[-1].start()
    for copy in copies:
        copy.wait()


def params(mib):
    return pltpu.CompilerParams(vmem_limit_bytes=mib * MIB)


def cost(mflops):
    return pl.CostEstimate(flops=mflops * 10**6, bytes_accessed=10**7, transcendentals=0)


def vmem():
    return pl.BlockSpec(memory_space=pltpu.VMEM)


def in_space(space, *arrays):
    return tuple(pltpu.with_memory_space_constraint(x, space) for x in arrays)


def call(kernel, name, outs, ins, mib, mflops, scratch=(), in_specs=None, out_specs=None):
    results = pl.pallas_call(
        kernel,
        out_shape=outs,
        in_specs=in_specs or [vmem()] * len(ins),
        out_specs=out_specs or (vmem(),) * len(outs),
        scratch_shapes=list(scratch),
        compiler_params=params(mib),
        cost_estimate=cost(mflops),
        name=name,
    )(*ins)
    return results if out_specs else in_space(pltpu.VMEM, *results)


def body(codes, in_proj, gain_up, up_kernel, gain_res, out_kernel):
    frames, rows, cols = codes.shape
    size = frames * cols
    width, share = up_kernel.shape[1:]
    ow = out_kernel.shape[1]
    height = 2 * rows
    inner = height - 4
    count = lax.axis_size("rows")
    joint = [pair for i in range(count - 1) for pair in ((2 * i + 1, 2 * i + 2), (2 * i + 2, 2 * i + 1))]
    swap = [(0, 1), (1, 0)]
    (mark,) = call(open_kernel, "open", (pltpu.VMEM((8, 128), F32),), (), 1, 1000)
    sent, mark = lax.optimization_barrier((codes, mark))
    (mark,) = in_space(pltpu.VMEM, mark)
    near = lax.ppermute(sent, ("rows", "section"), joint)
    gain_res = gain_res.reshape(1, -1)
    w, tap, proj, gain = in_space(pltpu.VMEM, up_kernel, out_kernel, in_proj, gain_up.reshape(1, -1))
    (codes,) = in_space(pltpu.VMEM, codes)
    hbm = pl.BlockSpec(memory_space=pltpu.HBM)

    (act,) = call(
        latent_kernel,
        "latent",
        (pltpu.VMEM((frames * rows * cols, width), BF16),),
        (codes, proj, gain, mark),
        4,
        1000,
    )
    cut = GROUPS[SPLIT][0]
    (own_first,) = call(
        functools.partial(own_first_kernel, rows * cols),
        "own_first",
        (pltpu.VMEM((rows * size, cut * share), F32),),
        (act, w),
        6,
        1000,
    )

    near, own_first = lax.optimization_barrier((near, own_first))
    far = lax.ppermute(near, "section", swap)
    near, far, own_first = in_space(pltpu.VMEM, near, far, own_first)
    inner_own, edge = call(
        functools.partial(own_rest_kernel, frames, cols),
        "own_rest",
        (pltpu.VMEM(((rows - 1) * size, 4 * share), BF16), pltpu.VMEM((2, size, 6 * share), F32)),
        (act, w, own_first, near),
        8,
        1000,
    )
    inner_other = lax.ppermute(inner_own, "section", swap)
    far, edge = lax.optimization_barrier((far, edge))
    far, edge = in_space(pltpu.VMEM, far, edge)
    (edge_own,) = call(
        halo_kernel,
        "halo",
        (pltpu.VMEM((2 * size, 4 * share), BF16),),
        (near, far, proj, gain, w, edge),
        8,
        20000,
    )
    edge_other = lax.ppermute(edge_own, "section", swap)
    inner_other, edge_other = in_space(pltpu.VMEM, inner_other, edge_other)

    mixed = pltpu.VMEM((max(inner, 4), 2 * size, 2 * ow), F32)
    out_inner, norm = call(
        functools.partial(inner_out_kernel, frames, cols),
        "out_inner",
        (pltpu.VMEM((frames, inner, 2 * cols, ow), BF16), pltpu.VMEM((4, size, 4 * share), BF16)),
        (inner_own, inner_other, gain_res, tap),
        12,
        2000,
        [mixed],
    )
    return call(
        functools.partial(edge_out_kernel, frames, cols),
        "out_edge",
        jax.ShapeDtypeStruct((frames, height, 2 * cols, ow), BF16),
        (edge_own, edge_other, gain_res, tap, norm, out_inner),
        12,
        1000,
        [pltpu.VMEM((frames, 4, 2 * cols, ow), BF16), mixed, pltpu.SemaphoreType.DMA((3,))],
        out_specs=hbm,
    )


def solution(mesh):
    in_specs = (
        P("clip", "rows", None),
        P(),
        P(),
        P(None, None, "section"),
        P(),
        P(None, "section", None),
    )
    out_specs = P("clip", "rows", None, "section")
    return jax.shard_map(body, mesh=mesh, in_specs=in_specs, out_specs=out_specs, check_vma=False)
```

```python
import functools

import jax
import jax.numpy as jnp
from jax import lax
from jax.experimental import pallas as pl
from jax.experimental.pallas import tpu as pltpu
from jax.sharding import PartitionSpec as P

BITS = 18
EPS = 1e-06
F32 = jnp.float32
BF16 = jnp.bfloat16
MIB = 1024 * 1024
GROUPS = ((0, 2), (2, 2), (4, 2), (6, 2), (8, 1))
SPLIT = 3


def silu_of_half(h):
    return h + h * jnp.tanh(h)


def latent_rows(rows, in_proj, gain):
    cols = rows[0].shape[1]
    count = len(rows)
    wide = jnp.concatenate([jnp.broadcast_to(row, (cols, cols)) for row in rows], axis=0)
    sub = lax.broadcasted_iota(jnp.int32, (count, cols, cols), 1).reshape(count * cols, cols)
    lane = lax.broadcasted_iota(jnp.int32, (count * cols, cols), 1)
    picked = jnp.where(sub == lane, wide, 0).astype(F32)
    column = jnp.sum(picked, axis=1, keepdims=True).astype(jnp.int32)
    spread = jnp.broadcast_to(column, (count * cols, BITS))
    shift = lax.broadcasted_iota(jnp.int32, (count * cols, BITS), 1)
    bits = ((jnp.right_shift(spread, shift) & 1) * 2 - 1).astype(F32).astype(BF16)
    latent = jnp.dot(bits, in_proj, preferred_element_type=F32)
    mean = jnp.mean(latent * latent, axis=1, keepdims=True)
    return silu_of_half(latent * lax.rsqrt(mean + EPS) * (0.5 * gain))


def shifted(x, cols, amount):
    rows, lanes = x.shape
    place = lax.broadcasted_iota(jnp.int32, (rows // cols, cols, lanes), 1).reshape(rows, lanes)
    moved = pltpu.roll(x, amount % rows, 0)
    return jnp.where(place == (0 if amount == 1 else cols - 1), 0.0, moved)


def weights(w_ref, a, group):
    return jnp.concatenate([w_ref[9 * a + group[0] + k] for k in range(group[1])], axis=1)


def products(act, n, w_ref, group):
    share = w_ref.shape[2]
    if group[1] == 1:
        both = jnp.concatenate([weights(w_ref, 2, group), weights(w_ref, 1, group)], axis=1)
        now = jnp.dot(act, both, preferred_element_type=F32)
        now, back = now[:, :share], now[: 3 * n, share:]
    else:
        now = jnp.dot(act, weights(w_ref, 2, group), preferred_element_type=F32)
        back = jnp.dot(act[: 3 * n], weights(w_ref, 1, group), preferred_element_type=F32)
    oldest = jnp.dot(act[: 2 * n], weights(w_ref, 0, group), preferred_element_type=F32)
    return jnp.concatenate([now[:n], now[n : 2 * n] + back[:n], now[2 * n :] + back[n:] + oldest], axis=0)


def open_kernel(mark_ref):
    mark_ref[...] = jnp.zeros_like(mark_ref)


def latent_kernel(codes_ref, proj_ref, gain_ref, mark_ref, act_ref):
    frames, rows, cols = codes_ref.shape
    codes = [codes_ref[t, r : r + 1, :] for t in range(frames) for r in range(rows)]
    act_ref[...] = latent_rows(codes, proj_ref[...], gain_ref[...]).astype(BF16)


def lanes_of(group, share, start=0):
    return pl.ds((group[0] - start) * share, group[1] * share)


def own_first_kernel(n, act_ref, w_ref, first_ref):
    for group in GROUPS[:SPLIT]:
        first_ref[:, lanes_of(group, w_ref.shape[2])] = products(act_ref[...], n, w_ref, group)


def of_row(part, frames, stride, start, cols):
    return jnp.concatenate([part[t * stride + start : t * stride + start + cols] for t in range(frames)], axis=0)


def put_hidden(upper, lower, cols, share, q, h_ref):
    size = upper(0).shape[0]
    sums = [[], []]
    for c in range(3):
        x = upper(c) + lower(6 + c)
        sums[0].append(x + upper(3 + c))
        sums[1].append(x + lower(3 + c))
    out = pl.ds(q * size, size)
    for py, (left, mid, right) in enumerate(sums):
        even = shifted(left, cols, 1) + (mid + right)
        odd = (left + mid) + shifted(right, cols, -1)
        h_ref[out, pl.ds(2 * py * share, share)] = even.astype(BF16)
        h_ref[out, pl.ds((2 * py + 1) * share, share)] = odd.astype(BF16)


def own_rest_kernel(frames, cols, act_ref, w_ref, first_ref, after_ref, h_ref, edge_ref):
    share = w_ref.shape[2]
    n = act_ref.shape[0] // frames
    rows = n // cols
    act = act_ref[...]
    done = [first_ref[...]] + [products(act, n, w_ref, group) for group in GROUPS[SPLIT:]]
    taken = []
    for part in done:
        taken += [part[:, k * share : (k + 1) * share] for k in range(part.shape[1] // share)]

    def row(r):
        return lambda tap: of_row(taken[tap], frames, n, r * cols, cols)

    for q in range(rows - 1):
        put_hidden(row(q), row(q + 1), cols, share, q, h_ref)
    for k in range(6):
        edge_ref[0, :, pl.ds(k * share, share)] = row(0)(3 + k)
        edge_ref[1, :, pl.ds(k * share, share)] = row(rows - 1)(k)


def halo_kernel(near_ref, far_ref, proj_ref, gain_ref, w_ref, edge_ref, h_ref):
    frames, rows, cols = near_ref.shape
    share = w_ref.shape[2]
    first = lax.axis_index("section") == 0
    place = lax.axis_index("rows")
    last = lax.axis_size("rows") - 1
    codes = []
    for t in range(frames):
        low = [ref[t, rows - 1 : rows, :] for ref in (near_ref, far_ref)]
        high = [ref[t, 0:1, :] for ref in (near_ref, far_ref)]
        codes += [jnp.where(first, low[0], low[1]), jnp.where(first, high[1], high[0])]
    act = latent_rows(codes, proj_ref[...], gain_ref[...])
    side = lax.broadcasted_iota(jnp.int32, (frames, 2, cols, act.shape[1]), 1).reshape(act.shape)
    keep = jnp.where(side == 0, (place > 0).astype(F32), (place < last).astype(F32))
    act = (act * keep).astype(BF16)
    halo = jnp.concatenate([products(act, 2 * cols, w_ref, group) for group in GROUPS], axis=1)

    def outer(e):
        return lambda tap: of_row(halo[:, tap * share : (tap + 1) * share], frames, 2 * cols, e * cols, cols)

    put_hidden(outer(0), lambda tap: edge_ref[0, :, pl.ds((tap - 3) * share, share)], cols, share, 0, h_ref)
    put_hidden(lambda tap: edge_ref[1, :, pl.ds(tap * share, share)], outer(1), cols, share, 1, h_ref)


def part_starts(part):
    section = lax.axis_index("section")
    return [pl.multiple_of(k * part, part) for k in (section, 1 - section)]


def normalise(size, own_ref, other_ref, gain_ref, keeps):
    part = own_ref.shape[1] // 4
    gains = [0.5 * gain_ref[:, pl.ds(start, part)] for start in part_starts(part)]
    rows = []
    for j, keep in enumerate(keeps):
        cells = []
        for px in range(2):
            lanes = pl.ds((2 * (j % 2) + px) * part, part)
            x = [ref[pl.ds(j // 2 * size, size), lanes].astype(F32) for ref in (own_ref, other_ref)]
            mean = jnp.sum(x[0] * x[0] + x[1] * x[1], axis=1, keepdims=True) / (2 * part)
            scale = lax.rsqrt(mean + EPS)
            if keep is not None:
                scale = jnp.where(keep, scale, 0.0)
            cells += [silu_of_half(x[s] * scale * gains[s]).astype(BF16) for s in range(2)]
        rows.append(jnp.concatenate(cells, axis=1))
    return rows


def out_products(windows, tap_ref, a, m):
    left = jnp.concatenate([jnp.concatenate([row[:m] for row in window], axis=1) for window in windows], axis=0)
    part = tap_ref.shape[2] // 2
    starts = part_starts(part)
    lines = [[], [], [], []]
    for b in range(3):
        w = [
            jnp.concatenate([tap_ref[9 * a + 3 * b + c, :, pl.ds(start, part)] for start in starts], axis=1)
            for c in range(3)
        ]
        zero = jnp.zeros_like(w[0])
        for line, cells in zip(lines, ((w[1], w[2]), (w[0], w[1]), (zero, w[0]), (w[2], zero))):
            line += cells
    right = jnp.concatenate([jnp.concatenate(line, axis=1) for line in lines], axis=0)
    total = lax.dot_general(left, right, (((1,), (1,)), ((), ())), preferred_element_type=F32)
    return total.reshape(len(windows), m, right.shape[0])


def out_rows(windows, tap_ref, frames, cols, mix_ref, o_ref):
    size = frames * cols
    height = len(windows)
    rows, ow = o_ref.shape[2:]
    now, back, oldest = [out_products(windows, tap_ref, a, -(-(frames - 2 + a) * cols // 16) * 16) for a in (2, 1, 0)]
    for y in range(height):
        full = jnp.concatenate(
            [
                now[y, :cols],
                now[y, cols : 2 * cols] + back[y, :cols],
                now[y, 2 * cols :] + back[y, cols : size - cols] + oldest[y, : size - 2 * cols],
            ],
            axis=0,
        )
        side = full[:, 2 * ow :]
        lane = lax.broadcasted_iota(jnp.int32, side.shape, 1)
        both = full[:, : 2 * ow] + jnp.where(lane < ow, shifted(side, cols, 1), shifted(side, cols, -1))
        mix_ref[y, pl.ds(0, size, stride=2), :] = both
        mix_ref[y, pl.ds(1, size, stride=2), :] = pltpu.roll(both, ow, 1)
    for y in range(height):
        result = mix_ref[y][:, :ow].astype(BF16)
        for t in range(frames):
            o_ref[t, y] = result[rows * t : rows * (t + 1)]


def inner_out_kernel(frames, cols, own_ref, other_ref, gain_ref, tap_ref, o_ref, norm_ref, mix_ref):
    size = frames * cols
    count = own_ref.shape[0] // size * 2
    rows = normalise(size, own_ref, other_ref, gain_ref, [None] * count)
    for k, j in enumerate((0, 1, count - 2, count - 1)):
        norm_ref[k] = rows[j]
    out_rows([rows[y : y + 3] for y in range(count - 2)], tap_ref, frames, cols, mix_ref, o_ref)


def edge_out_kernel(frames, cols, own_ref, other_ref, gain_ref, tap_ref, norm_ref, inner_ref, o_hbm, o_ref, mix_ref, sems):
    size = frames * cols
    inner = inner_ref.shape[1]
    copies = [pltpu.make_async_copy(inner_ref, o_hbm.at[:, pl.ds(2, inner)], sems.at[0])]
    copies[0].start()
    place = lax.axis_index("rows")
    last = lax.axis_size("rows") - 1
    edge = normalise(size, own_ref, other_ref, gain_ref, (place > 0, None, None, place < last))
    top = edge[:2] + [norm_ref[0], norm_ref[1]]
    bottom = [norm_ref[2], norm_ref[3]] + edge[2:]
    windows = [side[y : y + 3] for side in (top, bottom) for y in range(2)]
    out_rows(windows, tap_ref, frames, cols, mix_ref, o_ref)
    for k, start in enumerate((0, inner + 2)):
        copies.append(
            pltpu.make_async_copy(o_ref.at[:, pl.ds(2 * k, 2)], o_hbm.at[:, pl.ds(start, 2)], sems.at[1 + k])
        )
        copies[-1].start()
    for copy in copies:
        copy.wait()


def params(mib):
    return pltpu.CompilerParams(vmem_limit_bytes=mib * MIB)


def cost(mflops):
    return pl.CostEstimate(flops=mflops * 10**6, bytes_accessed=10**7, transcendentals=0)


def vmem():
    return pl.BlockSpec(memory_space=pltpu.VMEM)


def in_space(space, *arrays):
    return tuple(pltpu.with_memory_space_constraint(x, space) for x in arrays)


def call(kernel, name, outs, ins, mib, mflops, scratch=(), in_specs=None, out_specs=None):
    results = pl.pallas_call(
        kernel,
        out_shape=outs,
        in_specs=in_specs or [vmem()] * len(ins),
        out_specs=out_specs or (vmem(),) * len(outs),
        scratch_shapes=list(scratch),
        compiler_params=params(mib),
        cost_estimate=cost(mflops),
        name=name,
    )(*ins)
    return results if out_specs else in_space(pltpu.VMEM, *results)


def body(codes, in_proj, gain_up, up_kernel, gain_res, out_kernel):
    frames, rows, cols = codes.shape
    size = frames * cols
    width, share = up_kernel.shape[1:]
    ow = out_kernel.shape[1]
    height = 2 * rows
    inner = height - 4
    count = lax.axis_size("rows")
    joint = [pair for i in range(count - 1) for pair in ((2 * i + 1, 2 * i + 2), (2 * i + 2, 2 * i + 1))]
    swap = [(0, 1), (1, 0)]
    (mark,) = call(open_kernel, "open", (pltpu.VMEM((8, 128), F32),), (), 1, 1000)
    near = lax.ppermute(codes, ("rows", "section"), joint)
    gain_res = gain_res.reshape(1, -1)
    w, tap, proj, gain = in_space(pltpu.VMEM, up_kernel, out_kernel, in_proj, gain_up.reshape(1, -1))
    (codes,) = in_space(pltpu.VMEM, codes)
    hbm = pl.BlockSpec(memory_space=pltpu.HBM)

    (act,) = call(
        latent_kernel,
        "latent",
        (pltpu.VMEM((frames * rows * cols, width), BF16),),
        (codes, proj, gain, mark),
        4,
        1000,
    )
    cut = GROUPS[SPLIT][0]
    (own_first,) = call(
        functools.partial(own_first_kernel, rows * cols),
        "own_first",
        (pltpu.VMEM((rows * size, cut * share), F32),),
        (act, w),
        6,
        1000,
    )

    near, own_first = lax.optimization_barrier((near, own_first))
    far = lax.ppermute(near, "section", swap)
    near, far, own_first = in_space(pltpu.VMEM, near, far, own_first)
    inner_own, edge = call(
        functools.partial(own_rest_kernel, frames, cols),
        "own_rest",
        (pltpu.VMEM(((rows - 1) * size, 4 * share), BF16), pltpu.VMEM((2, size, 6 * share), F32)),
        (act, w, own_first, near),
        8,
        1000,
    )
    inner_other = lax.ppermute(inner_own, "section", swap)
    far, edge = lax.optimization_barrier((far, edge))
    far, edge = in_space(pltpu.VMEM, far, edge)
    (edge_own,) = call(
        halo_kernel,
        "halo",
        (pltpu.VMEM((2 * size, 4 * share), BF16),),
        (near, far, proj, gain, w, edge),
        8,
        20000,
    )
    edge_other = lax.ppermute(edge_own, "section", swap)
    inner_other, edge_other = in_space(pltpu.VMEM, inner_other, edge_other)

    mixed = pltpu.VMEM((max(inner, 4), 2 * size, 2 * ow), F32)
    out_inner, norm = call(
        functools.partial(inner_out_kernel, frames, cols),
        "out_inner",
        (pltpu.VMEM((frames, inner, 2 * cols, ow), BF16), pltpu.VMEM((4, size, 4 * share), BF16)),
        (inner_own, inner_other, gain_res, tap),
        12,
        2000,
        [mixed],
    )
    return call(
        functools.partial(edge_out_kernel, frames, cols),
        "out_edge",
        jax.ShapeDtypeStruct((frames, height, 2 * cols, ow), BF16),
        (edge_own, edge_other, gain_res, tap, norm, out_inner),
        12,
        1000,
        [pltpu.VMEM((frames, 4, 2 * cols, ow), BF16), mixed, pltpu.SemaphoreType.DMA((3,))],
        out_specs=hbm,
    )


def solution(mesh):
    in_specs = (
        P("clip", "rows", None),
        P(),
        P(),
        P(None, None, "section"),
        P(),
        P(None, "section", None),
    )
    out_specs = P("clip", "rows", None, "section")
    return jax.shard_map(body, mesh=mesh, in_specs=in_specs, out_specs=out_specs, check_vma=False)
```

```python
import functools

import jax
import jax.numpy as jnp
from jax import lax
from jax.experimental import pallas as pl
from jax.experimental.pallas import tpu as pltpu
from jax.sharding import PartitionSpec as P

BITS = 18
EPS = 1e-06
F32 = jnp.float32
BF16 = jnp.bfloat16
MIB = 1024 * 1024
GROUPS = ((0, 2), (2, 2), (4, 2), (6, 2), (8, 1))
SPLIT = 4


def silu_of_half(h):
    return h + h * jnp.tanh(h)


def latent_rows(rows, in_proj, gain):
    cols = rows[0].shape[1]
    count = len(rows)
    wide = jnp.concatenate([jnp.broadcast_to(row, (cols, cols)) for row in rows], axis=0)
    sub = lax.broadcasted_iota(jnp.int32, (count, cols, cols), 1).reshape(count * cols, cols)
    lane = lax.broadcasted_iota(jnp.int32, (count * cols, cols), 1)
    picked = jnp.where(sub == lane, wide, 0).astype(F32)
    column = jnp.sum(picked, axis=1, keepdims=True).astype(jnp.int32)
    spread = jnp.broadcast_to(column, (count * cols, BITS))
    shift = lax.broadcasted_iota(jnp.int32, (count * cols, BITS), 1)
    bits = ((jnp.right_shift(spread, shift) & 1) * 2 - 1).astype(F32).astype(BF16)
    latent = jnp.dot(bits, in_proj, preferred_element_type=F32)
    mean = jnp.mean(latent * latent, axis=1, keepdims=True)
    return silu_of_half(latent * lax.rsqrt(mean + EPS) * (0.5 * gain))


def shifted(x, cols, amount):
    rows, lanes = x.shape
    place = lax.broadcasted_iota(jnp.int32, (rows // cols, cols, lanes), 1).reshape(rows, lanes)
    moved = pltpu.roll(x, amount % rows, 0)
    return jnp.where(place == (0 if amount == 1 else cols - 1), 0.0, moved)


def weights(w_ref, a, group):
    return jnp.concatenate([w_ref[9 * a + group[0] + k] for k in range(group[1])], axis=1)


def products(act, n, w_ref, group):
    share = w_ref.shape[2]
    if group[1] == 1:
        both = jnp.concatenate([weights(w_ref, 2, group), weights(w_ref, 1, group)], axis=1)
        now = jnp.dot(act, both, preferred_element_type=F32)
        now, back = now[:, :share], now[: 3 * n, share:]
    else:
        now = jnp.dot(act, weights(w_ref, 2, group), preferred_element_type=F32)
        back = jnp.dot(act[: 3 * n], weights(w_ref, 1, group), preferred_element_type=F32)
    oldest = jnp.dot(act[: 2 * n], weights(w_ref, 0, group), preferred_element_type=F32)
    return jnp.concatenate([now[:n], now[n : 2 * n] + back[:n], now[2 * n :] + back[n:] + oldest], axis=0)


def open_kernel(mark_ref):
    mark_ref[...] = jnp.zeros_like(mark_ref)


def latent_kernel(codes_ref, proj_ref, gain_ref, mark_ref, act_ref):
    frames, rows, cols = codes_ref.shape
    codes = [codes_ref[t, r : r + 1, :] for t in range(frames) for r in range(rows)]
    act_ref[...] = latent_rows(codes, proj_ref[...], gain_ref[...]).astype(BF16)


def lanes_of(group, share, start=0):
    return pl.ds((group[0] - start) * share, group[1] * share)


def own_first_kernel(n, act_ref, w_ref, first_ref):
    for group in GROUPS[:SPLIT]:
        first_ref[:, lanes_of(group, w_ref.shape[2])] = products(act_ref[...], n, w_ref, group)


def of_row(part, frames, stride, start, cols):
    return jnp.concatenate([part[t * stride + start : t * stride + start + cols] for t in range(frames)], axis=0)


def put_hidden(upper, lower, cols, share, q, h_ref):
    size = upper(0).shape[0]
    sums = [[], []]
    for c in range(3):
        x = upper(c) + lower(6 + c)
        sums[0].append(x + upper(3 + c))
        sums[1].append(x + lower(3 + c))
    out = pl.ds(q * size, size)
    for py, (left, mid, right) in enumerate(sums):
        even = shifted(left, cols, 1) + (mid + right)
        odd = (left + mid) + shifted(right, cols, -1)
        h_ref[out, pl.ds(2 * py * share, share)] = even.astype(BF16)
        h_ref[out, pl.ds((2 * py + 1) * share, share)] = odd.astype(BF16)


def own_rest_kernel(frames, cols, act_ref, w_ref, first_ref, after_ref, h_ref, edge_ref):
    share = w_ref.shape[2]
    n = act_ref.shape[0] // frames
    rows = n // cols
    act = act_ref[...]
    done = [first_ref[...]] + [products(act, n, w_ref, group) for group in GROUPS[SPLIT:]]
    taken = []
    for part in done:
        taken += [part[:, k * share : (k + 1) * share] for k in range(part.shape[1] // share)]

    def row(r):
        return lambda tap: of_row(taken[tap], frames, n, r * cols, cols)

    for q in range(rows - 1):
        put_hidden(row(q), row(q + 1), cols, share, q, h_ref)
    for k in range(6):
        edge_ref[0, :, pl.ds(k * share, share)] = row(0)(3 + k)
        edge_ref[1, :, pl.ds(k * share, share)] = row(rows - 1)(k)


def halo_kernel(near_ref, far_ref, proj_ref, gain_ref, w_ref, edge_ref, h_ref):
    frames, rows, cols = near_ref.shape
    share = w_ref.shape[2]
    first = lax.axis_index("section") == 0
    place = lax.axis_index("rows")
    last = lax.axis_size("rows") - 1
    codes = []
    for t in range(frames):
        low = [ref[t, rows - 1 : rows, :] for ref in (near_ref, far_ref)]
        high = [ref[t, 0:1, :] for ref in (near_ref, far_ref)]
        codes += [jnp.where(first, low[0], low[1]), jnp.where(first, high[1], high[0])]
    act = latent_rows(codes, proj_ref[...], gain_ref[...])
    side = lax.broadcasted_iota(jnp.int32, (frames, 2, cols, act.shape[1]), 1).reshape(act.shape)
    keep = jnp.where(side == 0, (place > 0).astype(F32), (place < last).astype(F32))
    act = (act * keep).astype(BF16)
    halo = jnp.concatenate([products(act, 2 * cols, w_ref, group) for group in GROUPS], axis=1)

    def outer(e):
        return lambda tap: of_row(halo[:, tap * share : (tap + 1) * share], frames, 2 * cols, e * cols, cols)

    put_hidden(outer(0), lambda tap: edge_ref[0, :, pl.ds((tap - 3) * share, share)], cols, share, 0, h_ref)
    put_hidden(lambda tap: edge_ref[1, :, pl.ds(tap * share, share)], outer(1), cols, share, 1, h_ref)


def part_starts(part):
    section = lax.axis_index("section")
    return [pl.multiple_of(k * part, part) for k in (section, 1 - section)]


def normalise(size, own_ref, other_ref, gain_ref, keeps):
    part = own_ref.shape[1] // 4
    gains = [0.5 * gain_ref[:, pl.ds(start, part)] for start in part_starts(part)]
    rows = []
    for j, keep in enumerate(keeps):
        cells = []
        for px in range(2):
            lanes = pl.ds((2 * (j % 2) + px) * part, part)
            x = [ref[pl.ds(j // 2 * size, size), lanes].astype(F32) for ref in (own_ref, other_ref)]
            mean = jnp.sum(x[0] * x[0] + x[1] * x[1], axis=1, keepdims=True) / (2 * part)
            scale = lax.rsqrt(mean + EPS)
            if keep is not None:
                scale = jnp.where(keep, scale, 0.0)
            cells += [silu_of_half(x[s] * scale * gains[s]).astype(BF16) for s in range(2)]
        rows.append(jnp.concatenate(cells, axis=1))
    return rows


def out_products(windows, tap_ref, a, m):
    left = jnp.concatenate([jnp.concatenate([row[:m] for row in window], axis=1) for window in windows], axis=0)
    part = tap_ref.shape[2] // 2
    starts = part_starts(part)
    lines = [[], [], [], []]
    for b in range(3):
        w = [
            jnp.concatenate([tap_ref[9 * a + 3 * b + c, :, pl.ds(start, part)] for start in starts], axis=1)
            for c in range(3)
        ]
        zero = jnp.zeros_like(w[0])
        for line, cells in zip(lines, ((w[1], w[2]), (w[0], w[1]), (zero, w[0]), (w[2], zero))):
            line += cells
    right = jnp.concatenate([jnp.concatenate(line, axis=1) for line in lines], axis=0)
    total = lax.dot_general(left, right, (((1,), (1,)), ((), ())), preferred_element_type=F32)
    return total.reshape(len(windows), m, right.shape[0])


def out_rows(windows, tap_ref, frames, cols, mix_ref, o_ref):
    size = frames * cols
    height = len(windows)
    rows, ow = o_ref.shape[2:]
    now, back, oldest = [out_products(windows, tap_ref, a, -(-(frames - 2 + a) * cols // 16) * 16) for a in (2, 1, 0)]
    for y in range(height):
        full = jnp.concatenate(
            [
                now[y, :cols],
                now[y, cols : 2 * cols] + back[y, :cols],
                now[y, 2 * cols :] + back[y, cols : size - cols] + oldest[y, : size - 2 * cols],
            ],
            axis=0,
        )
        side = full[:, 2 * ow :]
        lane = lax.broadcasted_iota(jnp.int32, side.shape, 1)
        both = full[:, : 2 * ow] + jnp.where(lane < ow, shifted(side, cols, 1), shifted(side, cols, -1))
        mix_ref[y, pl.ds(0, size, stride=2), :] = both
        mix_ref[y, pl.ds(1, size, stride=2), :] = pltpu.roll(both, ow, 1)
    for y in range(height):
        result = mix_ref[y][:, :ow].astype(BF16)
        for t in range(frames):
            o_ref[t, y] = result[rows * t : rows * (t + 1)]


def inner_out_kernel(frames, cols, own_ref, other_ref, gain_ref, tap_ref, o_ref, norm_ref, mix_ref):
    size = frames * cols
    count = own_ref.shape[0] // size * 2
    rows = normalise(size, own_ref, other_ref, gain_ref, [None] * count)
    for k, j in enumerate((0, 1, count - 2, count - 1)):
        norm_ref[k] = rows[j]
    out_rows([rows[y : y + 3] for y in range(count - 2)], tap_ref, frames, cols, mix_ref, o_ref)


def edge_out_kernel(frames, cols, own_ref, other_ref, gain_ref, tap_ref, norm_ref, inner_ref, o_hbm, o_ref, mix_ref, sems):
    size = frames * cols
    inner = inner_ref.shape[1]
    copies = [pltpu.make_async_copy(inner_ref, o_hbm.at[:, pl.ds(2, inner)], sems.at[0])]
    copies[0].start()
    place = lax.axis_index("rows")
    last = lax.axis_size("rows") - 1
    edge = normalise(size, own_ref, other_ref, gain_ref, (place > 0, None, None, place < last))
    top = edge[:2] + [norm_ref[0], norm_ref[1]]
    bottom = [norm_ref[2], norm_ref[3]] + edge[2:]
    windows = [side[y : y + 3] for side in (top, bottom) for y in range(2)]
    out_rows(windows, tap_ref, frames, cols, mix_ref, o_ref)
    for k, start in enumerate((0, inner + 2)):
        copies.append(
            pltpu.make_async_copy(o_ref.at[:, pl.ds(2 * k, 2)], o_hbm.at[:, pl.ds(start, 2)], sems.at[1 + k])
        )
        copies[-1].start()
    for copy in copies:
        copy.wait()


def params(mib):
    return pltpu.CompilerParams(vmem_limit_bytes=mib * MIB)


def cost(mflops):
    return pl.CostEstimate(flops=mflops * 10**6, bytes_accessed=10**7, transcendentals=0)


def vmem():
    return pl.BlockSpec(memory_space=pltpu.VMEM)


def in_space(space, *arrays):
    return tuple(pltpu.with_memory_space_constraint(x, space) for x in arrays)


def call(kernel, name, outs, ins, mib, mflops, scratch=(), in_specs=None, out_specs=None):
    results = pl.pallas_call(
        kernel,
        out_shape=outs,
        in_specs=in_specs or [vmem()] * len(ins),
        out_specs=out_specs or (vmem(),) * len(outs),
        scratch_shapes=list(scratch),
        compiler_params=params(mib),
        cost_estimate=cost(mflops),
        name=name,
    )(*ins)
    return results if out_specs else in_space(pltpu.VMEM, *results)


def body(codes, in_proj, gain_up, up_kernel, gain_res, out_kernel):
    frames, rows, cols = codes.shape
    size = frames * cols
    width, share = up_kernel.shape[1:]
    ow = out_kernel.shape[1]
    height = 2 * rows
    inner = height - 4
    count = lax.axis_size("rows")
    joint = [pair for i in range(count - 1) for pair in ((2 * i + 1, 2 * i + 2), (2 * i + 2, 2 * i + 1))]
    swap = [(0, 1), (1, 0)]
    (mark,) = call(open_kernel, "open", (pltpu.VMEM((8, 128), F32),), (), 1, 1000)
    near = lax.ppermute(codes, ("rows", "section"), joint)
    gain_res = gain_res.reshape(1, -1)
    w, tap, proj, gain = in_space(pltpu.VMEM, up_kernel, out_kernel, in_proj, gain_up.reshape(1, -1))
    (codes,) = in_space(pltpu.VMEM, codes)
    hbm = pl.BlockSpec(memory_space=pltpu.HBM)

    (act,) = call(
        latent_kernel,
        "latent",
        (pltpu.VMEM((frames * rows * cols, width), BF16),),
        (codes, proj, gain, mark),
        4,
        1000,
    )
    cut = GROUPS[SPLIT][0]
    (own_first,) = call(
        functools.partial(own_first_kernel, rows * cols),
        "own_first",
        (pltpu.VMEM((rows * size, cut * share), F32),),
        (act, w),
        6,
        1000,
    )

    near, own_first = lax.optimization_barrier((near, own_first))
    far = lax.ppermute(near, "section", swap)
    near, far, own_first = in_space(pltpu.VMEM, near, far, own_first)
    inner_own, edge = call(
        functools.partial(own_rest_kernel, frames, cols),
        "own_rest",
        (pltpu.VMEM(((rows - 1) * size, 4 * share), BF16), pltpu.VMEM((2, size, 6 * share), F32)),
        (act, w, own_first, near),
        8,
        1000,
    )
    inner_other = lax.ppermute(inner_own, "section", swap)
    far, edge = lax.optimization_barrier((far, edge))
    far, edge = in_space(pltpu.VMEM, far, edge)
    (edge_own,) = call(
        halo_kernel,
        "halo",
        (pltpu.VMEM((2 * size, 4 * share), BF16),),
        (near, far, proj, gain, w, edge),
        8,
        20000,
    )
    edge_other = lax.ppermute(edge_own, "section", swap)
    inner_other, edge_other = in_space(pltpu.VMEM, inner_other, edge_other)

    mixed = pltpu.VMEM((max(inner, 4), 2 * size, 2 * ow), F32)
    out_inner, norm = call(
        functools.partial(inner_out_kernel, frames, cols),
        "out_inner",
        (pltpu.VMEM((frames, inner, 2 * cols, ow), BF16), pltpu.VMEM((4, size, 4 * share), BF16)),
        (inner_own, inner_other, gain_res, tap),
        12,
        2000,
        [mixed],
    )
    return call(
        functools.partial(edge_out_kernel, frames, cols),
        "out_edge",
        jax.ShapeDtypeStruct((frames, height, 2 * cols, ow), BF16),
        (edge_own, edge_other, gain_res, tap, norm, out_inner),
        12,
        1000,
        [pltpu.VMEM((frames, 4, 2 * cols, ow), BF16), mixed, pltpu.SemaphoreType.DMA((3,))],
        out_specs=hbm,
    )


def solution(mesh):
    in_specs = (
        P("clip", "rows", None),
        P(),
        P(),
        P(None, None, "section"),
        P(),
        P(None, "section", None),
    )
    out_specs = P("clip", "rows", None, "section")
    return jax.shard_map(body, mesh=mesh, in_specs=in_specs, out_specs=out_specs, check_vma=False)
```

```python
import functools

import jax
import jax.numpy as jnp
from jax import lax
from jax.experimental import pallas as pl
from jax.experimental.pallas import tpu as pltpu
from jax.sharding import PartitionSpec as P

BITS = 18
EPS = 1e-06
F32 = jnp.float32
BF16 = jnp.bfloat16
MIB = 1024 * 1024
GROUPS = ((0, 2), (2, 2), (4, 2), (6, 2), (8, 1))
SPLIT = 4


def silu_of_half(h):
    return h + h * jnp.tanh(h)


def latent_rows(rows, in_proj, gain):
    cols = rows[0].shape[1]
    count = len(rows)
    wide = jnp.concatenate([jnp.broadcast_to(row, (cols, cols)) for row in rows], axis=0)
    sub = lax.broadcasted_iota(jnp.int32, (count, cols, cols), 1).reshape(count * cols, cols)
    lane = lax.broadcasted_iota(jnp.int32, (count * cols, cols), 1)
    picked = jnp.where(sub == lane, wide, 0).astype(F32)
    column = jnp.sum(picked, axis=1, keepdims=True).astype(jnp.int32)
    spread = jnp.broadcast_to(column, (count * cols, BITS))
    shift = lax.broadcasted_iota(jnp.int32, (count * cols, BITS), 1)
    bits = ((jnp.right_shift(spread, shift) & 1) * 2 - 1).astype(F32).astype(BF16)
    latent = jnp.dot(bits, in_proj, preferred_element_type=F32)
    mean = jnp.mean(latent * latent, axis=1, keepdims=True)
    return silu_of_half(latent * lax.rsqrt(mean + EPS) * (0.5 * gain))


def shifted(x, cols, amount):
    rows, lanes = x.shape
    place = lax.broadcasted_iota(jnp.int32, (rows // cols, cols, lanes), 1).reshape(rows, lanes)
    moved = pltpu.roll(x, amount % rows, 0)
    return jnp.where(place == (0 if amount == 1 else cols - 1), 0.0, moved)


def weights(w_ref, a, group):
    return jnp.concatenate([w_ref[9 * a + group[0] + k] for k in range(group[1])], axis=1)


def products(act, n, w_ref, group):
    share = w_ref.shape[2]
    if group[1] == 1:
        both = jnp.concatenate([weights(w_ref, 2, group), weights(w_ref, 1, group)], axis=1)
        now = jnp.dot(act, both, preferred_element_type=F32)
        now, back = now[:, :share], now[: 3 * n, share:]
    else:
        now = jnp.dot(act, weights(w_ref, 2, group), preferred_element_type=F32)
        back = jnp.dot(act[: 3 * n], weights(w_ref, 1, group), preferred_element_type=F32)
    oldest = jnp.dot(act[: 2 * n], weights(w_ref, 0, group), preferred_element_type=F32)
    return jnp.concatenate([now[:n], now[n : 2 * n] + back[:n], now[2 * n :] + back[n:] + oldest], axis=0)


def open_kernel(mark_ref):
    mark_ref[...] = jnp.zeros_like(mark_ref)


def latent_kernel(codes_ref, proj_ref, gain_ref, mark_ref, act_ref):
    frames, rows, cols = codes_ref.shape
    codes = [codes_ref[t, r : r + 1, :] for t in range(frames) for r in range(rows)]
    act_ref[...] = latent_rows(codes, proj_ref[...], gain_ref[...]).astype(BF16)


def lanes_of(group, share, start=0):
    return pl.ds((group[0] - start) * share, group[1] * share)


def own_first_kernel(n, act_ref, w_ref, first_ref):
    for group in GROUPS[:SPLIT]:
        first_ref[:, lanes_of(group, w_ref.shape[2])] = products(act_ref[...], n, w_ref, group)


def of_row(part, frames, stride, start, cols):
    return jnp.concatenate([part[t * stride + start : t * stride + start + cols] for t in range(frames)], axis=0)


def put_hidden(upper, lower, cols, share, q, h_ref):
    size = upper(0).shape[0]
    sums = [[], []]
    for c in range(3):
        x = upper(c) + lower(6 + c)
        sums[0].append(x + upper(3 + c))
        sums[1].append(x + lower(3 + c))
    out = pl.ds(q * size, size)
    for py, (left, mid, right) in enumerate(sums):
        even = shifted(left, cols, 1) + (mid + right)
        odd = (left + mid) + shifted(right, cols, -1)
        h_ref[out, pl.ds(2 * py * share, share)] = even.astype(BF16)
        h_ref[out, pl.ds((2 * py + 1) * share, share)] = odd.astype(BF16)


def own_rest_kernel(frames, cols, act_ref, w_ref, first_ref, after_ref, h_ref, edge_ref):
    share = w_ref.shape[2]
    n = act_ref.shape[0] // frames
    rows = n // cols
    act = act_ref[...]
    done = [first_ref[...]] + [products(act, n, w_ref, group) for group in GROUPS[SPLIT:]]
    taken = []
    for part in done:
        taken += [part[:, k * share : (k + 1) * share] for k in range(part.shape[1] // share)]

    def row(r):
        return lambda tap: of_row(taken[tap], frames, n, r * cols, cols)

    for q in range(rows - 1):
        put_hidden(row(q), row(q + 1), cols, share, q, h_ref)
    for k in range(6):
        edge_ref[0, :, pl.ds(k * share, share)] = row(0)(3 + k)
        edge_ref[1, :, pl.ds(k * share, share)] = row(rows - 1)(k)


def halo_kernel(near_ref, far_ref, proj_ref, gain_ref, w_ref, edge_ref, h_ref):
    frames, rows, cols = near_ref.shape
    share = w_ref.shape[2]
    first = lax.axis_index("section") == 1
    place = lax.axis_index("rows")
    last = lax.axis_size("rows") - 1
    codes = []
    for t in range(frames):
        low = [ref[t, rows - 1 : rows, :] for ref in (near_ref, far_ref)]
        high = [ref[t, 0:1, :] for ref in (near_ref, far_ref)]
        codes += [jnp.where(first, low[0], low[1]), jnp.where(first, high[1], high[0])]
    act = latent_rows(codes, proj_ref[...], gain_ref[...])
    side = lax.broadcasted_iota(jnp.int32, (frames, 2, cols, act.shape[1]), 1).reshape(act.shape)
    keep = jnp.where(side == 0, (place > 0).astype(F32), (place < last).astype(F32))
    act = (act * keep).astype(BF16)
    halo = jnp.concatenate([products(act, 2 * cols, w_ref, group) for group in GROUPS], axis=1)

    def outer(e):
        return lambda tap: of_row(halo[:, tap * share : (tap + 1) * share], frames, 2 * cols, e * cols, cols)

    put_hidden(outer(0), lambda tap: edge_ref[0, :, pl.ds((tap - 3) * share, share)], cols, share, 0, h_ref)
    put_hidden(lambda tap: edge_ref[1, :, pl.ds(tap * share, share)], outer(1), cols, share, 1, h_ref)


def part_starts(part):
    section = lax.axis_index("section")
    return [pl.multiple_of(k * part, part) for k in (section, 1 - section)]


def normalise(size, own_ref, other_ref, gain_ref, keeps):
    part = own_ref.shape[1] // 4
    gains = [0.5 * gain_ref[:, pl.ds(start, part)] for start in part_starts(part)]
    rows = []
    for j, keep in enumerate(keeps):
        cells = []
        for px in range(2):
            lanes = pl.ds((2 * (j % 2) + px) * part, part)
            x = [ref[pl.ds(j // 2 * size, size), lanes].astype(F32) for ref in (own_ref, other_ref)]
            mean = jnp.sum(x[0] * x[0] + x[1] * x[1], axis=1, keepdims=True) / (2 * part)
            scale = lax.rsqrt(mean + EPS)
            if keep is not None:
                scale = jnp.where(keep, scale, 0.0)
            cells += [silu_of_half(x[s] * scale * gains[s]).astype(BF16) for s in range(2)]
        rows.append(jnp.concatenate(cells, axis=1))
    return rows


def out_products(windows, tap_ref, a, m):
    left = jnp.concatenate([jnp.concatenate([row[:m] for row in window], axis=1) for window in windows], axis=0)
    part = tap_ref.shape[2] // 2
    starts = part_starts(part)
    lines = [[], [], [], []]
    for b in range(3):
        w = [
            jnp.concatenate([tap_ref[9 * a + 3 * b + c, :, pl.ds(start, part)] for start in starts], axis=1)
            for c in range(3)
        ]
        zero = jnp.zeros_like(w[0])
        for line, cells in zip(lines, ((w[1], w[2]), (w[0], w[1]), (zero, w[0]), (w[2], zero))):
            line += cells
    right = jnp.concatenate([jnp.concatenate(line, axis=1) for line in lines], axis=0)
    total = lax.dot_general(left, right, (((1,), (1,)), ((), ())), preferred_element_type=F32)
    return total.reshape(len(windows), m, right.shape[0])


def out_rows(windows, tap_ref, frames, cols, mix_ref, o_ref):
    size = frames * cols
    height = len(windows)
    rows, ow = o_ref.shape[2:]
    now, back, oldest = [out_products(windows, tap_ref, a, -(-(frames - 2 + a) * cols // 16) * 16) for a in (2, 1, 0)]
    for y in range(height):
        full = jnp.concatenate(
            [
                now[y, :cols],
                now[y, cols : 2 * cols] + back[y, :cols],
                now[y, 2 * cols :] + back[y, cols : size - cols] + oldest[y, : size - 2 * cols],
            ],
            axis=0,
        )
        side = full[:, 2 * ow :]
        lane = lax.broadcasted_iota(jnp.int32, side.shape, 1)
        both = full[:, : 2 * ow] + jnp.where(lane < ow, shifted(side, cols, 1), shifted(side, cols, -1))
        mix_ref[y, pl.ds(0, size, stride=2), :] = both
        mix_ref[y, pl.ds(1, size, stride=2), :] = pltpu.roll(both, ow, 1)
    for y in range(height):
        result = mix_ref[y][:, :ow].astype(BF16)
        for t in range(frames):
            o_ref[t, y] = result[rows * t : rows * (t + 1)]


def inner_out_kernel(frames, cols, own_ref, other_ref, gain_ref, tap_ref, o_ref, norm_ref, mix_ref):
    size = frames * cols
    count = own_ref.shape[0] // size * 2
    rows = normalise(size, own_ref, other_ref, gain_ref, [None] * count)
    for k, j in enumerate((0, 1, count - 2, count - 1)):
        norm_ref[k] = rows[j]
    out_rows([rows[y : y + 3] for y in range(count - 2)], tap_ref, frames, cols, mix_ref, o_ref)


def edge_out_kernel(frames, cols, own_ref, other_ref, gain_ref, tap_ref, norm_ref, inner_ref, o_hbm, o_ref, mix_ref, sems):
    size = frames * cols
    inner = inner_ref.shape[1]
    copies = [pltpu.make_async_copy(inner_ref, o_hbm.at[:, pl.ds(2, inner)], sems.at[0])]
    copies[0].start()
    place = lax.axis_index("rows")
    last = lax.axis_size("rows") - 1
    edge = normalise(size, own_ref, other_ref, gain_ref, (place > 0, None, None, place < last))
    top = edge[:2] + [norm_ref[0], norm_ref[1]]
    bottom = [norm_ref[2], norm_ref[3]] + edge[2:]
    windows = [side[y : y + 3] for side in (top, bottom) for y in range(2)]
    out_rows(windows, tap_ref, frames, cols, mix_ref, o_ref)
    for k, start in enumerate((0, inner + 2)):
        copies.append(
            pltpu.make_async_copy(o_ref.at[:, pl.ds(2 * k, 2)], o_hbm.at[:, pl.ds(start, 2)], sems.at[1 + k])
        )
        copies[-1].start()
    for copy in copies:
        copy.wait()


def params(mib):
    return pltpu.CompilerParams(vmem_limit_bytes=mib * MIB)


def cost(mflops):
    return pl.CostEstimate(flops=mflops * 10**6, bytes_accessed=10**7, transcendentals=0)


def vmem():
    return pl.BlockSpec(memory_space=pltpu.VMEM)


def in_space(space, *arrays):
    return tuple(pltpu.with_memory_space_constraint(x, space) for x in arrays)


def call(kernel, name, outs, ins, mib, mflops, scratch=(), in_specs=None, out_specs=None):
    results = pl.pallas_call(
        kernel,
        out_shape=outs,
        in_specs=in_specs or [vmem()] * len(ins),
        out_specs=out_specs or (vmem(),) * len(outs),
        scratch_shapes=list(scratch),
        compiler_params=params(mib),
        cost_estimate=cost(mflops),
        name=name,
    )(*ins)
    return results if out_specs else in_space(pltpu.VMEM, *results)


def body(codes, in_proj, gain_up, up_kernel, gain_res, out_kernel):
    frames, rows, cols = codes.shape
    size = frames * cols
    width, share = up_kernel.shape[1:]
    ow = out_kernel.shape[1]
    height = 2 * rows
    inner = height - 4
    count = lax.axis_size("rows")
    joint = [pair for i in range(count - 1) for pair in ((2 * i, 2 * i + 3), (2 * i + 3, 2 * i))]
    swap = [(0, 1), (1, 0)]
    (mark,) = call(open_kernel, "open", (pltpu.VMEM((8, 128), F32),), (), 1, 1000)
    near = lax.ppermute(codes, ("rows", "section"), joint)
    gain_res = gain_res.reshape(1, -1)
    w, tap, proj, gain = in_space(pltpu.VMEM, up_kernel, out_kernel, in_proj, gain_up.reshape(1, -1))
    (codes,) = in_space(pltpu.VMEM, codes)
    hbm = pl.BlockSpec(memory_space=pltpu.HBM)

    (act,) = call(
        latent_kernel,
        "latent",
        (pltpu.VMEM((frames * rows * cols, width), BF16),),
        (codes, proj, gain, mark),
        4,
        1000,
    )
    cut = GROUPS[SPLIT][0]
    (own_first,) = call(
        functools.partial(own_first_kernel, rows * cols),
        "own_first",
        (pltpu.VMEM((rows * size, cut * share), F32),),
        (act, w),
        6,
        1000,
    )

    near, own_first = lax.optimization_barrier((near, own_first))
    far = lax.ppermute(near, "section", swap)
    near, far, own_first = in_space(pltpu.VMEM, near, far, own_first)
    inner_own, edge = call(
        functools.partial(own_rest_kernel, frames, cols),
        "own_rest",
        (pltpu.VMEM(((rows - 1) * size, 4 * share), BF16), pltpu.VMEM((2, size, 6 * share), F32)),
        (act, w, own_first, near),
        8,
        1000,
    )
    inner_other = lax.ppermute(inner_own, "section", swap)
    far, edge = lax.optimization_barrier((far, edge))
    far, edge = in_space(pltpu.VMEM, far, edge)
    (edge_own,) = call(
        halo_kernel,
        "halo",
        (pltpu.VMEM((2 * size, 4 * share), BF16),),
        (near, far, proj, gain, w, edge),
        8,
        20000,
    )
    edge_other = lax.ppermute(edge_own, "section", swap)
    inner_other, edge_other = in_space(pltpu.VMEM, inner_other, edge_other)

    mixed = pltpu.VMEM((max(inner, 4), 2 * size, 2 * ow), F32)
    out_inner, norm = call(
        functools.partial(inner_out_kernel, frames, cols),
        "out_inner",
        (pltpu.VMEM((frames, inner, 2 * cols, ow), BF16), pltpu.VMEM((4, size, 4 * share), BF16)),
        (inner_own, inner_other, gain_res, tap),
        12,
        2000,
        [mixed],
    )
    return call(
        functools.partial(edge_out_kernel, frames, cols),
        "out_edge",
        jax.ShapeDtypeStruct((frames, height, 2 * cols, ow), BF16),
        (edge_own, edge_other, gain_res, tap, norm, out_inner),
        12,
        1000,
        [pltpu.VMEM((frames, 4, 2 * cols, ow), BF16), mixed, pltpu.SemaphoreType.DMA((3,))],
        out_specs=hbm,
    )


def solution(mesh):
    in_specs = (
        P("clip", "rows", None),
        P(),
        P(),
        P(None, None, "section"),
        P(),
        P(None, "section", None),
    )
    out_specs = P("clip", "rows", None, "section")
    return jax.shard_map(body, mesh=mesh, in_specs=in_specs, out_specs=out_specs, check_vma=False)
```

```python
import functools

import jax
import jax.numpy as jnp
from jax import lax
from jax.experimental import pallas as pl
from jax.experimental.pallas import tpu as pltpu
from jax.sharding import PartitionSpec as P

BITS = 18
EPS = 1e-06
F32 = jnp.float32
BF16 = jnp.bfloat16
MIB = 1024 * 1024
GROUPS = ((0, 2), (2, 2), (4, 2), (6, 2), (8, 1))


def silu_of_half(h):
    return h + h * jnp.tanh(h)


def latent_rows(rows, in_proj, gain):
    cols = rows[0].shape[1]
    count = len(rows)
    wide = jnp.concatenate([jnp.broadcast_to(row, (cols, cols)) for row in rows], axis=0)
    sub = lax.broadcasted_iota(jnp.int32, (count, cols, cols), 1).reshape(count * cols, cols)
    lane = lax.broadcasted_iota(jnp.int32, (count * cols, cols), 1)
    picked = jnp.where(sub == lane, wide, 0).astype(F32)
    column = jnp.sum(picked, axis=1, keepdims=True).astype(jnp.int32)
    spread = jnp.broadcast_to(column, (count * cols, BITS))
    shift = lax.broadcasted_iota(jnp.int32, (count * cols, BITS), 1)
    bits = ((jnp.right_shift(spread, shift) & 1) * 2 - 1).astype(F32).astype(BF16)
    latent = jnp.dot(bits, in_proj, preferred_element_type=F32)
    mean = jnp.mean(latent * latent, axis=1, keepdims=True)
    return silu_of_half(latent * lax.rsqrt(mean + EPS) * (0.5 * gain))


def shifted(x, cols, amount):
    rows, lanes = x.shape
    place = lax.broadcasted_iota(jnp.int32, (rows // cols, cols, lanes), 1).reshape(rows, lanes)
    moved = pltpu.roll(x, amount % rows, 0)
    return jnp.where(place == (0 if amount == 1 else cols - 1), 0.0, moved)


def weights(w_ref, a, group):
    return jnp.concatenate([w_ref[9 * a + group[0] + k] for k in range(group[1])], axis=1)


def products(act, n, w_ref, group):
    share = w_ref.shape[2]
    if group[1] == 1:
        both = jnp.concatenate([weights(w_ref, 2, group), weights(w_ref, 1, group)], axis=1)
        now = jnp.dot(act, both, preferred_element_type=F32)
        now, back = now[:, :share], now[: 3 * n, share:]
    else:
        now = jnp.dot(act, weights(w_ref, 2, group), preferred_element_type=F32)
        back = jnp.dot(act[: 3 * n], weights(w_ref, 1, group), preferred_element_type=F32)
    oldest = jnp.dot(act[: 2 * n], weights(w_ref, 0, group), preferred_element_type=F32)
    return jnp.concatenate([now[:n], now[n : 2 * n] + back[:n], now[2 * n :] + back[n:] + oldest], axis=0)


def open_kernel(mark_ref):
    mark_ref[...] = jnp.zeros_like(mark_ref)


def latent_kernel(codes_ref, proj_ref, gain_ref, mark_ref, act_ref):
    frames, rows, cols = codes_ref.shape
    codes = [codes_ref[t, r : r + 1, :] for t in range(frames) for r in range(rows)]
    act_ref[...] = latent_rows(codes, proj_ref[...], gain_ref[...]).astype(BF16)


def row_products(act, n, w_ref, base):
    parts = []
    for first in range(0, 6, 2):
        total = []
        for a in range(3):
            m = -(-(2 + a) * n // 16) * 16
            pair = jnp.concatenate([w_ref[9 * a + base + first + k] for k in range(2)], axis=1)
            total.append(jnp.dot(act[:m], pair, preferred_element_type=F32))
        oldest, back, now = total
        parts.append(
            jnp.concatenate(
                [now[:n], now[n : 2 * n] + back[:n], now[2 * n :] + back[n : 3 * n] + oldest[: 2 * n]], axis=0
            )
        )
    return jnp.concatenate(parts, axis=1)


def of_row(part, frames, stride, start, cols):
    return jnp.concatenate([part[t * stride + start : t * stride + start + cols] for t in range(frames)], axis=0)


def put_hidden(upper, lower, cols, share, q, h_ref):
    size = upper(0).shape[0]
    sums = [[], []]
    for c in range(3):
        x = upper(c) + lower(6 + c)
        sums[0].append(x + upper(3 + c))
        sums[1].append(x + lower(3 + c))
    out = pl.ds(q * size, size)
    for py, (left, mid, right) in enumerate(sums):
        even = shifted(left, cols, 1) + (mid + right)
        odd = (left + mid) + shifted(right, cols, -1)
        h_ref[out, pl.ds(2 * py * share, share)] = even.astype(BF16)
        h_ref[out, pl.ds((2 * py + 1) * share, share)] = odd.astype(BF16)


def own_kernel(frames, cols, act_ref, w_ref, h_ref, edge_ref):
    share = w_ref.shape[2]
    n = act_ref.shape[0] // frames
    rows = n // cols
    act = act_ref[...]
    taken = []
    for group in GROUPS:
        part = products(act, n, w_ref, group)
        taken += [part[:, k * share : (k + 1) * share] for k in range(group[1])]

    def row(r):
        return lambda tap: of_row(taken[tap], frames, n, r * cols, cols)

    for q in range(rows - 1):
        put_hidden(row(q), row(q + 1), cols, share, q, h_ref)
    for k in range(6):
        edge_ref[0, :, pl.ds(k * share, share)] = row(0)(3 + k)
        edge_ref[1, :, pl.ds(k * share, share)] = row(rows - 1)(k)


def halo_products(codes_ref, below, proj_ref, gain_ref, w_ref):
    frames, rows, cols = codes_ref.shape
    place = lax.axis_index("rows")
    last = lax.axis_size("rows") - 1
    codes = [jnp.where(below, codes_ref[t, rows - 1 : rows, :], codes_ref[t, 0:1, :]) for t in range(frames)]
    act = latent_rows(codes, proj_ref[...], gain_ref[...])
    inside = jnp.where(below, place > 0, place < last)
    act = jnp.where(inside, act, 0.0).astype(BF16)
    return row_products(act, cols, w_ref, jnp.where(below, 0, 3))


def near_kernel(near_ref, proj_ref, gain_ref, w_ref, part_ref):
    below = lax.axis_index("section") == 1
    part_ref[...] = halo_products(near_ref, below, proj_ref, gain_ref, w_ref)


def halo_kernel(far_ref, proj_ref, gain_ref, w_ref, near_ref, edge_ref, h_ref):
    share = w_ref.shape[2]
    cols = far_ref.shape[2]
    below = lax.axis_index("section") == 0
    far = halo_products(far_ref, below, proj_ref, gain_ref, w_ref)

    def of(part, k):
        return part[:, k * share : (k + 1) * share]

    def lower_row(tap):
        return jnp.where(below, of(far, tap), near_ref[:, pl.ds(tap * share, share)])

    def upper_row(tap):
        return jnp.where(below, near_ref[:, pl.ds((tap - 3) * share, share)], of(far, tap - 3))

    put_hidden(lower_row, lambda tap: edge_ref[0, :, pl.ds((tap - 3) * share, share)], cols, share, 0, h_ref)
    put_hidden(lambda tap: edge_ref[1, :, pl.ds(tap * share, share)], upper_row, cols, share, 1, h_ref)


def part_starts(part):
    section = lax.axis_index("section")
    return [pl.multiple_of(k * part, part) for k in (section, 1 - section)]


def normalise(size, own_ref, other_ref, gain_ref, keeps):
    part = own_ref.shape[1] // 4
    gains = [0.5 * gain_ref[:, pl.ds(start, part)] for start in part_starts(part)]
    rows = []
    for j, keep in enumerate(keeps):
        cells = []
        for px in range(2):
            lanes = pl.ds((2 * (j % 2) + px) * part, part)
            x = [ref[pl.ds(j // 2 * size, size), lanes].astype(F32) for ref in (own_ref, other_ref)]
            mean = jnp.sum(x[0] * x[0] + x[1] * x[1], axis=1, keepdims=True) / (2 * part)
            scale = lax.rsqrt(mean + EPS)
            if keep is not None:
                scale = jnp.where(keep, scale, 0.0)
            cells += [silu_of_half(x[s] * scale * gains[s]).astype(BF16) for s in range(2)]
        rows.append(jnp.concatenate(cells, axis=1))
    return rows


def out_products(windows, tap_ref, a, m):
    left = jnp.concatenate([jnp.concatenate([row[:m] for row in window], axis=1) for window in windows], axis=0)
    part = tap_ref.shape[2] // 2
    starts = part_starts(part)
    lines = [[], [], [], []]
    for b in range(3):
        w = [
            jnp.concatenate([tap_ref[9 * a + 3 * b + c, :, pl.ds(start, part)] for start in starts], axis=1)
            for c in range(3)
        ]
        zero = jnp.zeros_like(w[0])
        for line, cells in zip(lines, ((w[1], w[2]), (w[0], w[1]), (zero, w[0]), (w[2], zero))):
            line += cells
    right = jnp.concatenate([jnp.concatenate(line, axis=1) for line in lines], axis=0)
    total = lax.dot_general(left, right, (((1,), (1,)), ((), ())), preferred_element_type=F32)
    return total.reshape(len(windows), m, right.shape[0])


def out_rows(windows, tap_ref, frames, cols, mix_ref, o_ref):
    size = frames * cols
    height = len(windows)
    rows, ow = o_ref.shape[2:]
    now, back, oldest = [out_products(windows, tap_ref, a, -(-(frames - 2 + a) * cols // 16) * 16) for a in (2, 1, 0)]
    for y in range(height):
        full = jnp.concatenate(
            [
                now[y, :cols],
                now[y, cols : 2 * cols] + back[y, :cols],
                now[y, 2 * cols :] + back[y, cols : size - cols] + oldest[y, : size - 2 * cols],
            ],
            axis=0,
        )
        side = full[:, 2 * ow :]
        lane = lax.broadcasted_iota(jnp.int32, side.shape, 1)
        both = full[:, : 2 * ow] + jnp.where(lane < ow, shifted(side, cols, 1), shifted(side, cols, -1))
        mix_ref[y, pl.ds(0, size, stride=2), :] = both
        mix_ref[y, pl.ds(1, size, stride=2), :] = pltpu.roll(both, ow, 1)
    for y in range(height):
        result = mix_ref[y][:, :ow].astype(BF16)
        for t in range(frames):
            o_ref[t, y] = result[rows * t : rows * (t + 1)]


def inner_out_kernel(frames, cols, own_ref, other_ref, gain_ref, tap_ref, o_ref, norm_ref, mix_ref):
    size = frames * cols
    count = own_ref.shape[0] // size * 2
    rows = normalise(size, own_ref, other_ref, gain_ref, [None] * count)
    for k, j in enumerate((0, 1, count - 2, count - 1)):
        norm_ref[k] = rows[j]
    out_rows([rows[y : y + 3] for y in range(count - 2)], tap_ref, frames, cols, mix_ref, o_ref)


def edge_out_kernel(frames, cols, own_ref, other_ref, gain_ref, tap_ref, norm_ref, inner_ref, o_hbm, o_ref, mix_ref, sems):
    size = frames * cols
    inner = inner_ref.shape[1]
    copies = [pltpu.make_async_copy(inner_ref, o_hbm.at[:, pl.ds(2, inner)], sems.at[0])]
    copies[0].start()
    place = lax.axis_index("rows")
    last = lax.axis_size("rows") - 1
    edge = normalise(size, own_ref, other_ref, gain_ref, (place > 0, None, None, place < last))
    top = edge[:2] + [norm_ref[0], norm_ref[1]]
    bottom = [norm_ref[2], norm_ref[3]] + edge[2:]
    windows = [side[y : y + 3] for side in (top, bottom) for y in range(2)]
    out_rows(windows, tap_ref, frames, cols, mix_ref, o_ref)
    for k, start in enumerate((0, inner + 2)):
        copies.append(
            pltpu.make_async_copy(o_ref.at[:, pl.ds(2 * k, 2)], o_hbm.at[:, pl.ds(start, 2)], sems.at[1 + k])
        )
        copies[-1].start()
    for copy in copies:
        copy.wait()


def params(mib):
    return pltpu.CompilerParams(vmem_limit_bytes=mib * MIB)


def cost(mflops):
    return pl.CostEstimate(flops=mflops * 10**6, bytes_accessed=10**7, transcendentals=0)


def vmem():
    return pl.BlockSpec(memory_space=pltpu.VMEM)


def in_space(space, *arrays):
    return tuple(pltpu.with_memory_space_constraint(x, space) for x in arrays)


def call(kernel, name, outs, ins, mib, mflops, scratch=(), in_specs=None, out_specs=None):
    results = pl.pallas_call(
        kernel,
        out_shape=outs,
        in_specs=in_specs or [vmem()] * len(ins),
        out_specs=out_specs or (vmem(),) * len(outs),
        scratch_shapes=list(scratch),
        compiler_params=params(mib),
        cost_estimate=cost(mflops),
        name=name,
    )(*ins)
    return results if out_specs else in_space(pltpu.VMEM, *results)


def body(codes, in_proj, gain_up, up_kernel, gain_res, out_kernel):
    frames, rows, cols = codes.shape
    size = frames * cols
    width, share = up_kernel.shape[1:]
    ow = out_kernel.shape[1]
    height = 2 * rows
    inner = height - 4
    count = lax.axis_size("rows")
    joint = [pair for i in range(count - 1) for pair in ((2 * i, 2 * i + 3), (2 * i + 3, 2 * i))]
    swap = [(0, 1), (1, 0)]
    (mark,) = call(open_kernel, "open", (pltpu.VMEM((8, 128), F32),), (), 1, 1000)
    near = lax.ppermute(codes, ("rows", "section"), joint)
    gain_res = gain_res.reshape(1, -1)
    w, tap, proj, gain = in_space(pltpu.VMEM, up_kernel, out_kernel, in_proj, gain_up.reshape(1, -1))
    (codes,) = in_space(pltpu.VMEM, codes)
    hbm = pl.BlockSpec(memory_space=pltpu.HBM)

    (act,) = call(
        latent_kernel,
        "latent",
        (pltpu.VMEM((frames * rows * cols, width), BF16),),
        (codes, proj, gain, mark),
        4,
        1000,
    )
    inner_own, edge = call(
        functools.partial(own_kernel, frames, cols),
        "own",
        (pltpu.VMEM(((rows - 1) * size, 4 * share), BF16), pltpu.VMEM((2, size, 6 * share), F32)),
        (act, w),
        8,
        1000,
    )
    inner_other = lax.ppermute(inner_own, "section", swap)

    near, edge = lax.optimization_barrier((near, edge))
    far = lax.ppermute(near, "section", swap)
    near, far, edge = in_space(pltpu.VMEM, near, far, edge)
    (near_part,) = call(
        near_kernel,
        "near",
        (pltpu.VMEM((size, 6 * share), F32),),
        (near, proj, gain, w),
        6,
        3000,
    )
    far, near_part = lax.optimization_barrier((far, near_part))
    far, near_part = in_space(pltpu.VMEM, far, near_part)
    (edge_own,) = call(
        halo_kernel,
        "halo",
        (pltpu.VMEM((2 * size, 4 * share), BF16),),
        (far, proj, gain, w, near_part, edge),
        8,
        20000,
    )
    edge_other = lax.ppermute(edge_own, "section", swap)
    inner_other, edge_other = in_space(pltpu.VMEM, inner_other, edge_other)

    mixed = pltpu.VMEM((max(inner, 4), 2 * size, 2 * ow), F32)
    out_inner, norm = call(
        functools.partial(inner_out_kernel, frames, cols),
        "out_inner",
        (pltpu.VMEM((frames, inner, 2 * cols, ow), BF16), pltpu.VMEM((4, size, 4 * share), BF16)),
        (inner_own, inner_other, gain_res, tap),
        12,
        2000,
        [mixed],
    )
    return call(
        functools.partial(edge_out_kernel, frames, cols),
        "out_edge",
        jax.ShapeDtypeStruct((frames, height, 2 * cols, ow), BF16),
        (edge_own, edge_other, gain_res, tap, norm, out_inner),
        12,
        1000,
        [pltpu.VMEM((frames, 4, 2 * cols, ow), BF16), mixed, pltpu.SemaphoreType.DMA((3,))],
        out_specs=hbm,
    )


def solution(mesh):
    in_specs = (
        P("clip", "rows", None),
        P(),
        P(),
        P(None, None, "section"),
        P(),
        P(None, "section", None),
    )
    out_specs = P("clip", "rows", None, "section")
    return jax.shard_map(body, mesh=mesh, in_specs=in_specs, out_specs=out_specs, check_vma=False)
```

```python
import functools

import jax
import jax.numpy as jnp
from jax import lax
from jax.experimental import pallas as pl
from jax.experimental.pallas import tpu as pltpu
from jax.sharding import PartitionSpec as P

BITS = 18
EPS = 1e-06
F32 = jnp.float32
BF16 = jnp.bfloat16
MIB = 1024 * 1024
GROUPS = ((0, 2), (2, 2), (4, 2), (6, 2), (8, 1))


def silu_of_half(h):
    return h + h * jnp.tanh(h)


def latent_rows(rows, in_proj, gain):
    cols = rows[0].shape[1]
    count = len(rows)
    wide = jnp.concatenate([jnp.broadcast_to(row, (cols, cols)) for row in rows], axis=0)
    sub = lax.broadcasted_iota(jnp.int32, (count, cols, cols), 1).reshape(count * cols, cols)
    lane = lax.broadcasted_iota(jnp.int32, (count * cols, cols), 1)
    picked = jnp.where(sub == lane, wide, 0).astype(F32)
    column = jnp.sum(picked, axis=1, keepdims=True).astype(jnp.int32)
    spread = jnp.broadcast_to(column, (count * cols, BITS))
    shift = lax.broadcasted_iota(jnp.int32, (count * cols, BITS), 1)
    bits = ((jnp.right_shift(spread, shift) & 1) * 2 - 1).astype(F32).astype(BF16)
    latent = jnp.dot(bits, in_proj, preferred_element_type=F32)
    mean = jnp.mean(latent * latent, axis=1, keepdims=True)
    return silu_of_half(latent * lax.rsqrt(mean + EPS) * (0.5 * gain))


def shifted(x, cols, amount):
    rows, lanes = x.shape
    place = lax.broadcasted_iota(jnp.int32, (rows // cols, cols, lanes), 1).reshape(rows, lanes)
    moved = pltpu.roll(x, amount % rows, 0)
    return jnp.where(place == (0 if amount == 1 else cols - 1), 0.0, moved)


def weights(w_ref, a, group):
    return jnp.concatenate([w_ref[9 * a + group[0] + k] for k in range(group[1])], axis=1)


def products(act, n, w_ref, group):
    share = w_ref.shape[2]
    if group[1] == 1:
        both = jnp.concatenate([weights(w_ref, 2, group), weights(w_ref, 1, group)], axis=1)
        now = jnp.dot(act, both, preferred_element_type=F32)
        now, back = now[:, :share], now[: 3 * n, share:]
    else:
        now = jnp.dot(act, weights(w_ref, 2, group), preferred_element_type=F32)
        back = jnp.dot(act[: 3 * n], weights(w_ref, 1, group), preferred_element_type=F32)
    oldest = jnp.dot(act[: 2 * n], weights(w_ref, 0, group), preferred_element_type=F32)
    return jnp.concatenate([now[:n], now[n : 2 * n] + back[:n], now[2 * n :] + back[n:] + oldest], axis=0)


def open_kernel(mark_ref):
    mark_ref[...] = jnp.zeros_like(mark_ref)


def latent_kernel(codes_ref, proj_ref, gain_ref, mark_ref, act_ref):
    frames, rows, cols = codes_ref.shape
    codes = [codes_ref[t, r : r + 1, :] for t in range(frames) for r in range(rows)]
    act_ref[...] = latent_rows(codes, proj_ref[...], gain_ref[...]).astype(BF16)


def row_products(act, n, w_ref, base):
    parts = []
    for first in range(0, 6, 2):
        total = []
        for a in range(3):
            m = -(-(2 + a) * n // 16) * 16
            pair = jnp.concatenate([w_ref[9 * a + base + first + k] for k in range(2)], axis=1)
            total.append(jnp.dot(act[:m], pair, preferred_element_type=F32))
        oldest, back, now = total
        parts.append(
            jnp.concatenate(
                [now[:n], now[n : 2 * n] + back[:n], now[2 * n :] + back[n : 3 * n] + oldest[: 2 * n]], axis=0
            )
        )
    return jnp.concatenate(parts, axis=1)


def of_row(part, frames, stride, start, cols):
    return jnp.concatenate([part[t * stride + start : t * stride + start + cols] for t in range(frames)], axis=0)


def put_hidden(upper, lower, cols, share, q, h_ref):
    size = upper(0).shape[0]
    sums = [[], []]
    for c in range(3):
        x = upper(c) + lower(6 + c)
        sums[0].append(x + upper(3 + c))
        sums[1].append(x + lower(3 + c))
    out = pl.ds(q * size, size)
    for py, (left, mid, right) in enumerate(sums):
        even = shifted(left, cols, 1) + (mid + right)
        odd = (left + mid) + shifted(right, cols, -1)
        h_ref[out, pl.ds(2 * py * share, share)] = even.astype(BF16)
        h_ref[out, pl.ds((2 * py + 1) * share, share)] = odd.astype(BF16)


def own_kernel(frames, cols, act_ref, w_ref, h_ref, edge_ref):
    share = w_ref.shape[2]
    n = act_ref.shape[0] // frames
    rows = n // cols
    act = act_ref[...]
    taken = []
    for group in GROUPS:
        part = products(act, n, w_ref, group)
        taken += [part[:, k * share : (k + 1) * share] for k in range(group[1])]

    def row(r):
        return lambda tap: of_row(taken[tap], frames, n, r * cols, cols)

    for q in range(rows - 1):
        put_hidden(row(q), row(q + 1), cols, share, q, h_ref)
    for k in range(6):
        edge_ref[0, :, pl.ds(k * share, share)] = row(0)(3 + k)
        edge_ref[1, :, pl.ds(k * share, share)] = row(rows - 1)(k)


def halo_products(codes_ref, below, proj_ref, gain_ref, w_ref):
    frames, rows, cols = codes_ref.shape
    place = lax.axis_index("rows")
    last = lax.axis_size("rows") - 1
    codes = [jnp.where(below, codes_ref[t, rows - 1 : rows, :], codes_ref[t, 0:1, :]) for t in range(frames)]
    act = latent_rows(codes, proj_ref[...], gain_ref[...])
    inside = jnp.where(below, place > 0, place < last)
    act = jnp.where(inside, act, 0.0).astype(BF16)
    return row_products(act, cols, w_ref, jnp.where(below, 0, 3))


def near_kernel(near_ref, proj_ref, gain_ref, w_ref, part_ref):
    below = lax.axis_index("section") == 1
    part_ref[...] = halo_products(near_ref, below, proj_ref, gain_ref, w_ref)


def halo_kernel(far_ref, proj_ref, gain_ref, w_ref, near_ref, edge_ref, h_ref):
    share = w_ref.shape[2]
    cols = far_ref.shape[2]
    below = lax.axis_index("section") == 0
    far = halo_products(far_ref, below, proj_ref, gain_ref, w_ref)

    def of(part, k):
        return part[:, k * share : (k + 1) * share]

    def lower_row(tap):
        return jnp.where(below, of(far, tap), near_ref[:, pl.ds(tap * share, share)])

    def upper_row(tap):
        return jnp.where(below, near_ref[:, pl.ds((tap - 3) * share, share)], of(far, tap - 3))

    put_hidden(lower_row, lambda tap: edge_ref[0, :, pl.ds((tap - 3) * share, share)], cols, share, 0, h_ref)
    put_hidden(lambda tap: edge_ref[1, :, pl.ds(tap * share, share)], upper_row, cols, share, 1, h_ref)


def part_starts(part):
    section = lax.axis_index("section")
    return [pl.multiple_of(k * part, part) for k in (section, 1 - section)]


def normalise(size, own_ref, other_ref, gain_ref, keeps):
    part = own_ref.shape[1] // 4
    gains = [0.5 * gain_ref[:, pl.ds(start, part)] for start in part_starts(part)]
    rows = []
    for j, keep in enumerate(keeps):
        cells = []
        for px in range(2):
            lanes = pl.ds((2 * (j % 2) + px) * part, part)
            x = [ref[pl.ds(j // 2 * size, size), lanes].astype(F32) for ref in (own_ref, other_ref)]
            mean = jnp.sum(x[0] * x[0] + x[1] * x[1], axis=1, keepdims=True) / (2 * part)
            scale = lax.rsqrt(mean + EPS)
            if keep is not None:
                scale = jnp.where(keep, scale, 0.0)
            cells += [silu_of_half(x[s] * scale * gains[s]).astype(BF16) for s in range(2)]
        rows.append(jnp.concatenate(cells, axis=1))
    return rows


def table(tap_ref, a, b):
    part = tap_ref.shape[2] // 2
    w = [
        jnp.concatenate([tap_ref[9 * a + 3 * b + c, :, pl.ds(start, part)] for start in part_starts(part)], axis=1)
        for c in range(3)
    ]
    zero = jnp.zeros_like(w[0])
    lines = ((w[1], w[2]), (w[0], w[1]), (zero, w[0]), (w[2], zero))
    return jnp.concatenate([jnp.concatenate(line, axis=1) for line in lines], axis=0)


def times(left, right, count):
    total = lax.dot_general(left, right, (((1,), (1,)), ((), ())), preferred_element_type=F32)
    return total.reshape(count, left.shape[0] // count, right.shape[0])


def reach(frames, cols, a):
    return -(-(frames - 2 + a) * cols // 16) * 16


def in_time(now, back, oldest, cols):
    size = now.shape[0]
    return jnp.concatenate(
        [
            now[:cols],
            now[cols : 2 * cols] + back[:cols],
            now[2 * cols :] + back[cols : size - cols] + oldest[: size - 2 * cols],
        ],
        axis=0,
    )


def window_sums(windows, tap_ref, frames, cols):
    sums = []
    for a in (2, 1, 0):
        m = reach(frames, cols, a)
        left = jnp.concatenate([jnp.concatenate([row[:m] for row in window], axis=1) for window in windows], axis=0)
        right = jnp.concatenate([table(tap_ref, a, b) for b in range(3)], axis=1)
        sums.append(times(left, right, len(windows)))
    return [in_time(*[part[y] for part in sums], cols) for y in range(len(windows))]


def partial_sums(terms, tap_ref, frames, cols):
    sums = []
    for a in (2, 1, 0):
        m = reach(frames, cols, a)
        share = {}
        for b, pairs in enumerate(terms):
            part = times(jnp.concatenate([row[:m] for _, row in pairs], axis=0), table(tap_ref, a, b), len(pairs))
            for k, (y, _) in enumerate(pairs):
                share[y] = share[y] + part[k] if y in share else part[k]
        sums.append(share)
    return [in_time(*[share[y] for share in sums], cols) for y in sorted(sums[0])]


def put_rows(fulls, frames, cols, mix_ref, o_ref):
    size = frames * cols
    rows, ow = o_ref.shape[2:]
    for y, full in enumerate(fulls):
        side = full[:, 2 * ow :]
        lane = lax.broadcasted_iota(jnp.int32, side.shape, 1)
        both = full[:, : 2 * ow] + jnp.where(lane < ow, shifted(side, cols, 1), shifted(side, cols, -1))
        mix_ref[y, pl.ds(0, size, stride=2), :] = both
        mix_ref[y, pl.ds(1, size, stride=2), :] = pltpu.roll(both, ow, 1)
    for y in range(len(fulls)):
        result = mix_ref[y][:, :ow].astype(BF16)
        for t in range(frames):
            o_ref[t, y] = result[rows * t : rows * (t + 1)]


def norm_kernel(size, own_ref, other_ref, gain_ref, norm_ref):
    for j, row in enumerate(normalise(size, own_ref, other_ref, gain_ref, [None] * norm_ref.shape[0])):
        norm_ref[j] = row


def inner_out_kernel(frames, cols, norm_ref, tap_ref, o_ref, held_ref, mix_ref):
    count = norm_ref.shape[0]
    rows = [norm_ref[j] for j in range(count)]
    fulls = window_sums([rows[y : y + 3] for y in range(count - 2)], tap_ref, frames, cols)
    terms = (
        ((2, rows[-2]), (3, rows[-1])),
        ((1, rows[0]), (2, rows[-1])),
        ((0, rows[0]), (1, rows[1])),
    )
    for y, full in enumerate(partial_sums(terms, tap_ref, frames, cols)):
        held_ref[y] = full
    put_rows(fulls, frames, cols, mix_ref, o_ref)


def edge_out_kernel(frames, cols, own_ref, other_ref, gain_ref, tap_ref, held_ref, inner_ref, o_hbm, o_ref, mix_ref, sems):
    size = frames * cols
    inner = inner_ref.shape[1]
    copies = [pltpu.make_async_copy(inner_ref, o_hbm.at[:, pl.ds(2, inner)], sems.at[0])]
    copies[0].start()
    place = lax.axis_index("rows")
    last = lax.axis_size("rows") - 1
    edge = normalise(size, own_ref, other_ref, gain_ref, (place > 0, None, None, place < last))
    terms = (
        ((0, edge[0]), (1, edge[1])),
        ((0, edge[1]), (3, edge[2])),
        ((2, edge[2]), (3, edge[3])),
    )
    fulls = [held_ref[y] + full for y, full in enumerate(partial_sums(terms, tap_ref, frames, cols))]
    put_rows(fulls, frames, cols, mix_ref, o_ref)
    for k, start in enumerate((0, inner + 2)):
        copies.append(
            pltpu.make_async_copy(o_ref.at[:, pl.ds(2 * k, 2)], o_hbm.at[:, pl.ds(start, 2)], sems.at[1 + k])
        )
        copies[-1].start()
    for copy in copies:
        copy.wait()


def params(mib):
    return pltpu.CompilerParams(vmem_limit_bytes=mib * MIB)


def cost(mflops):
    return pl.CostEstimate(flops=mflops * 10**6, bytes_accessed=10**7, transcendentals=0)


def vmem():
    return pl.BlockSpec(memory_space=pltpu.VMEM)


def in_space(space, *arrays):
    return tuple(pltpu.with_memory_space_constraint(x, space) for x in arrays)


def call(kernel, name, outs, ins, mib, mflops, scratch=(), in_specs=None, out_specs=None):
    results = pl.pallas_call(
        kernel,
        out_shape=outs,
        in_specs=in_specs or [vmem()] * len(ins),
        out_specs=out_specs or (vmem(),) * len(outs),
        scratch_shapes=list(scratch),
        compiler_params=params(mib),
        cost_estimate=cost(mflops),
        name=name,
    )(*ins)
    return results if out_specs else in_space(pltpu.VMEM, *results)


def body(codes, in_proj, gain_up, up_kernel, gain_res, out_kernel):
    frames, rows, cols = codes.shape
    size = frames * cols
    width, share = up_kernel.shape[1:]
    ow = out_kernel.shape[1]
    height = 2 * rows
    inner = height - 4
    count = lax.axis_size("rows")
    joint = [pair for i in range(count - 1) for pair in ((2 * i, 2 * i + 3), (2 * i + 3, 2 * i))]
    swap = [(0, 1), (1, 0)]
    (mark,) = call(open_kernel, "open", (pltpu.VMEM((8, 128), F32),), (), 1, 1000)
    near = lax.ppermute(codes, ("rows", "section"), joint)
    gain_res = gain_res.reshape(1, -1)
    w, tap, proj, gain = in_space(pltpu.VMEM, up_kernel, out_kernel, in_proj, gain_up.reshape(1, -1))
    (codes,) = in_space(pltpu.VMEM, codes)
    hbm = pl.BlockSpec(memory_space=pltpu.HBM)

    (act,) = call(
        latent_kernel,
        "latent",
        (pltpu.VMEM((frames * rows * cols, width), BF16),),
        (codes, proj, gain, mark),
        4,
        1000,
    )
    inner_own, edge = call(
        functools.partial(own_kernel, frames, cols),
        "own",
        (pltpu.VMEM(((rows - 1) * size, 4 * share), BF16), pltpu.VMEM((2, size, 6 * share), F32)),
        (act, w),
        8,
        1000,
    )
    inner_other = lax.ppermute(inner_own, "section", swap)

    near, edge = lax.optimization_barrier((near, edge))
    far = lax.ppermute(near, "section", swap)
    near, far, edge = in_space(pltpu.VMEM, near, far, edge)
    (near_part,) = call(
        near_kernel,
        "near",
        (pltpu.VMEM((size, 6 * share), F32),),
        (near, proj, gain, w),
        6,
        20000,
    )
    inner_other, near_part = lax.optimization_barrier((inner_other, near_part))
    inner_own, inner_other = in_space(pltpu.VMEM, inner_own, inner_other)
    (norm,) = call(
        functools.partial(norm_kernel, size),
        "norm",
        (pltpu.VMEM((height - 2, size, 4 * share), BF16),),
        (inner_own, inner_other, gain_res),
        6,
        1000,
    )
    far, near_part, norm = lax.optimization_barrier((far, near_part, norm))
    far, near_part, norm = in_space(pltpu.VMEM, far, near_part, norm)
    (edge_own,) = call(
        halo_kernel,
        "halo",
        (pltpu.VMEM((2 * size, 4 * share), BF16),),
        (far, proj, gain, w, near_part, edge),
        8,
        20000,
    )
    edge_other = lax.ppermute(edge_own, "section", swap)
    (edge_other,) = in_space(pltpu.VMEM, edge_other)

    mixed = pltpu.VMEM((max(inner, 4), 2 * size, 2 * ow), F32)
    out_inner, held = call(
        functools.partial(inner_out_kernel, frames, cols),
        "out_inner",
        (pltpu.VMEM((frames, inner, 2 * cols, ow), BF16), pltpu.VMEM((4, size, 4 * ow), F32)),
        (norm, tap),
        12,
        2000,
        [mixed],
    )
    return call(
        functools.partial(edge_out_kernel, frames, cols),
        "out_edge",
        jax.ShapeDtypeStruct((frames, height, 2 * cols, ow), BF16),
        (edge_own, edge_other, gain_res, tap, held, out_inner),
        12,
        1000,
        [pltpu.VMEM((frames, 4, 2 * cols, ow), BF16), mixed, pltpu.SemaphoreType.DMA((3,))],
        out_specs=hbm,
    )


def solution(mesh):
    in_specs = (
        P("clip", "rows", None),
        P(),
        P(),
        P(None, None, "section"),
        P(),
        P(None, "section", None),
    )
    out_specs = P("clip", "rows", None, "section")
    return jax.shard_map(body, mesh=mesh, in_specs=in_specs, out_specs=out_specs, check_vma=False)
```

```python
import functools

import jax
import jax.numpy as jnp
from jax import lax
from jax.experimental import pallas as pl
from jax.experimental.pallas import tpu as pltpu
from jax.sharding import PartitionSpec as P

BITS = 18
EPS = 1e-06
F32 = jnp.float32
BF16 = jnp.bfloat16
MIB = 1024 * 1024
GROUPS = ((0, 2), (2, 2), (4, 2), (6, 2), (8, 1))


def silu_of_half(h):
    return h + h * jnp.tanh(h)


def latent_rows(rows, in_proj, gain):
    cols = rows[0].shape[1]
    count = len(rows)
    wide = jnp.concatenate([jnp.broadcast_to(row, (cols, cols)) for row in rows], axis=0)
    sub = lax.broadcasted_iota(jnp.int32, (count, cols, cols), 1).reshape(count * cols, cols)
    lane = lax.broadcasted_iota(jnp.int32, (count * cols, cols), 1)
    picked = jnp.where(sub == lane, wide, 0).astype(F32)
    column = jnp.sum(picked, axis=1, keepdims=True).astype(jnp.int32)
    spread = jnp.broadcast_to(column, (count * cols, BITS))
    shift = lax.broadcasted_iota(jnp.int32, (count * cols, BITS), 1)
    bits = ((jnp.right_shift(spread, shift) & 1) * 2 - 1).astype(F32).astype(BF16)
    latent = jnp.dot(bits, in_proj, preferred_element_type=F32)
    mean = jnp.mean(latent * latent, axis=1, keepdims=True)
    return silu_of_half(latent * lax.rsqrt(mean + EPS) * (0.5 * gain))


def shifted(x, cols, amount):
    rows, lanes = x.shape
    place = lax.broadcasted_iota(jnp.int32, (rows // cols, cols, lanes), 1).reshape(rows, lanes)
    moved = pltpu.roll(x, amount % rows, 0)
    return jnp.where(place == (0 if amount == 1 else cols - 1), 0.0, moved)


def weights(w_ref, a, group):
    return jnp.concatenate([w_ref[9 * a + group[0] + k] for k in range(group[1])], axis=1)


def products(act, n, w_ref, group):
    share = w_ref.shape[2]
    if group[1] == 1:
        both = jnp.concatenate([weights(w_ref, 2, group), weights(w_ref, 1, group)], axis=1)
        now = jnp.dot(act, both, preferred_element_type=F32)
        now, back = now[:, :share], now[: 3 * n, share:]
    else:
        now = jnp.dot(act, weights(w_ref, 2, group), preferred_element_type=F32)
        back = jnp.dot(act[: 3 * n], weights(w_ref, 1, group), preferred_element_type=F32)
    oldest = jnp.dot(act[: 2 * n], weights(w_ref, 0, group), preferred_element_type=F32)
    return jnp.concatenate([now[:n], now[n : 2 * n] + back[:n], now[2 * n :] + back[n:] + oldest], axis=0)


def open_kernel(mark_ref):
    mark_ref[...] = jnp.zeros_like(mark_ref)


def latent_kernel(codes_ref, proj_ref, gain_ref, mark_ref, act_ref):
    frames, rows, cols = codes_ref.shape
    codes = [codes_ref[t, r : r + 1, :] for t in range(frames) for r in range(rows)]
    act_ref[...] = latent_rows(codes, proj_ref[...], gain_ref[...]).astype(BF16)


def row_products(act, n, w_ref, base):
    parts = []
    for first in range(0, 6, 2):
        total = []
        for a in range(3):
            m = -(-(2 + a) * n // 16) * 16
            pair = jnp.concatenate([w_ref[9 * a + base + first + k] for k in range(2)], axis=1)
            total.append(jnp.dot(act[:m], pair, preferred_element_type=F32))
        oldest, back, now = total
        parts.append(
            jnp.concatenate(
                [now[:n], now[n : 2 * n] + back[:n], now[2 * n :] + back[n : 3 * n] + oldest[: 2 * n]], axis=0
            )
        )
    return jnp.concatenate(parts, axis=1)


def of_row(part, frames, stride, start, cols):
    return jnp.concatenate([part[t * stride + start : t * stride + start + cols] for t in range(frames)], axis=0)


def put_hidden(upper, lower, cols, share, q, h_ref):
    size = upper(0).shape[0]
    sums = [[], []]
    for c in range(3):
        x = upper(c) + lower(6 + c)
        sums[0].append(x + upper(3 + c))
        sums[1].append(x + lower(3 + c))
    out = pl.ds(q * size, size)
    for py, (left, mid, right) in enumerate(sums):
        even = shifted(left, cols, 1) + (mid + right)
        odd = (left + mid) + shifted(right, cols, -1)
        h_ref[out, pl.ds(2 * py * share, share)] = even.astype(BF16)
        h_ref[out, pl.ds((2 * py + 1) * share, share)] = odd.astype(BF16)


def own_kernel(frames, cols, act_ref, w_ref, h_ref, edge_ref):
    share = w_ref.shape[2]
    n = act_ref.shape[0] // frames
    rows = n // cols
    act = act_ref[...]
    taken = []
    for group in GROUPS:
        part = products(act, n, w_ref, group)
        taken += [part[:, k * share : (k + 1) * share] for k in range(group[1])]

    def row(r):
        return lambda tap: of_row(taken[tap], frames, n, r * cols, cols)

    for q in range(rows - 1):
        put_hidden(row(q), row(q + 1), cols, share, q, h_ref)
    for k in range(6):
        edge_ref[0, :, pl.ds(k * share, share)] = row(0)(3 + k)
        edge_ref[1, :, pl.ds(k * share, share)] = row(rows - 1)(k)


def halo_products(codes_ref, below, proj_ref, gain_ref, w_ref):
    frames, rows, cols = codes_ref.shape
    place = lax.axis_index("rows")
    last = lax.axis_size("rows") - 1
    codes = [jnp.where(below, codes_ref[t, rows - 1 : rows, :], codes_ref[t, 0:1, :]) for t in range(frames)]
    act = latent_rows(codes, proj_ref[...], gain_ref[...])
    inside = jnp.where(below, place > 0, place < last)
    act = jnp.where(inside, act, 0.0).astype(BF16)
    return row_products(act, cols, w_ref, jnp.where(below, 0, 3))


def near_kernel(near_ref, proj_ref, gain_ref, w_ref, part_ref):
    below = lax.axis_index("section") == 1
    part_ref[...] = halo_products(near_ref, below, proj_ref, gain_ref, w_ref)


def halo_kernel(far_ref, proj_ref, gain_ref, w_ref, near_ref, edge_ref, h_ref):
    share = w_ref.shape[2]
    cols = far_ref.shape[2]
    below = lax.axis_index("section") == 0
    far = halo_products(far_ref, below, proj_ref, gain_ref, w_ref)

    def of(part, k):
        return part[:, k * share : (k + 1) * share]

    def lower_row(tap):
        return jnp.where(below, of(far, tap), near_ref[:, pl.ds(tap * share, share)])

    def upper_row(tap):
        return jnp.where(below, near_ref[:, pl.ds((tap - 3) * share, share)], of(far, tap - 3))

    put_hidden(lower_row, lambda tap: edge_ref[0, :, pl.ds((tap - 3) * share, share)], cols, share, 0, h_ref)
    put_hidden(lambda tap: edge_ref[1, :, pl.ds(tap * share, share)], upper_row, cols, share, 1, h_ref)


def part_starts(part):
    section = lax.axis_index("section")
    return [pl.multiple_of(k * part, part) for k in (section, 1 - section)]


def normalise(size, own_ref, other_ref, gain_ref, keeps):
    part = own_ref.shape[1] // 4
    gains = [0.5 * gain_ref[:, pl.ds(start, part)] for start in part_starts(part)]
    rows = []
    for j, keep in enumerate(keeps):
        cells = []
        for px in range(2):
            lanes = pl.ds((2 * (j % 2) + px) * part, part)
            x = [ref[pl.ds(j // 2 * size, size), lanes].astype(F32) for ref in (own_ref, other_ref)]
            mean = jnp.sum(x[0] * x[0] + x[1] * x[1], axis=1, keepdims=True) / (2 * part)
            scale = lax.rsqrt(mean + EPS)
            if keep is not None:
                scale = jnp.where(keep, scale, 0.0)
            cells += [silu_of_half(x[s] * scale * gains[s]).astype(BF16) for s in range(2)]
        rows.append(jnp.concatenate(cells, axis=1))
    return rows


def out_products(windows, tap_ref, a, m):
    left = jnp.concatenate([jnp.concatenate([row[:m] for row in window], axis=1) for window in windows], axis=0)
    part = tap_ref.shape[2] // 2
    starts = part_starts(part)
    lines = [[], [], [], []]
    for b in range(3):
        w = [
            jnp.concatenate([tap_ref[9 * a + 3 * b + c, :, pl.ds(start, part)] for start in starts], axis=1)
            for c in range(3)
        ]
        zero = jnp.zeros_like(w[0])
        for line, cells in zip(lines, ((w[1], w[2]), (w[0], w[1]), (zero, w[0]), (w[2], zero))):
            line += cells
    right = jnp.concatenate([jnp.concatenate(line, axis=1) for line in lines], axis=0)
    total = lax.dot_general(left, right, (((1,), (1,)), ((), ())), preferred_element_type=F32)
    return total.reshape(len(windows), m, right.shape[0])


def out_rows(windows, tap_ref, frames, cols, mix_ref, o_ref, after_half=None):
    size = frames * cols
    height = len(windows)
    rows, ow = o_ref.shape[2:]
    now, back, oldest = [out_products(windows, tap_ref, a, -(-(frames - 2 + a) * cols // 16) * 16) for a in (2, 1, 0)]
    for y in range(height):
        full = jnp.concatenate(
            [
                now[y, :cols],
                now[y, cols : 2 * cols] + back[y, :cols],
                now[y, 2 * cols :] + back[y, cols : size - cols] + oldest[y, : size - 2 * cols],
            ],
            axis=0,
        )
        side = full[:, 2 * ow :]
        lane = lax.broadcasted_iota(jnp.int32, side.shape, 1)
        both = full[:, : 2 * ow] + jnp.where(lane < ow, shifted(side, cols, 1), shifted(side, cols, -1))
        mix_ref[y, pl.ds(0, size, stride=2), :] = both
        mix_ref[y, pl.ds(1, size, stride=2), :] = pltpu.roll(both, ow, 1)
    for y in range(height):
        result = mix_ref[y][:, :ow].astype(BF16)
        for t in range(frames):
            o_ref[t, y] = result[rows * t : rows * (t + 1)]
        if after_half is not None and 2 * (y + 1) == height:
            after_half()


def inner_out_kernel(frames, cols, own_ref, other_ref, gain_ref, tap_ref, o_ref, norm_ref, mix_ref):
    size = frames * cols
    count = own_ref.shape[0] // size * 2
    rows = normalise(size, own_ref, other_ref, gain_ref, [None] * count)
    for k, j in enumerate((0, 1, count - 2, count - 1)):
        norm_ref[k] = rows[j]
    out_rows([rows[y : y + 3] for y in range(count - 2)], tap_ref, frames, cols, mix_ref, o_ref)


def edge_out_kernel(frames, cols, own_ref, other_ref, gain_ref, tap_ref, norm_ref, inner_ref, o_hbm, o_ref, mix_ref, sems):
    size = frames * cols
    inner = inner_ref.shape[1]
    copies = [pltpu.make_async_copy(inner_ref, o_hbm.at[:, pl.ds(2, inner)], sems.at[0])]
    copies[0].start()
    place = lax.axis_index("rows")
    last = lax.axis_size("rows") - 1
    edge = normalise(size, own_ref, other_ref, gain_ref, (place > 0, None, None, place < last))
    top = edge[:2] + [norm_ref[0], norm_ref[1]]
    bottom = [norm_ref[2], norm_ref[3]] + edge[2:]
    windows = [side[y : y + 3] for side in (top, bottom) for y in range(2)]
    for k, start in enumerate((0, inner + 2)):
        copies.append(
            pltpu.make_async_copy(o_ref.at[:, pl.ds(2 * k, 2)], o_hbm.at[:, pl.ds(start, 2)], sems.at[1 + k])
        )
    out_rows(windows, tap_ref, frames, cols, mix_ref, o_ref, copies[1].start)
    copies[2].start()
    for copy in copies:
        copy.wait()


def params(mib):
    return pltpu.CompilerParams(vmem_limit_bytes=mib * MIB)


def cost(mflops):
    return pl.CostEstimate(flops=mflops * 10**6, bytes_accessed=10**7, transcendentals=0)


def vmem():
    return pl.BlockSpec(memory_space=pltpu.VMEM)


def in_space(space, *arrays):
    return tuple(pltpu.with_memory_space_constraint(x, space) for x in arrays)


def call(kernel, name, outs, ins, mib, mflops, scratch=(), in_specs=None, out_specs=None):
    results = pl.pallas_call(
        kernel,
        out_shape=outs,
        in_specs=in_specs or [vmem()] * len(ins),
        out_specs=out_specs or (vmem(),) * len(outs),
        scratch_shapes=list(scratch),
        compiler_params=params(mib),
        cost_estimate=cost(mflops),
        name=name,
    )(*ins)
    return results if out_specs else in_space(pltpu.VMEM, *results)


def body(codes, in_proj, gain_up, up_kernel, gain_res, out_kernel):
    frames, rows, cols = codes.shape
    size = frames * cols
    width, share = up_kernel.shape[1:]
    ow = out_kernel.shape[1]
    height = 2 * rows
    inner = height - 4
    count = lax.axis_size("rows")
    joint = [pair for i in range(count - 1) for pair in ((2 * i, 2 * i + 3), (2 * i + 3, 2 * i))]
    swap = [(0, 1), (1, 0)]
    (mark,) = call(open_kernel, "open", (pltpu.VMEM((8, 128), F32),), (), 1, 1000)
    near = lax.ppermute(codes, ("rows", "section"), joint)
    gain_res = gain_res.reshape(1, -1)
    w, tap, proj, gain = in_space(pltpu.VMEM, up_kernel, out_kernel, in_proj, gain_up.reshape(1, -1))
    (codes,) = in_space(pltpu.VMEM, codes)
    hbm = pl.BlockSpec(memory_space=pltpu.HBM)

    (act,) = call(
        latent_kernel,
        "latent",
        (pltpu.VMEM((frames * rows * cols, width), BF16),),
        (codes, proj, gain, mark),
        4,
        1000,
    )
    inner_own, edge = call(
        functools.partial(own_kernel, frames, cols),
        "own",
        (pltpu.VMEM(((rows - 1) * size, 4 * share), BF16), pltpu.VMEM((2, size, 6 * share), F32)),
        (act, w),
        8,
        1000,
    )
    inner_other = lax.ppermute(inner_own, "section", swap)

    near, edge = lax.optimization_barrier((near, edge))
    far = lax.ppermute(near, "section", swap)
    near, far, edge = in_space(pltpu.VMEM, near, far, edge)
    (near_part,) = call(
        near_kernel,
        "near",
        (pltpu.VMEM((size, 6 * share), F32),),
        (near, proj, gain, w),
        6,
        3000,
    )
    far, near_part = lax.optimization_barrier((far, near_part))
    far, near_part = in_space(pltpu.VMEM, far, near_part)
    (edge_own,) = call(
        halo_kernel,
        "halo",
        (pltpu.VMEM((2 * size, 4 * share), BF16),),
        (far, proj, gain, w, near_part, edge),
        8,
        20000,
    )
    edge_other = lax.ppermute(edge_own, "section", swap)
    inner_other, edge_other = in_space(pltpu.VMEM, inner_other, edge_other)

    mixed = pltpu.VMEM((max(inner, 4), 2 * size, 2 * ow), F32)
    out_inner, norm = call(
        functools.partial(inner_out_kernel, frames, cols),
        "out_inner",
        (pltpu.VMEM((frames, inner, 2 * cols, ow), BF16), pltpu.VMEM((4, size, 4 * share), BF16)),
        (inner_own, inner_other, gain_res, tap),
        12,
        2000,
        [mixed],
    )
    return call(
        functools.partial(edge_out_kernel, frames, cols),
        "out_edge",
        jax.ShapeDtypeStruct((frames, height, 2 * cols, ow), BF16),
        (edge_own, edge_other, gain_res, tap, norm, out_inner),
        12,
        1000,
        [pltpu.VMEM((frames, 4, 2 * cols, ow), BF16), mixed, pltpu.SemaphoreType.DMA((3,))],
        out_specs=hbm,
    )


def solution(mesh):
    in_specs = (
        P("clip", "rows", None),
        P(),
        P(),
        P(None, None, "section"),
        P(),
        P(None, "section", None),
    )
    out_specs = P("clip", "rows", None, "section")
    return jax.shard_map(body, mesh=mesh, in_specs=in_specs, out_specs=out_specs, check_vma=False)
```

```python
import functools

import jax
import jax.numpy as jnp
from jax import lax
from jax.experimental import pallas as pl
from jax.experimental.pallas import tpu as pltpu
from jax.sharding import PartitionSpec as P

BITS = 18
EPS = 1e-06
F32 = jnp.float32
BF16 = jnp.bfloat16
MIB = 1024 * 1024
GROUPS = ((0, 2), (2, 2), (4, 2), (6, 2), (8, 1))


def silu_of_half(h):
    return h + h * jnp.tanh(h)


def latent_rows(rows, in_proj, gain):
    cols = rows[0].shape[1]
    count = len(rows)
    wide = jnp.concatenate([jnp.broadcast_to(row, (cols, cols)) for row in rows], axis=0)
    sub = lax.broadcasted_iota(jnp.int32, (count, cols, cols), 1).reshape(count * cols, cols)
    lane = lax.broadcasted_iota(jnp.int32, (count * cols, cols), 1)
    picked = jnp.where(sub == lane, wide, 0).astype(F32)
    column = jnp.sum(picked, axis=1, keepdims=True).astype(jnp.int32)
    spread = jnp.broadcast_to(column, (count * cols, BITS))
    shift = lax.broadcasted_iota(jnp.int32, (count * cols, BITS), 1)
    bits = ((jnp.right_shift(spread, shift) & 1) * 2 - 1).astype(F32).astype(BF16)
    latent = jnp.dot(bits, in_proj, preferred_element_type=F32)
    mean = jnp.mean(latent * latent, axis=1, keepdims=True)
    return silu_of_half(latent * lax.rsqrt(mean + EPS) * (0.5 * gain))


def shifted(x, cols, amount):
    rows, lanes = x.shape
    place = lax.broadcasted_iota(jnp.int32, (rows // cols, cols, lanes), 1).reshape(rows, lanes)
    moved = pltpu.roll(x, amount % rows, 0)
    return jnp.where(place == (0 if amount == 1 else cols - 1), 0.0, moved)


def weights(w_ref, a, group):
    return jnp.concatenate([w_ref[9 * a + group[0] + k] for k in range(group[1])], axis=1)


def products(act, n, w_ref, group):
    share = w_ref.shape[2]
    if group[1] == 1:
        both = jnp.concatenate([weights(w_ref, 2, group), weights(w_ref, 1, group)], axis=1)
        now = jnp.dot(act, both, preferred_element_type=F32)
        now, back = now[:, :share], now[: 3 * n, share:]
    else:
        now = jnp.dot(act, weights(w_ref, 2, group), preferred_element_type=F32)
        back = jnp.dot(act[: 3 * n], weights(w_ref, 1, group), preferred_element_type=F32)
    oldest = jnp.dot(act[: 2 * n], weights(w_ref, 0, group), preferred_element_type=F32)
    return jnp.concatenate([now[:n], now[n : 2 * n] + back[:n], now[2 * n :] + back[n:] + oldest], axis=0)


def open_kernel(mark_ref):
    mark_ref[...] = jnp.zeros_like(mark_ref)


def latent_kernel(codes_ref, proj_ref, gain_ref, mark_ref, act_ref):
    frames, rows, cols = codes_ref.shape
    codes = [codes_ref[t, r : r + 1, :] for t in range(frames) for r in range(rows)]
    act_ref[...] = latent_rows(codes, proj_ref[...], gain_ref[...]).astype(BF16)


def row_products(act, n, w_ref, base):
    parts = []
    for first in range(0, 6, 2):
        total = []
        for a in range(3):
            m = -(-(2 + a) * n // 16) * 16
            pair = jnp.concatenate([w_ref[9 * a + base + first + k] for k in range(2)], axis=1)
            total.append(jnp.dot(act[:m], pair, preferred_element_type=F32))
        oldest, back, now = total
        parts.append(
            jnp.concatenate(
                [now[:n], now[n : 2 * n] + back[:n], now[2 * n :] + back[n : 3 * n] + oldest[: 2 * n]], axis=0
            )
        )
    return jnp.concatenate(parts, axis=1)


def of_row(part, frames, stride, start, cols):
    return jnp.concatenate([part[t * stride + start : t * stride + start + cols] for t in range(frames)], axis=0)


def put_hidden(upper, lower, cols, share, q, h_ref):
    size = upper(0).shape[0]
    sums = [[], []]
    for c in range(3):
        x = upper(c) + lower(6 + c)
        sums[0].append(x + upper(3 + c))
        sums[1].append(x + lower(3 + c))
    out = pl.ds(q * size, size)
    for py, (left, mid, right) in enumerate(sums):
        even = shifted(left, cols, 1) + (mid + right)
        odd = (left + mid) + shifted(right, cols, -1)
        h_ref[out, pl.ds(2 * py * share, share)] = even.astype(BF16)
        h_ref[out, pl.ds((2 * py + 1) * share, share)] = odd.astype(BF16)


def own_kernel(frames, cols, act_ref, w_ref, h_ref, edge_ref):
    share = w_ref.shape[2]
    n = act_ref.shape[0] // frames
    rows = n // cols
    act = act_ref[...]
    taken = []
    for group in GROUPS:
        part = products(act, n, w_ref, group)
        taken += [part[:, k * share : (k + 1) * share] for k in range(group[1])]

    def row(r):
        return lambda tap: of_row(taken[tap], frames, n, r * cols, cols)

    for q in range(rows - 1):
        put_hidden(row(q), row(q + 1), cols, share, q, h_ref)
    for k in range(6):
        edge_ref[0, :, pl.ds(k * share, share)] = row(0)(3 + k)
        edge_ref[1, :, pl.ds(k * share, share)] = row(rows - 1)(k)


def halo_products(codes_ref, below, proj_ref, gain_ref, w_ref):
    frames, rows, cols = codes_ref.shape
    place = lax.axis_index("rows")
    last = lax.axis_size("rows") - 1
    codes = [jnp.where(below, codes_ref[t, rows - 1 : rows, :], codes_ref[t, 0:1, :]) for t in range(frames)]
    act = latent_rows(codes, proj_ref[...], gain_ref[...])
    inside = jnp.where(below, place > 0, place < last)
    act = jnp.where(inside, act, 0.0).astype(BF16)
    return row_products(act, cols, w_ref, jnp.where(below, 0, 3))


def near_kernel(near_ref, proj_ref, gain_ref, w_ref, part_ref):
    below = lax.axis_index("section") == 1
    part_ref[...] = halo_products(near_ref, below, proj_ref, gain_ref, w_ref)


def halo_kernel(far_ref, proj_ref, gain_ref, w_ref, near_ref, edge_ref, h_ref):
    share = w_ref.shape[2]
    cols = far_ref.shape[2]
    below = lax.axis_index("section") == 0
    far = halo_products(far_ref, below, proj_ref, gain_ref, w_ref)

    def of(part, k):
        return part[:, k * share : (k + 1) * share]

    def lower_row(tap):
        return jnp.where(below, of(far, tap), near_ref[:, pl.ds(tap * share, share)])

    def upper_row(tap):
        return jnp.where(below, near_ref[:, pl.ds((tap - 3) * share, share)], of(far, tap - 3))

    put_hidden(lower_row, lambda tap: edge_ref[0, :, pl.ds((tap - 3) * share, share)], cols, share, 0, h_ref)
    put_hidden(lambda tap: edge_ref[1, :, pl.ds(tap * share, share)], upper_row, cols, share, 1, h_ref)


def part_starts(part):
    section = lax.axis_index("section")
    return [pl.multiple_of(k * part, part) for k in (section, 1 - section)]


def normalise(size, own_ref, other_ref, gain_ref, keeps):
    part = own_ref.shape[1] // 4
    gains = [0.5 * gain_ref[:, pl.ds(start, part)] for start in part_starts(part)]
    rows = []
    for j, keep in enumerate(keeps):
        cells = []
        for px in range(2):
            lanes = pl.ds((2 * (j % 2) + px) * part, part)
            x = [ref[pl.ds(j // 2 * size, size), lanes].astype(F32) for ref in (own_ref, other_ref)]
            mean = jnp.sum(x[0] * x[0] + x[1] * x[1], axis=1, keepdims=True) / (2 * part)
            scale = lax.rsqrt(mean + EPS)
            if keep is not None:
                scale = jnp.where(keep, scale, 0.0)
            cells += [silu_of_half(x[s] * scale * gains[s]).astype(BF16) for s in range(2)]
        rows.append(jnp.concatenate(cells, axis=1))
    return rows


def out_products(windows, tap_ref, a, m):
    left = jnp.concatenate([jnp.concatenate([row[:m] for row in window], axis=1) for window in windows], axis=0)
    part = tap_ref.shape[2] // 2
    starts = part_starts(part)
    lines = [[], [], [], []]
    for b in range(3):
        w = [
            jnp.concatenate([tap_ref[9 * a + 3 * b + c, :, pl.ds(start, part)] for start in starts], axis=1)
            for c in range(3)
        ]
        zero = jnp.zeros_like(w[0])
        for line, cells in zip(lines, ((w[1], w[2]), (w[0], w[1]), (zero, w[0]), (w[2], zero))):
            line += cells
    right = jnp.concatenate([jnp.concatenate(line, axis=1) for line in lines], axis=0)
    total = lax.dot_general(left, right, (((1,), (1,)), ((), ())), preferred_element_type=F32)
    return total.reshape(len(windows), m, right.shape[0])


def out_rows(windows, tap_ref, frames, cols, mix_ref, o_ref, after_half=None):
    size = frames * cols
    height = len(windows)
    rows, ow = o_ref.shape[2:]
    now, back, oldest = [out_products(windows, tap_ref, a, -(-(frames - 2 + a) * cols // 16) * 16) for a in (2, 1, 0)]
    half = height // 2
    for part in (range(half), range(half, height)):
        for y in part:
            full = jnp.concatenate(
                [
                    now[y, :cols],
                    now[y, cols : 2 * cols] + back[y, :cols],
                    now[y, 2 * cols :] + back[y, cols : size - cols] + oldest[y, : size - 2 * cols],
                ],
                axis=0,
            )
            side = full[:, 2 * ow :]
            lane = lax.broadcasted_iota(jnp.int32, side.shape, 1)
            both = full[:, : 2 * ow] + jnp.where(lane < ow, shifted(side, cols, 1), shifted(side, cols, -1))
            mix_ref[y, pl.ds(0, size, stride=2), :] = both
            mix_ref[y, pl.ds(1, size, stride=2), :] = pltpu.roll(both, ow, 1)
        for y in part:
            result = mix_ref[y][:, :ow].astype(BF16)
            for t in range(frames):
                o_ref[t, y] = result[rows * t : rows * (t + 1)]
        if after_half is not None and part.start == 0:
            after_half()


def inner_out_kernel(frames, cols, own_ref, other_ref, gain_ref, tap_ref, o_ref, norm_ref, mix_ref):
    size = frames * cols
    count = own_ref.shape[0] // size * 2
    rows = normalise(size, own_ref, other_ref, gain_ref, [None] * count)
    for k, j in enumerate((0, 1, count - 2, count - 1)):
        norm_ref[k] = rows[j]
    out_rows([rows[y : y + 3] for y in range(count - 2)], tap_ref, frames, cols, mix_ref, o_ref)


def edge_out_kernel(frames, cols, own_ref, other_ref, gain_ref, tap_ref, norm_ref, inner_ref, o_hbm, o_ref, mix_ref, sems):
    size = frames * cols
    inner = inner_ref.shape[1]
    copies = [pltpu.make_async_copy(inner_ref, o_hbm.at[:, pl.ds(2, inner)], sems.at[0])]
    copies[0].start()
    place = lax.axis_index("rows")
    last = lax.axis_size("rows") - 1
    edge = normalise(size, own_ref, other_ref, gain_ref, (place > 0, None, None, place < last))
    top = edge[:2] + [norm_ref[0], norm_ref[1]]
    bottom = [norm_ref[2], norm_ref[3]] + edge[2:]
    windows = [side[y : y + 3] for side in (top, bottom) for y in range(2)]
    for k, start in enumerate((0, inner + 2)):
        copies.append(
            pltpu.make_async_copy(o_ref.at[:, pl.ds(2 * k, 2)], o_hbm.at[:, pl.ds(start, 2)], sems.at[1 + k])
        )
    out_rows(windows, tap_ref, frames, cols, mix_ref, o_ref, copies[1].start)
    copies[2].start()
    for copy in copies:
        copy.wait()


def params(mib):
    return pltpu.CompilerParams(vmem_limit_bytes=mib * MIB)


def cost(mflops):
    return pl.CostEstimate(flops=mflops * 10**6, bytes_accessed=10**7, transcendentals=0)


def vmem():
    return pl.BlockSpec(memory_space=pltpu.VMEM)


def in_space(space, *arrays):
    return tuple(pltpu.with_memory_space_constraint(x, space) for x in arrays)


def call(kernel, name, outs, ins, mib, mflops, scratch=(), in_specs=None, out_specs=None):
    results = pl.pallas_call(
        kernel,
        out_shape=outs,
        in_specs=in_specs or [vmem()] * len(ins),
        out_specs=out_specs or (vmem(),) * len(outs),
        scratch_shapes=list(scratch),
        compiler_params=params(mib),
        cost_estimate=cost(mflops),
        name=name,
    )(*ins)
    return results if out_specs else in_space(pltpu.VMEM, *results)


def body(codes, in_proj, gain_up, up_kernel, gain_res, out_kernel):
    frames, rows, cols = codes.shape
    size = frames * cols
    width, share = up_kernel.shape[1:]
    ow = out_kernel.shape[1]
    height = 2 * rows
    inner = height - 4
    count = lax.axis_size("rows")
    joint = [pair for i in range(count - 1) for pair in ((2 * i, 2 * i + 3), (2 * i + 3, 2 * i))]
    swap = [(0, 1), (1, 0)]
    (mark,) = call(open_kernel, "open", (pltpu.VMEM((8, 128), F32),), (), 1, 1000)
    near = lax.ppermute(codes, ("rows", "section"), joint)
    gain_res = gain_res.reshape(1, -1)
    w, tap, proj, gain = in_space(pltpu.VMEM, up_kernel, out_kernel, in_proj, gain_up.reshape(1, -1))
    (codes,) = in_space(pltpu.VMEM, codes)
    hbm = pl.BlockSpec(memory_space=pltpu.HBM)

    (act,) = call(
        latent_kernel,
        "latent",
        (pltpu.VMEM((frames * rows * cols, width), BF16),),
        (codes, proj, gain, mark),
        4,
        1000,
    )
    inner_own, edge = call(
        functools.partial(own_kernel, frames, cols),
        "own",
        (pltpu.VMEM(((rows - 1) * size, 4 * share), BF16), pltpu.VMEM((2, size, 6 * share), F32)),
        (act, w),
        8,
        1000,
    )
    inner_other = lax.ppermute(inner_own, "section", swap)

    near, edge = lax.optimization_barrier((near, edge))
    far = lax.ppermute(near, "section", swap)
    near, far, edge = in_space(pltpu.VMEM, near, far, edge)
    (near_part,) = call(
        near_kernel,
        "near",
        (pltpu.VMEM((size, 6 * share), F32),),
        (near, proj, gain, w),
        6,
        3000,
    )
    far, near_part = lax.optimization_barrier((far, near_part))
    far, near_part = in_space(pltpu.VMEM, far, near_part)
    (edge_own,) = call(
        halo_kernel,
        "halo",
        (pltpu.VMEM((2 * size, 4 * share), BF16),),
        (far, proj, gain, w, near_part, edge),
        8,
        20000,
    )
    edge_other = lax.ppermute(edge_own, "section", swap)
    inner_other, edge_other = in_space(pltpu.VMEM, inner_other, edge_other)

    mixed = pltpu.VMEM((max(inner, 4), 2 * size, 2 * ow), F32)
    out_inner, norm = call(
        functools.partial(inner_out_kernel, frames, cols),
        "out_inner",
        (pltpu.VMEM((frames, inner, 2 * cols, ow), BF16), pltpu.VMEM((4, size, 4 * share), BF16)),
        (inner_own, inner_other, gain_res, tap),
        12,
        2000,
        [mixed],
    )
    return call(
        functools.partial(edge_out_kernel, frames, cols),
        "out_edge",
        jax.ShapeDtypeStruct((frames, height, 2 * cols, ow), BF16),
        (edge_own, edge_other, gain_res, tap, norm, out_inner),
        12,
        1000,
        [pltpu.VMEM((frames, 4, 2 * cols, ow), BF16), mixed, pltpu.SemaphoreType.DMA((3,))],
        out_specs=hbm,
    )


def solution(mesh):
    in_specs = (
        P("clip", "rows", None),
        P(),
        P(),
        P(None, None, "section"),
        P(),
        P(None, "section", None),
    )
    out_specs = P("clip", "rows", None, "section")
    return jax.shard_map(body, mesh=mesh, in_specs=in_specs, out_specs=out_specs, check_vma=False)
```

```python
import functools

import jax
import jax.numpy as jnp
from jax import lax
from jax.experimental import pallas as pl
from jax.experimental.pallas import tpu as pltpu
from jax.sharding import PartitionSpec as P

BITS = 18
EPS = 1e-06
F32 = jnp.float32
BF16 = jnp.bfloat16
MIB = 1024 * 1024
GROUPS = ((0, 2), (2, 2), (4, 2), (6, 2), (8, 1))


def silu_of_half(h):
    return h + h * jnp.tanh(h)


def latent_rows(rows, in_proj, gain):
    cols = rows[0].shape[1]
    count = len(rows)
    wide = jnp.concatenate([jnp.broadcast_to(row, (cols, cols)) for row in rows], axis=0)
    sub = lax.broadcasted_iota(jnp.int32, (count, cols, cols), 1).reshape(count * cols, cols)
    lane = lax.broadcasted_iota(jnp.int32, (count * cols, cols), 1)
    picked = jnp.where(sub == lane, wide, 0).astype(F32)
    column = jnp.sum(picked, axis=1, keepdims=True).astype(jnp.int32)
    spread = jnp.broadcast_to(column, (count * cols, BITS))
    shift = lax.broadcasted_iota(jnp.int32, (count * cols, BITS), 1)
    bits = ((jnp.right_shift(spread, shift) & 1) * 2 - 1).astype(F32).astype(BF16)
    latent = jnp.dot(bits, in_proj, preferred_element_type=F32)
    mean = jnp.mean(latent * latent, axis=1, keepdims=True)
    return silu_of_half(latent * lax.rsqrt(mean + EPS) * (0.5 * gain))


def shifted(x, cols, amount):
    rows, lanes = x.shape
    place = lax.broadcasted_iota(jnp.int32, (rows // cols, cols, lanes), 1).reshape(rows, lanes)
    moved = pltpu.roll(x, amount % rows, 0)
    return jnp.where(place == (0 if amount == 1 else cols - 1), 0.0, moved)


def weights(w_ref, a, group):
    return jnp.concatenate([w_ref[9 * a + group[0] + k] for k in range(group[1])], axis=1)


def products(act, n, w_ref, group):
    share = w_ref.shape[2]
    if group[1] == 1:
        both = jnp.concatenate([weights(w_ref, 2, group), weights(w_ref, 1, group)], axis=1)
        now = jnp.dot(act, both, preferred_element_type=F32)
        now, back = now[:, :share], now[: 3 * n, share:]
    else:
        now = jnp.dot(act, weights(w_ref, 2, group), preferred_element_type=F32)
        back = jnp.dot(act[: 3 * n], weights(w_ref, 1, group), preferred_element_type=F32)
    oldest = jnp.dot(act[: 2 * n], weights(w_ref, 0, group), preferred_element_type=F32)
    return jnp.concatenate([now[:n], now[n : 2 * n] + back[:n], now[2 * n :] + back[n:] + oldest], axis=0)


def open_kernel(mark_ref):
    mark_ref[...] = jnp.zeros_like(mark_ref)


def latent_kernel(codes_ref, proj_ref, gain_ref, mark_ref, act_ref):
    frames, rows, cols = codes_ref.shape
    codes = [codes_ref[t, r : r + 1, :] for t in range(frames) for r in range(rows)]
    act_ref[...] = latent_rows(codes, proj_ref[...], gain_ref[...]).astype(BF16)


def row_products(act, n, w_ref, base):
    parts = []
    for first in range(0, 6, 2):
        total = []
        for a in range(3):
            m = -(-(2 + a) * n // 16) * 16
            pair = jnp.concatenate([w_ref[9 * a + base + first + k] for k in range(2)], axis=1)
            total.append(jnp.dot(act[:m], pair, preferred_element_type=F32))
        oldest, back, now = total
        parts.append(
            jnp.concatenate(
                [now[:n], now[n : 2 * n] + back[:n], now[2 * n :] + back[n : 3 * n] + oldest[: 2 * n]], axis=0
            )
        )
    return jnp.concatenate(parts, axis=1)


def of_row(part, frames, stride, start, cols):
    return jnp.concatenate([part[t * stride + start : t * stride + start + cols] for t in range(frames)], axis=0)


def put_hidden(upper, lower, cols, share, q, h_ref):
    size = upper(0).shape[0]
    sums = [[], []]
    for c in range(3):
        x = upper(c) + lower(6 + c)
        sums[0].append(x + upper(3 + c))
        sums[1].append(x + lower(3 + c))
    out = pl.ds(q * size, size)
    for py, (left, mid, right) in enumerate(sums):
        even = shifted(left, cols, 1) + (mid + right)
        odd = (left + mid) + shifted(right, cols, -1)
        h_ref[out, pl.ds(2 * py * share, share)] = even.astype(BF16)
        h_ref[out, pl.ds((2 * py + 1) * share, share)] = odd.astype(BF16)


def own_kernel(frames, cols, act_ref, w_ref, h_ref, edge_ref):
    share = w_ref.shape[2]
    n = act_ref.shape[0] // frames
    rows = n // cols
    act = act_ref[...]
    taken = []
    for group in GROUPS:
        part = products(act, n, w_ref, group)
        taken += [part[:, k * share : (k + 1) * share] for k in range(group[1])]

    def row(r):
        return lambda tap: of_row(taken[tap], frames, n, r * cols, cols)

    for q in range(rows - 1):
        put_hidden(row(q), row(q + 1), cols, share, q, h_ref)
    for k in range(6):
        edge_ref[0, :, pl.ds(k * share, share)] = row(0)(3 + k)
        edge_ref[1, :, pl.ds(k * share, share)] = row(rows - 1)(k)


def halo_products(codes_ref, below, proj_ref, gain_ref, w_ref):
    frames, rows, cols = codes_ref.shape
    place = lax.axis_index("rows")
    last = lax.axis_size("rows") - 1
    codes = [jnp.where(below, codes_ref[t, rows - 1 : rows, :], codes_ref[t, 0:1, :]) for t in range(frames)]
    act = latent_rows(codes, proj_ref[...], gain_ref[...])
    inside = jnp.where(below, place > 0, place < last)
    act = jnp.where(inside, act, 0.0).astype(BF16)
    return row_products(act, cols, w_ref, jnp.where(below, 0, 3))


def near_kernel(near_ref, proj_ref, gain_ref, w_ref, part_ref):
    below = lax.axis_index("section") == 1
    part_ref[...] = halo_products(near_ref, below, proj_ref, gain_ref, w_ref)


def halo_kernel(far_ref, proj_ref, gain_ref, w_ref, near_ref, edge_ref, h_ref):
    share = w_ref.shape[2]
    cols = far_ref.shape[2]
    below = lax.axis_index("section") == 0
    far = halo_products(far_ref, below, proj_ref, gain_ref, w_ref)

    def of(part, k):
        return part[:, k * share : (k + 1) * share]

    def lower_row(tap):
        return jnp.where(below, of(far, tap), near_ref[:, pl.ds(tap * share, share)])

    def upper_row(tap):
        return jnp.where(below, near_ref[:, pl.ds((tap - 3) * share, share)], of(far, tap - 3))

    put_hidden(lower_row, lambda tap: edge_ref[0, :, pl.ds((tap - 3) * share, share)], cols, share, 0, h_ref)
    put_hidden(lambda tap: edge_ref[1, :, pl.ds(tap * share, share)], upper_row, cols, share, 1, h_ref)


def part_starts(part):
    section = lax.axis_index("section")
    return [pl.multiple_of(k * part, part) for k in (section, 1 - section)]


def normalise(size, own_ref, other_ref, gain_ref, keeps):
    part = own_ref.shape[1] // 4
    gains = [0.5 * gain_ref[:, pl.ds(start, part)] for start in part_starts(part)]
    rows = []
    for j, keep in enumerate(keeps):
        cells = []
        for px in range(2):
            lanes = pl.ds((2 * (j % 2) + px) * part, part)
            x = [ref[pl.ds(j // 2 * size, size), lanes].astype(F32) for ref in (own_ref, other_ref)]
            mean = jnp.sum(x[0] * x[0] + x[1] * x[1], axis=1, keepdims=True) / (2 * part)
            scale = lax.rsqrt(mean + EPS)
            if keep is not None:
                scale = jnp.where(keep, scale, 0.0)
            cells += [silu_of_half(x[s] * scale * gains[s]).astype(BF16) for s in range(2)]
        rows.append(jnp.concatenate(cells, axis=1))
    return rows


def out_products(windows, tap_ref, a, m):
    left = jnp.concatenate([jnp.concatenate([row[:m] for row in window], axis=1) for window in windows], axis=0)
    part = tap_ref.shape[2] // 2
    starts = part_starts(part)
    lines = [[], [], [], []]
    for b in range(3):
        w = [
            jnp.concatenate([tap_ref[9 * a + 3 * b + c, :, pl.ds(start, part)] for start in starts], axis=1)
            for c in range(3)
        ]
        zero = jnp.zeros_like(w[0])
        for line, cells in zip(lines, ((w[1], w[2]), (w[0], w[1]), (zero, w[0]), (w[2], zero))):
            line += cells
    right = jnp.concatenate([jnp.concatenate(line, axis=1) for line in lines], axis=0)
    total = lax.dot_general(left, right, (((1,), (1,)), ((), ())), preferred_element_type=F32)
    return total.reshape(len(windows), m, right.shape[0])


def out_rows(windows, tap_ref, frames, cols, mix_ref, o_ref, after_half=None):
    size = frames * cols
    height = len(windows)
    rows, ow = o_ref.shape[2:]
    now, back, oldest = [out_products(windows, tap_ref, a, -(-(frames - 2 + a) * cols // 16) * 16) for a in (2, 1, 0)]
    for y in range(height):
        full = jnp.concatenate(
            [
                now[y, :cols],
                now[y, cols : 2 * cols] + back[y, :cols],
                now[y, 2 * cols :] + back[y, cols : size - cols] + oldest[y, : size - 2 * cols],
            ],
            axis=0,
        )
        side = full[:, 2 * ow :]
        lane = lax.broadcasted_iota(jnp.int32, side.shape, 1)
        both = full[:, : 2 * ow] + jnp.where(lane < ow, shifted(side, cols, 1), shifted(side, cols, -1))
        mix_ref[y, pl.ds(0, size, stride=2), :] = both
        mix_ref[y, pl.ds(1, size, stride=2), :] = pltpu.roll(both, ow, 1)
    for y in range(height):
        result = mix_ref[y][:, :ow].astype(BF16)
        for t in range(frames):
            o_ref[t, y] = result[rows * t : rows * (t + 1)]
        if after_half is not None and 2 * (y + 1) == height:
            after_half()


def inner_out_kernel(frames, cols, own_ref, other_ref, gain_ref, tap_ref, o_ref, norm_ref, mix_ref):
    size = frames * cols
    count = own_ref.shape[0] // size * 2
    rows = normalise(size, own_ref, other_ref, gain_ref, [None] * count)
    out_rows([rows[y : y + 3] for y in range(count - 2)], tap_ref, frames, cols, mix_ref, o_ref)
    for k, j in enumerate((0, 1, count - 2, count - 1)):
        norm_ref[k] = rows[j]


def edge_out_kernel(frames, cols, own_ref, other_ref, gain_ref, tap_ref, norm_ref, inner_ref, o_hbm, o_ref, mix_ref, sems):
    size = frames * cols
    inner = inner_ref.shape[1]
    copies = [pltpu.make_async_copy(inner_ref, o_hbm.at[:, pl.ds(2, inner)], sems.at[0])]
    copies[0].start()
    place = lax.axis_index("rows")
    last = lax.axis_size("rows") - 1
    edge = normalise(size, own_ref, other_ref, gain_ref, (place > 0, None, None, place < last))
    top = edge[:2] + [norm_ref[0], norm_ref[1]]
    bottom = [norm_ref[2], norm_ref[3]] + edge[2:]
    windows = [side[y : y + 3] for side in (top, bottom) for y in range(2)]
    for k, start in enumerate((0, inner + 2)):
        copies.append(
            pltpu.make_async_copy(o_ref.at[:, pl.ds(2 * k, 2)], o_hbm.at[:, pl.ds(start, 2)], sems.at[1 + k])
        )
    out_rows(windows, tap_ref, frames, cols, mix_ref, o_ref, copies[1].start)
    copies[2].start()
    for copy in copies:
        copy.wait()


def params(mib):
    return pltpu.CompilerParams(vmem_limit_bytes=mib * MIB)


def cost(mflops):
    return pl.CostEstimate(flops=mflops * 10**6, bytes_accessed=10**7, transcendentals=0)


def vmem():
    return pl.BlockSpec(memory_space=pltpu.VMEM)


def in_space(space, *arrays):
    return tuple(pltpu.with_memory_space_constraint(x, space) for x in arrays)


def call(kernel, name, outs, ins, mib, mflops, scratch=(), in_specs=None, out_specs=None):
    results = pl.pallas_call(
        kernel,
        out_shape=outs,
        in_specs=in_specs or [vmem()] * len(ins),
        out_specs=out_specs or (vmem(),) * len(outs),
        scratch_shapes=list(scratch),
        compiler_params=params(mib),
        cost_estimate=cost(mflops),
        name=name,
    )(*ins)
    return results if out_specs else in_space(pltpu.VMEM, *results)


def body(codes, in_proj, gain_up, up_kernel, gain_res, out_kernel):
    frames, rows, cols = codes.shape
    size = frames * cols
    width, share = up_kernel.shape[1:]
    ow = out_kernel.shape[1]
    height = 2 * rows
    inner = height - 4
    count = lax.axis_size("rows")
    joint = [pair for i in range(count - 1) for pair in ((2 * i, 2 * i + 3), (2 * i + 3, 2 * i))]
    swap = [(0, 1), (1, 0)]
    (mark,) = call(open_kernel, "open", (pltpu.VMEM((8, 128), F32),), (), 1, 1000)
    near = lax.ppermute(codes, ("rows", "section"), joint)
    gain_res = gain_res.reshape(1, -1)
    w, tap, proj, gain = in_space(pltpu.VMEM, up_kernel, out_kernel, in_proj, gain_up.reshape(1, -1))
    (codes,) = in_space(pltpu.VMEM, codes)
    hbm = pl.BlockSpec(memory_space=pltpu.HBM)

    (act,) = call(
        latent_kernel,
        "latent",
        (pltpu.VMEM((frames * rows * cols, width), BF16),),
        (codes, proj, gain, mark),
        4,
        1000,
    )
    inner_own, edge = call(
        functools.partial(own_kernel, frames, cols),
        "own",
        (pltpu.VMEM(((rows - 1) * size, 4 * share), BF16), pltpu.VMEM((2, size, 6 * share), F32)),
        (act, w),
        8,
        1000,
    )
    inner_other = lax.ppermute(inner_own, "section", swap)

    near, edge = lax.optimization_barrier((near, edge))
    far = lax.ppermute(near, "section", swap)
    near, far, edge = in_space(pltpu.VMEM, near, far, edge)
    (near_part,) = call(
        near_kernel,
        "near",
        (pltpu.VMEM((size, 6 * share), F32),),
        (near, proj, gain, w),
        6,
        3000,
    )
    far, near_part = lax.optimization_barrier((far, near_part))
    far, near_part = in_space(pltpu.VMEM, far, near_part)
    (edge_own,) = call(
        halo_kernel,
        "halo",
        (pltpu.VMEM((2 * size, 4 * share), BF16),),
        (far, proj, gain, w, near_part, edge),
        8,
        20000,
    )
    edge_other = lax.ppermute(edge_own, "section", swap)
    inner_other, edge_other = in_space(pltpu.VMEM, inner_other, edge_other)

    mixed = pltpu.VMEM((max(inner, 4), 2 * size, 2 * ow), F32)
    out_inner, norm = call(
        functools.partial(inner_out_kernel, frames, cols),
        "out_inner",
        (pltpu.VMEM((frames, inner, 2 * cols, ow), BF16), pltpu.VMEM((4, size, 4 * share), BF16)),
        (inner_own, inner_other, gain_res, tap),
        12,
        2000,
        [mixed],
    )
    return call(
        functools.partial(edge_out_kernel, frames, cols),
        "out_edge",
        jax.ShapeDtypeStruct((frames, height, 2 * cols, ow), BF16),
        (edge_own, edge_other, gain_res, tap, norm, out_inner),
        12,
        1000,
        [pltpu.VMEM((frames, 4, 2 * cols, ow), BF16), mixed, pltpu.SemaphoreType.DMA((3,))],
        out_specs=hbm,
    )


def solution(mesh):
    in_specs = (
        P("clip", "rows", None),
        P(),
        P(),
        P(None, None, "section"),
        P(),
        P(None, "section", None),
    )
    out_specs = P("clip", "rows", None, "section")
    return jax.shard_map(body, mesh=mesh, in_specs=in_specs, out_specs=out_specs, check_vma=False)
```
